512 devices in a mesh: wide: 64 (over y_hi, z, x), narrow: 8 (over y_lo, core).
Axes of the slice: x: 4, y: 8 (y_hi: 2, y_lo: 4; y = y_hi * 4 + y_lo), z: 8, core: 2. Of those that a mesh axis runs over, the one named last changes fastest.
Arguments:
- hidden_in: bfloat16 [16384, 2048], P('wide', 'narrow'), may hold values from -32 to 32
- attn_gain: bfloat16 [2048], P('narrow'), may hold values from 0.099609375 to 1.8984375
- qkv_weight: bfloat16 [2048, 1920], P('narrow', 'wide'), may hold values from -0.125 to 0.125
- q_gain: bfloat16 [64], replicated, may hold values from 1 to 2
- k_gain: bfloat16 [64], replicated, may hold values from 1 to 2
- out_weight: bfloat16 [1280, 2048], P('wide', 'narrow'), may hold values from -0.3125 to 0.3125
- lengths: int32 [4], replicated, may hold values from 1 to 8192, 16384 in all
- page_table: int32 [256], P('wide'), may hold values from 0 to 3, as said below
Outputs:
- hidden_out: bfloat16 [16384, 2048], P('wide', 'narrow')
- kv_cache: bfloat16 [256, 64, 640], P('wide', 'narrow')
The draws below stay inside these ranges and needn't reach their ends.
Inputs may be any that keep to these rules, and one draw needn't show every extreme that they name: `lengths`: the 4 prompts sum to 16384 tokens and the longest has exactly 8192. `page_table`: each aligned block of 4 entries holds each slot once.
All inputs are finite; a program needn't handle non-finite values.
Results may differ from the reference program's by a relative error of at most 0.0033.
The reference program's roundings to bfloat16 on the way (of `scaled`, `queries`, `keys`, `values`, `weight_low` and `attended`) count: a program that leaves them out, or rounds other values in their place, can miss the bound.
Values may be sent and summed in bfloat16 or wider, within the bound.
No kernel may reach another device: no remote copies, remote signals or barrier semaphores. Data moves between devices by JAX's collectives and lax.ppermute only.
A program may use at most 128 MiB of HBM per device.

```python
import math
import jax
import jax.numpy as jnp
import numpy as np
from jax import lax

D = 2048
HEADS = 20
KV_HEADS = 5
HEAD = 64
TOK_DEV = 256
PAGE = 64
SEGS = 4
GROUP = 4
Q_DIM = 1280
KV_DIM = 640
QKV_DIM = 1920
TOKENS = 16384
PAGES_DEV = 4
PAGES = 256


def draw_hidden_in(key, part):
    normal_key = jax.random.fold_in(key, 11)
    scale_key = jax.random.fold_in(key, 12)
    column_scale = jnp.exp(math.log(10.0) * (jnp.arange(D, dtype=jnp.float32) / D - 0.5))
    base_values = jnp.clip(jax.random.normal(normal_key, (TOKENS, D), jnp.float32), -5.0, 5.0)
    row_scale = jnp.exp(jax.random.uniform(scale_key, (TOKENS, 1), jnp.float32, math.log(0.5), math.log(2.0)))
    return (base_values * row_scale * column_scale[None, :]).astype(jnp.bfloat16)


def draw_page_table(key, part):
    block_keys = jax.random.split(jax.random.fold_in(key, 21), TOKENS // TOK_DEV)
    permuted = jax.vmap(lambda block_key: jax.random.permutation(block_key, PAGES_DEV))(block_keys)
    return permuted.reshape(-1).astype(jnp.int32)


def block_scale(rng, dims, cuts, low, largest):
    def one(axis_at, parts):
        steps = jax.random.uniform(jax.random.fold_in(jax.random.fold_in(rng, 6), axis_at), (parts,), jnp.float32, low / len(cuts), largest / len(cuts))
        return jnp.repeat(jnp.exp(steps), dims[axis_at] // parts).reshape((-1,) + (1,) * (len(dims) - axis_at - 1))

    level = one(*cuts[0])
    for cut in cuts[1:]:
        level = level * one(*cut)
    return level


def split_up(number_of, total, limit, slope):
    loads = [(1 << 20) // math.isqrt(grade ** slope) + 1 for grade in range(2, number_of + 1)]
    rest, holding = total - limit - (number_of - 1), [1] * (number_of - 1)
    while rest > 0:
        candidates = [i for i in range(number_of - 1) if holding[i] < limit]
        whole, remaining = sum([loads[i] for i in candidates]), rest
        for i in candidates:
            extra = min(limit - holding[i], max(1, remaining * loads[i] // whole), rest)
            holding[i] = holding[i] + extra
            rest = rest - extra
    return np.array([limit] + holding)


def uneven(key, number_of, total, reach, skew):
    if number_of == 2:
        one = jax.random.randint(key, (), max(1, total - reach), min(reach, total - 1) + 1)
        return jnp.stack([one, total - one])
    tallies = jnp.asarray(split_up(number_of, total, reach, skew), jnp.int32)
    twos = (number_of - 1) // 2
    source_of, receiver = tallies[1:1 + 2 * twos:2], tallies[2:2 + 2 * twos:2]
    slack = jnp.minimum(source_of - 1, reach - receiver)
    shifted = jax.random.randint(jax.random.fold_in(key, 1), (twos,), 0, 1 << 20) % (slack + 1)
    tallies = tallies.at[1:1 + 2 * twos:2].set(source_of - shifted).at[2:2 + 2 * twos:2].set(receiver + shifted)
    return tallies[jax.random.permutation(jax.random.fold_in(key, 2), number_of)]


def bell_draw(own_key, shape, spread, reach, cuts=(), kind=jnp.bfloat16):
    level = block_scale(own_key, shape, cuts, -0.22, 0.18) if cuts else 1.0
    entries = jax.random.normal(own_key, shape, jnp.float32) * spread * level
    return jnp.minimum(jnp.maximum(entries, -reach), reach).astype(kind)


def setup_inputs(seed: int = 0) -> dict:
    splits = jax.random.split(jax.random.key(seed), 9)
    hidden_in = draw_hidden_in(jax.random.fold_in(splits[8], 71), 0)
    attn_gain = jnp.clip(1.0 + 0.18 * jax.random.normal(splits[1], (D,), jnp.float32), 0.099609375, 1.8984375).astype(jnp.bfloat16)
    qkv_weight = bell_draw(splits[2], (D, QKV_DIM), D ** -0.5, 0.125, ((0, 8), (1, 64)))
    q_gain = jnp.clip(jax.random.uniform(splits[3], (HEAD,), jnp.float32, 1.0, 2.0), 1.0, 2.0).astype(jnp.bfloat16)
    k_gain = jnp.clip(jax.random.uniform(splits[4], (HEAD,), jnp.float32, 1.0, 2.0), 1.0, 2.0).astype(jnp.bfloat16)
    out_weight = bell_draw(splits[5], (Q_DIM, D), (Q_DIM // 4) ** -0.5, 0.3125, ((0, 64), (1, 8)))
    lengths = uneven(splits[6], SEGS, TOKENS, TOKENS // 2, 2).astype(jnp.int32)
    page_table = draw_page_table(jax.random.fold_in(splits[8], 71), 0)
    return {"hidden_in": hidden_in, "attn_gain": attn_gain, "qkv_weight": qkv_weight, "q_gain": q_gain, "k_gain": k_gain, "out_weight": out_weight, "lengths": lengths, "page_table": page_table}


rope_base = 10000.0

def token_place(token_ids, lengths):
    prompt_ends = jnp.cumsum(lengths).astype(jnp.int32)
    prompt_starts = (prompt_ends - lengths).astype(jnp.int32)
    segment = lax.optimization_barrier(jnp.sum((token_ids[:, None] >= prompt_ends[None, :]).astype(jnp.int32), axis=1)).astype(jnp.int32)
    matches = segment[:, None] == jnp.arange(lengths.shape[0], dtype=jnp.int32)[None, :]
    position = token_ids - lax.optimization_barrier(jnp.sum(jnp.where(matches, prompt_starts[None, :], 0), axis=1)).astype(jnp.int32)
    return (segment, position)

def rotate(projected_part, head_count, head_gain, position):
    row_count = projected_part.shape[0]
    per_head = projected_part.reshape(row_count, head_count, HEAD)
    per_head = per_head * lax.rsqrt(lax.optimization_barrier(jnp.mean(per_head * per_head, axis=-1, keepdims=True)) + 1e-06)
    per_head = per_head * head_gain.astype(jnp.float32)
    halfway = HEAD // 2
    frequency = jnp.exp(jnp.arange(halfway, dtype=jnp.float32) * (-2.0 * math.log(rope_base) / HEAD))
    angles = position.astype(jnp.float32)[:, None] * frequency[None, :]
    cosine_table = jnp.cos(angles)[:, None, :]
    sine_table = jnp.sin(angles)[:, None, :]
    lower_half = per_head[..., :halfway]
    upper_half = per_head[..., halfway:]
    rotated = jnp.concatenate([lower_half * cosine_table - upper_half * sine_table, upper_half * cosine_table + lower_half * sine_table], axis=-1)
    return rotated.reshape(row_count, head_count * HEAD)

def attention(queries, keys, values, segment, token_ids):
    block_size = min(1024, TOKENS)
    block_count = TOKENS // block_size
    scale = HEAD ** (-0.5)
    query_groups = queries.astype(jnp.float32).reshape(block_count, block_size, KV_HEADS, GROUP, HEAD)
    key_groups = keys.astype(jnp.float32).reshape(block_count, block_size, KV_HEADS, HEAD)
    value_groups = values.astype(jnp.float32).reshape(block_count, block_size, KV_HEADS, HEAD)
    segment_blocks = segment.reshape(block_count, block_size)
    token_blocks = token_ids.reshape(block_count, block_size)
    block_ids = jnp.arange(block_count, dtype=jnp.int32)

    def per_query(query_items):
        query_block, query_segment, query_tokens, query_index = query_items

        def key_step(totals, key_items):
            key_block, value_block, key_segment, key_tokens, key_index = key_items

            def compute(current):
                scores = jnp.einsum('tkgd,nkd->tkgn', query_block, key_block, precision=lax.Precision.HIGHEST) * scale
                visible = (key_segment[None, :] == query_segment[:, None]) & (key_tokens[None, :] <= query_tokens[:, None])
                weights = jnp.where(visible[:, None, None, :], jnp.exp(scores), 0.0)
                weight_low = weights.astype(jnp.bfloat16).astype(jnp.float32)
                numerator = current[0] + jnp.einsum('tkgn,nkd->tkgd', weight_low, value_block, precision=lax.Precision.HIGHEST)
                denominator = current[1] + lax.optimization_barrier(jnp.sum(weights, axis=-1))
                return (numerator, denominator)

            def unchanged(current):
                return current
            return (lax.cond(key_index <= query_index, compute, unchanged, totals), None)
        start_values = (jnp.zeros((block_size, KV_HEADS, GROUP, HEAD), jnp.float32), jnp.zeros((block_size, KV_HEADS, GROUP), jnp.float32))
        totals, unused = lax.scan(key_step, start_values, (key_groups, value_groups, segment_blocks, token_blocks, block_ids))
        attended = totals[0] / totals[1][..., None]
        return attended.reshape(block_size, Q_DIM).astype(jnp.bfloat16)
    attended_blocks = lax.map(per_query, (query_groups, segment_blocks, token_blocks, block_ids))
    return attended_blocks.reshape(TOKENS, Q_DIM)

def reference(hidden_in, attn_gain, qkv_weight, q_gain, k_gain, out_weight, lengths, page_table):
    input_values = hidden_in.astype(jnp.float32)
    scaled = (input_values * attn_gain.astype(jnp.float32)[None, :]).astype(jnp.bfloat16)
    inverse_norm = lax.rsqrt(lax.optimization_barrier(jnp.sum(input_values * input_values, axis=1)) / D + 1e-06)
    projected = jnp.dot(scaled, qkv_weight, preferred_element_type=jnp.float32) * inverse_norm[:, None]
    token_ids = jnp.arange(TOKENS, dtype=jnp.int32)
    segment, position = token_place(token_ids, lengths)
    key_width = KV_DIM // 2
    queries = rotate(projected[:, :Q_DIM], HEADS, q_gain, position).astype(jnp.bfloat16)
    keys = rotate(projected[:, Q_DIM:Q_DIM + key_width], KV_HEADS, k_gain, position).astype(jnp.bfloat16)
    values = projected[:, Q_DIM + key_width:].astype(jnp.bfloat16)
    attended = attention(queries, keys, values, segment, token_ids)
    mixed_rows = jnp.dot(attended, out_weight, preferred_element_type=jnp.float32)
    hidden_out = (input_values + mixed_rows).astype(jnp.bfloat16)
    cache_pages = jnp.concatenate([keys, values], axis=1).reshape(PAGES, PAGE, KV_DIM)
    destination = jnp.arange(PAGES, dtype=jnp.int32) // PAGES_DEV * PAGES_DEV + page_table.astype(jnp.int32)
    kv_cache = jnp.zeros((PAGES, PAGE, KV_DIM), jnp.bfloat16).at[destination].set(cache_pages)
    return (hidden_out, kv_cache)
```

```python
import functools
import math

import jax
import jax.numpy as jnp
from jax import lax
from jax.experimental import pallas as pl
from jax.experimental.pallas import tpu as pltpu
from jax.sharding import Mesh, PartitionSpec as P

D = 2048
HEADS = 20
KV_HEADS = 5
HEAD = 64
GROUP = 4
Q_DIM = 1280
KV_DIM = 640
QKV_DIM = 1920
TOK_DEV = 256
PAGE = 64
PAGES_DEV = 4
ROWS = 32
ROPE_BASE = 10000.0
SUMS = Q_DIM + 128
BF = jnp.bfloat16
F32 = jnp.float32
HIDDEN_BIAS = -1e30
EXP2_SCALE = HEAD ** (-0.5) * math.log2(math.e)

VM = pl.BlockSpec(memory_space=pltpu.VMEM)
SM = pl.BlockSpec(memory_space=pltpu.SMEM)


def call(body, out_shape, in_specs, name, scratch=()):
    many = isinstance(out_shape, tuple)
    return pl.pallas_call(
        body,
        out_shape=out_shape,
        in_specs=in_specs,
        out_specs=(VM,) * len(out_shape) if many else VM,
        scratch_shapes=list(scratch),
        compiler_params=pltpu.CompilerParams(vmem_limit_bytes=48 << 20),
        name=name,
    )


def project_body(flip, place, hidden, gain, weight, out):
    core = place[3] if not flip else 1 - place[3]
    rows = [hidden[p, yl, core].astype(F32) for yl in range(4) for p in range(PAGES_DEV)]
    values = jnp.concatenate(rows, axis=0)
    scaled = (values * gain[...].astype(F32)).astype(BF)
    out[:, :QKV_DIM] = lax.dot_general(
        scaled, weight[...], (((1,), (1,)), ((), ())), preferred_element_type=F32
    )
    squares = jnp.sum(values * values, axis=1, keepdims=True)
    out[:, QKV_DIM:] = jnp.broadcast_to(squares, (128, 128))


def rotate_body(table, parts, cosine, sine, q_gain, k_gain, queries, kv, cache):
    lane = lax.broadcasted_iota(jnp.int32, (ROWS, 128), 1)
    upper_head = lane >= HEAD
    lower_part = (lane % HEAD) < HEAD // 2

    def total(tile):
        at = pl.ds(tile * 128, 128)
        return (parts[0, :, at] + parts[1, :, at]) + (parts[2, :, at] + parts[3, :, at])

    inverse = lax.rsqrt(total(15) / D + 1e-06)
    cos = cosine[...]
    sin = jnp.where(lower_part, -sine[...], sine[...])

    def turned(u, gain):
        square = u * u
        both = jnp.sum(jnp.where(upper_head, 0.0, square), axis=1, keepdims=True)
        other = jnp.sum(jnp.where(upper_head, square, 0.0), axis=1, keepdims=True)
        mean = jnp.where(upper_head, other, both) * (1.0 / HEAD)
        w = u * lax.rsqrt(mean + 1e-06) * gain
        partner = jnp.where(lower_part, pltpu.roll(w, 96, 1), pltpu.roll(w, 32, 1))
        return w * cos + partner * sin

    for tile in range(10):
        u = total(tile) * inverse
        queries[:, tile * 128 : tile * 128 + 128] = turned(u, q_gain[...]).astype(BF)
    for tile in range(10, 15):
        u = total(tile) * inverse
        if tile == 12:
            u = jnp.where(upper_head, u, turned(u, k_gain[...]))
        elif tile < 12:
            u = turned(u, k_gain[...])
        kv[:, (tile - 10) * 128 : (tile - 9) * 128] = u.astype(BF)
    for p in range(PAGES_DEV):
        cache[pl.ds(table[p], 1)] = kv[p * 8 : p * 8 + 8, :].reshape(1, 8, KV_DIM)


def attend_body(flip, place, lengths, q, blocks, far, out, bias, bias_far):
    yh, index, wide, narrow = place[0], place[1], place[2], place[4]
    core = place[3] if not flip else 1 - place[3]
    row = lax.broadcasted_iota(jnp.int32, (128, 1), 0)
    token = (
        wide * TOK_DEV
        + (row % ROWS) // 8 * PAGE
        + row // ROWS * 16
        + core * 8
        + row % 8
    )
    begin = jnp.zeros_like(token)
    end = jnp.int32(0)
    for s in range(3):
        end = end + lengths[s]
        begin = jnp.where(token >= end, end, begin)

    def hide(first_block, lanes, fixed):
        lane = lax.broadcasted_iota(jnp.int32, (1, lanes), 1)
        block = first_block + lane // ROWS
        if fixed:
            source = (1 - yh) * 32 + block
        else:
            source = jnp.where(block <= index, yh, 1 - yh) * 32 + block
        key = source * TOK_DEV + (lane % ROWS) // 8 * PAGE + narrow * 8 + lane % 8
        return jnp.where((key <= token) & (key >= begin), 0.0, HIDDEN_BIAS)

    for chunk in range(4):
        bias[chunk] = hide(chunk * 8, 256, False)
    bias_far[...] = hide(index, ROWS, True)
    half = [q[2 * yl + core] for yl in range(4)]
    half = jnp.concatenate(half, axis=0)
    out[:, Q_DIM:] = jnp.zeros((128, 128), F32)
    for g in range(KV_HEADS):
        heads = [
            half[:, (g * GROUP + h) * HEAD : (g * GROUP + h + 1) * HEAD] for h in range(GROUP)
        ]
        stacked = jnp.concatenate(heads, axis=0)
        denominator = None
        numerator = None
        tail = None
        for chunk in range(5):
            if chunk < 4:
                keys = blocks[chunk * 8 : chunk * 8 + 8, :, g * HEAD : (g + 1) * HEAD]
                keys = keys.reshape(256, HEAD)
                values = blocks[chunk * 8 : chunk * 8 + 8, :, 320 + g * HEAD : 320 + (g + 1) * HEAD]
                values = values.reshape(256, HEAD)
                shade = bias[chunk]
            else:
                keys = far[:, g * HEAD : (g + 1) * HEAD]
                values = far[:, 320 + g * HEAD : 320 + (g + 1) * HEAD]
                shade = bias_far[...]
            scores = lax.dot_general(
                stacked, keys, (((1,), (1,)), ((), ())), preferred_element_type=F32
            )
            wide_scores = scores.reshape(GROUP, 128, keys.shape[0]) * EXP2_SCALE + shade[None]
            weight = jnp.exp2(wide_scores).reshape(GROUP * 128, keys.shape[0])
            product = jnp.dot(weight.astype(BF), values, preferred_element_type=F32)
            numerator = product if numerator is None else numerator + product
            if chunk < 4:
                folded = weight[:, :128] + weight[:, 128:]
                denominator = folded if denominator is None else denominator + folded
            else:
                tail = jnp.sum(weight, axis=1, keepdims=True)
        denominator = jnp.sum(denominator, axis=1, keepdims=True) + tail
        for h in range(GROUP):
            head = g * GROUP + h
            out[:, head * HEAD : (head + 1) * HEAD] = numerator[h * 128 : (h + 1) * 128]
            out[:, Q_DIM + head : Q_DIM + head + 1] = denominator[h * 128 : (h + 1) * 128]


def divide_body(parts, out):
    upper_head = lax.broadcasted_iota(jnp.int32, (ROWS, 128), 1) >= HEAD

    def total(tile):
        at = pl.ds(tile * 128, 128)
        return (parts[0, :, at] + parts[1, :, at]) + (parts[2, :, at] + parts[3, :, at])

    under = total(10)
    for tile in range(10):
        low, high = under[:, 2 * tile : 2 * tile + 1], under[:, 2 * tile + 1 : 2 * tile + 2]
        out[:, tile * 128 : tile * 128 + 128] = (
            total(tile) / jnp.where(upper_head, high, low)
        ).astype(BF)


def mix_body(attended, weight, hidden, out):
    mixed = jnp.dot(attended[...], weight[...], preferred_element_type=F32)
    for n in range(8):
        for p in range(PAGES_DEV):
            at = (n * PAGES_DEV + p) * 8
            out[p, n] = (hidden[p, n].astype(F32) + mixed[at : at + 8]).astype(BF)


def spread(x, axes, count):
    return lax.all_to_all(jnp.broadcast_to(x[None], (count,) + x.shape), axes, 0, 0)


def on_device(hidden_in, attn_gain, qkv_weight, q_gain, k_gain, out_weight, lengths, page_table):
    yh, z, x = lax.axis_index("yh"), lax.axis_index("z"), lax.axis_index("x")
    yl, core = lax.axis_index("yl"), lax.axis_index("c")
    index = z * 4 + x
    wide = yh * 32 + index
    narrow = yl * 2 + core
    place = jnp.stack([yh, index, wide, core, narrow]).astype(jnp.int32)
    swap = [(0, 1), (1, 0)]
    wide_axes = ("yh", "z", "x")

    weight = spread(qkv_weight.T, wide_axes, 64).reshape(QKV_DIM, TOK_DEV)
    hidden5 = hidden_in.reshape(PAGES_DEV, 4, 2, 8, 256)
    gain = attn_gain.reshape(1, 256)
    half_shape = jax.ShapeDtypeStruct((128, 2048), F32)

    def project(flip):
        return call(
            functools.partial(project_body, flip), half_shape, [SM, VM, VM, VM], f"project{flip}"
        )(place, hidden5, gain, weight)

    sent = project(1)
    arrived = lax.ppermute(sent, "c", swap)
    partial = (project(0) + arrived).reshape(4, ROWS, 2048)
    out_part, partial = lax.optimization_barrier((out_weight, partial))
    parts = lax.all_to_all(partial, "yl", 0, 0)

    row = jnp.arange(ROWS, dtype=jnp.int32)
    own = wide * TOK_DEV + row // 8 * PAGE + narrow * 8 + row % 8
    ends = jnp.cumsum(lengths)
    begin = jnp.max(jnp.where(own[:, None] >= ends[None, :], ends[None, :], 0), axis=1)
    position = own - begin
    half = HEAD // 2
    frequency = jnp.exp(jnp.arange(half, dtype=F32) * (-2.0 * math.log(ROPE_BASE) / HEAD))
    angles = position.astype(F32)[:, None] * jnp.tile(frequency, 4)[None, :]
    queries, kv, cache = call(
        rotate_body,
        (
            jax.ShapeDtypeStruct((ROWS, Q_DIM), BF),
            jax.ShapeDtypeStruct((ROWS, KV_DIM), BF),
            jax.ShapeDtypeStruct((PAGES_DEV, 8, KV_DIM), BF),
        ),
        [SM] + [VM] * 5,
        "rotate",
    )(
        page_table,
        parts,
        jnp.cos(angles),
        jnp.sin(angles),
        jnp.tile(q_gain.astype(F32), 2)[None, :],
        jnp.tile(k_gain.astype(F32), 2)[None, :],
    )

    far = lax.ppermute(kv, "yh", swap)
    all_queries = lax.all_gather(queries, ("yl", "c"), axis=0, tiled=False)
    target = jnp.arange(32, dtype=jnp.int32)[:, None, None]
    blocks = lax.all_to_all(jnp.where(target >= index, kv[None], far[None]), ("z", "x"), 0, 0)

    def attend(flip):
        return call(
            functools.partial(attend_body, flip),
            jax.ShapeDtypeStruct((128, SUMS), F32),
            [SM, SM, VM, VM, VM],
            f"attend{flip}",
            [pltpu.VMEM((4, 128, 256), F32), pltpu.VMEM((128, ROWS), F32)],
        )(place, lengths, all_queries, blocks, far)

    sent = attend(1)
    arrived = lax.ppermute(sent, "c", swap)
    sums = (attend(0) + arrived).reshape(4, ROWS, SUMS)
    parts = lax.all_to_all(sums, "yl", 0, 0)
    attended = call(divide_body, jax.ShapeDtypeStruct((ROWS, Q_DIM), BF), [VM], "divide")(parts)
    attended = lax.all_gather(attended, ("yl", "c"), axis=0, tiled=True)
    mixing = spread(out_part, wide_axes, 64).reshape(Q_DIM, 256)
    hidden_out = call(
        mix_body, jax.ShapeDtypeStruct((PAGES_DEV, 8, 8, 256), BF), [VM] * 3, "mix"
    )(attended, mixing, hidden_in.reshape(PAGES_DEV, 8, 8, 256))
    return (hidden_out.reshape(TOK_DEV, 256), cache)


def solution(mesh):
    fine = Mesh(mesh.devices.reshape(2, 8, 4, 4, 2), ("yh", "z", "x", "yl", "c"))
    rows, columns = ("yh", "z", "x"), ("yl", "c")
    return jax.shard_map(
        on_device,
        mesh=fine,
        in_specs=(
            P(rows, columns),
            P(columns),
            P(columns, rows),
            P(),
            P(),
            P(rows, columns),
            P(),
            P(rows),
        ),
        out_specs=(P(rows, columns), P(rows, columns, None)),
        check_vma=False,
    )
```

```python
import functools
import math

import jax
import jax.numpy as jnp
from jax import lax
from jax.experimental import pallas as pl
from jax.experimental.pallas import tpu as pltpu
from jax.sharding import Mesh, PartitionSpec as P

D = 2048
HEADS = 20
KV_HEADS = 5
HEAD = 64
GROUP = 4
Q_DIM = 1280
KV_DIM = 640
QKV_DIM = 1920
TOK_DEV = 256
PAGE = 64
PAGES_DEV = 4
ROWS = 32
PIECE = 30
ROPE_BASE = 10000.0
SUMS = Q_DIM + 128
BF = jnp.bfloat16
F32 = jnp.float32
HIDDEN_BIAS = -1e30
EXP2_SCALE = HEAD ** (-0.5) * math.log2(math.e)

VM = pl.BlockSpec(memory_space=pltpu.VMEM)
SM = pl.BlockSpec(memory_space=pltpu.SMEM)


def call(body, out_shape, in_specs, name, scratch=()):
    many = isinstance(out_shape, tuple)
    return pl.pallas_call(
        body,
        out_shape=out_shape,
        in_specs=in_specs,
        out_specs=(VM,) * len(out_shape) if many else VM,
        scratch_shapes=list(scratch),
        compiler_params=pltpu.CompilerParams(vmem_limit_bytes=48 << 20),
        name=name,
    )


def project_body(flip, place, gain, weight, here, one, two, three, out):
    core = place[3] if not flip else 1 - place[3]
    x = place[5]
    lane = lax.broadcasted_iota(jnp.int32, (128, 128), 1)
    for step, hidden in enumerate((here, one, two, three)):
        rows = [hidden[p, yl, core].astype(F32) for yl in range(4) for p in range(PAGES_DEV)]
        values = jnp.concatenate(rows, axis=0)
        scaled = (values * gain[...].astype(F32)).astype(BF)
        product = lax.dot_general(
            scaled, weight[...], (((1,), (1,)), ((), ())), preferred_element_type=F32
        )
        squares = jnp.sum(values * values, axis=1, keepdims=True)
        owner = lax.rem(x + 4 - step, 4)
        out[pl.ds(owner, 1), :, :128] = jnp.where(lane == 30, squares, product[:, :128])[None]
        out[pl.ds(owner, 1), :, 128:] = product[None, :, 128:]


def rotate_body(table, parts, cosine, sine, q_gain, k_gain, queries, kv, cache):
    lane = lax.broadcasted_iota(jnp.int32, (ROWS, 128), 1)
    upper_head = lane >= HEAD
    lower_part = (lane % HEAD) < HEAD // 2

    def summed(x, tile):
        at = pl.ds(tile * 128, 128)
        low, high = parts[4 * x, :, at] + parts[4 * x + 1, :, at], parts[4 * x + 2, :, at]
        return low + (high + parts[4 * x + 3, :, at])

    tiles = [None] * 15
    inverse = None
    for tile in range(4):
        for x in range(4):
            source = summed(x, tile)
            if x == 0 and tile == 0:
                inverse = lax.rsqrt(source[:, 30:31] / D + 1e-06)
            for piece in range(4):
                z, yh = divmod(tile * 4 + piece, 2)
                start = PIECE * (yh * 32 + z * 4 + x)
                moved = pltpu.roll(source, (start - piece * 32) % 128, 1)
                for place_at in range(start // 128, (start + PIECE - 1) // 128 + 1):
                    first, last = start - place_at * 128, start + PIECE - place_at * 128
                    inside = (lane >= first) & (lane < last)
                    old = tiles[place_at]
                    tiles[place_at] = jnp.where(inside, moved, 0.0 if old is None else old)
    cos = cosine[...]
    sin = jnp.where(lower_part, -sine[...], sine[...])

    def turned(u, gain):
        square = u * u
        both = jnp.sum(jnp.where(upper_head, 0.0, square), axis=1, keepdims=True)
        other = jnp.sum(jnp.where(upper_head, square, 0.0), axis=1, keepdims=True)
        mean = jnp.where(upper_head, other, both) * (1.0 / HEAD)
        w = u * lax.rsqrt(mean + 1e-06) * gain
        partner = jnp.where(lower_part, pltpu.roll(w, 96, 1), pltpu.roll(w, 32, 1))
        return w * cos + partner * sin

    for tile in range(10):
        u = tiles[tile] * inverse
        queries[:, tile * 128 : tile * 128 + 128] = turned(u, q_gain[...]).astype(BF)
    for tile in range(10, 15):
        u = tiles[tile] * inverse
        if tile == 12:
            u = jnp.where(upper_head, u, turned(u, k_gain[...]))
        elif tile < 12:
            u = turned(u, k_gain[...])
        kv[:, (tile - 10) * 128 : (tile - 9) * 128] = u.astype(BF)
    for p in range(PAGES_DEV):
        cache[pl.ds(table[p], 1)] = kv[p * 8 : p * 8 + 8, :].reshape(1, 8, KV_DIM)


def attend_body(flip, place, lengths, q0, q1, q2, q3, blocks, far, out, bias, bias_far):
    yh, index, wide, narrow = place[0], place[1], place[2], place[4]
    row = lax.broadcasted_iota(jnp.int32, (128, 1), 0)
    owner = (narrow + 8 - flip - row // ROWS * 2) & 7
    token = wide * TOK_DEV + (row % ROWS) // 8 * PAGE + owner * 8 + row % 8
    begin = jnp.zeros_like(token)
    end = jnp.int32(0)
    for s in range(3):
        end = end + lengths[s]
        begin = jnp.where(token >= end, end, begin)

    def hide(first_block, lanes, fixed):
        lane = lax.broadcasted_iota(jnp.int32, (1, lanes), 1)
        block = first_block + lane // ROWS
        if fixed:
            source = (1 - yh) * 32 + block
        else:
            source = jnp.where(block <= index, yh, 1 - yh) * 32 + block
        key = source * TOK_DEV + (lane % ROWS) // 8 * PAGE + narrow * 8 + lane % 8
        return jnp.where((key <= token) & (key >= begin), 0.0, HIDDEN_BIAS)

    for chunk in range(4):
        bias[chunk] = hide(chunk * 8, 256, False)
    bias_far[...] = hide(index, ROWS, True)
    half = jnp.concatenate([q0[...], q1[...], q2[...], q3[...]], axis=0)
    owners = [((narrow + 8 - flip - 2 * k) & 7) // 2 for k in range(4)]
    out[:, :, Q_DIM:] = jnp.zeros((4, ROWS, 128), F32)
    for g in range(KV_HEADS):
        heads = [
            half[:, (g * GROUP + h) * HEAD : (g * GROUP + h + 1) * HEAD] for h in range(GROUP)
        ]
        stacked = jnp.concatenate(heads, axis=0)
        denominator = None
        numerator = None
        tail = None
        for chunk in range(5):
            if chunk < 4:
                keys = blocks[chunk * 8 : chunk * 8 + 8, :, g * HEAD : (g + 1) * HEAD]
                keys = keys.reshape(256, HEAD)
                values = blocks[chunk * 8 : chunk * 8 + 8, :, 320 + g * HEAD : 320 + (g + 1) * HEAD]
                values = values.reshape(256, HEAD)
                shade = bias[chunk]
            else:
                keys = far[:, g * HEAD : (g + 1) * HEAD]
                values = far[:, 320 + g * HEAD : 320 + (g + 1) * HEAD]
                shade = bias_far[...]
            scores = lax.dot_general(
                stacked, keys, (((1,), (1,)), ((), ())), preferred_element_type=F32
            )
            wide_scores = scores.reshape(GROUP, 128, keys.shape[0]) * EXP2_SCALE + shade[None]
            weight = jnp.exp2(wide_scores).reshape(GROUP * 128, keys.shape[0])
            product = jnp.dot(weight.astype(BF), values, preferred_element_type=F32)
            numerator = product if numerator is None else numerator + product
            if chunk < 4:
                folded = weight[:, :128] + weight[:, 128:]
                denominator = folded if denominator is None else denominator + folded
            else:
                tail = jnp.sum(weight, axis=1, keepdims=True)
        denominator = jnp.sum(denominator, axis=1, keepdims=True) + tail
        for h in range(GROUP):
            head = g * GROUP + h
            for k in range(4):
                at = slice(h * 128 + k * ROWS, h * 128 + (k + 1) * ROWS)
                to = pl.ds(owners[k], 1)
                out[to, :, head * HEAD : (head + 1) * HEAD] = numerator[at][None]
                out[to, :, Q_DIM + head : Q_DIM + head + 1] = denominator[at][None]


def divide_body(parts, out):
    upper_head = lax.broadcasted_iota(jnp.int32, (ROWS, 128), 1) >= HEAD

    def total(tile):
        at = pl.ds(tile * 128, 128)
        return (parts[0, :, at] + parts[1, :, at]) + (parts[2, :, at] + parts[3, :, at])

    under = total(10)
    for tile in range(10):
        low, high = under[:, 2 * tile : 2 * tile + 1], under[:, 2 * tile + 1 : 2 * tile + 2]
        out[:, tile * 128 : tile * 128 + 128] = (
            total(tile) / jnp.where(upper_head, high, low)
        ).astype(BF)


def mix_body(attended, weight, hidden, out):
    mixed = jnp.dot(attended[...], weight[...], preferred_element_type=F32)
    for n in range(8):
        for p in range(PAGES_DEV):
            at = (n * PAGES_DEV + p) * 8
            out[p, n] = (hidden[p, n].astype(F32) + mixed[at : at + 8]).astype(BF)


def spread(x, axes, count):
    return lax.all_to_all(jnp.broadcast_to(x[None], (count,) + x.shape), axes, 0, 0)


def on_device(hidden_in, attn_gain, qkv_weight, q_gain, k_gain, out_weight, lengths, page_table):
    yh, z, x = lax.axis_index("yh"), lax.axis_index("z"), lax.axis_index("x")
    yl, core = lax.axis_index("yl"), lax.axis_index("c")
    index = z * 4 + x
    wide = yh * 32 + index
    narrow = yl * 2 + core
    place = jnp.stack([yh, index, wide, core, narrow, x]).astype(jnp.int32)
    swap = [(0, 1), (1, 0)]

    def both(own):
        other = lax.ppermute(own, "yh", swap)
        return jnp.where(yh == 0, jnp.stack([own, other]), jnp.stack([other, own]))

    own = jnp.concatenate(
        [jnp.pad(qkv_weight.T, ((0, 2), (0, 0))), jnp.pad(out_weight, ((0, 4), (0, 0)))], axis=0
    )
    shifts = [[(i, (i + step) % 4) for i in range(4)] for step in range(4)]
    hidden = [hidden_in] + [lax.ppermute(hidden_in, "x", shifts[step]) for step in range(1, 4)]
    gathered = spread(both(own), "z", 8)
    weight = gathered[:, :, :32].reshape(512, TOK_DEV)
    mixing = gathered[:, :, 32:52]
    hidden = [h.reshape(PAGES_DEV, 4, 2, 8, 256) for h in hidden]
    gain = attn_gain.reshape(1, 256)
    half_shape = jax.ShapeDtypeStruct((4, 128, 512), F32)

    def project(flip):
        return call(
            functools.partial(project_body, flip), half_shape, [SM] + [VM] * 6, f"project{flip}"
        )(place, gain, weight, *hidden)

    sent = project(1)
    arrived = lax.ppermute(sent, "c", swap)
    partial = (project(0) + arrived).reshape(16, ROWS, 512)
    mixing, partial = lax.optimization_barrier((mixing, partial))
    parts = lax.all_to_all(partial, ("x", "yl"), 0, 0)
    ring = [mixing] + [lax.ppermute(mixing, "x", shifts[step]) for step in range(1, 4)]
    ring = jnp.stack([ring[(3 - k) % 4] for k in range(7)])
    mixing = lax.dynamic_slice_in_dim(ring, 3 - x, 4, 0)
    mixing = mixing.transpose(2, 1, 0, 3, 4).reshape(Q_DIM, 256)

    row = jnp.arange(ROWS, dtype=jnp.int32)
    own = wide * TOK_DEV + row // 8 * PAGE + narrow * 8 + row % 8
    ends = jnp.cumsum(lengths)
    begin = jnp.max(jnp.where(own[:, None] >= ends[None, :], ends[None, :], 0), axis=1)
    position = own - begin
    half = HEAD // 2
    frequency = jnp.exp(jnp.arange(half, dtype=F32) * (-2.0 * math.log(ROPE_BASE) / HEAD))
    angles = position.astype(F32)[:, None] * jnp.tile(frequency, 4)[None, :]
    queries, kv, cache = call(
        rotate_body,
        (
            jax.ShapeDtypeStruct((ROWS, Q_DIM), BF),
            jax.ShapeDtypeStruct((ROWS, KV_DIM), BF),
            jax.ShapeDtypeStruct((PAGES_DEV, 8, KV_DIM), BF),
        ),
        [SM] + [VM] * 5,
        "rotate",
    )(
        page_table,
        parts,
        jnp.cos(angles),
        jnp.sin(angles),
        jnp.tile(q_gain.astype(F32), 2)[None, :],
        jnp.tile(k_gain.astype(F32), 2)[None, :],
    )

    far = lax.ppermute(kv, "yh", swap)
    all_queries = [queries] + [
        lax.ppermute(queries, ("yl", "c"), [(i, (i + step) % 8) for i in range(8)])
        for step in range(1, 8)
    ]
    target = jnp.arange(32, dtype=jnp.int32)[:, None, None]
    blocks = lax.all_to_all(jnp.where(target >= index, kv[None], far[None]), ("z", "x"), 0, 0)

    blocks, mixing, all_queries = lax.optimization_barrier((blocks, mixing, all_queries))

    def attend(flip):
        return call(
            functools.partial(attend_body, flip),
            jax.ShapeDtypeStruct((4, ROWS, SUMS), F32),
            [SM, SM] + [VM] * 6,
            f"attend{flip}",
            [pltpu.VMEM((4, 128, 256), F32), pltpu.VMEM((128, ROWS), F32)],
        )(place, lengths, *all_queries[flip::2], blocks, far)

    sent = attend(1)
    arrived = lax.ppermute(sent, "c", swap)
    parts = lax.all_to_all(attend(0) + arrived, "yl", 0, 0)
    attended = call(divide_body, jax.ShapeDtypeStruct((ROWS, Q_DIM), BF), [VM], "divide")(parts)
    attended = lax.all_gather(attended, ("yl", "c"), axis=0, tiled=True)
    hidden_out = call(
        mix_body, jax.ShapeDtypeStruct((PAGES_DEV, 8, 8, 256), BF), [VM] * 3, "mix"
    )(attended, mixing, hidden_in.reshape(PAGES_DEV, 8, 8, 256))
    return (hidden_out.reshape(TOK_DEV, 256), cache)


def solution(mesh):
    fine = Mesh(mesh.devices.reshape(2, 8, 4, 4, 2), ("yh", "z", "x", "yl", "c"))
    rows, columns = ("yh", "z", "x"), ("yl", "c")
    return jax.shard_map(
        on_device,
        mesh=fine,
        in_specs=(
            P(rows, columns),
            P(columns),
            P(columns, rows),
            P(),
            P(),
            P(rows, columns),
            P(),
            P(rows),
        ),
        out_specs=(P(rows, columns), P(rows, columns, None)),
        check_vma=False,
    )
```

```python
import functools
import math

import jax
import jax.numpy as jnp
from jax import lax
from jax.experimental import pallas as pl
from jax.experimental.pallas import tpu as pltpu
from jax.sharding import Mesh, PartitionSpec as P

D = 2048
HEADS = 20
KV_HEADS = 5
HEAD = 64
GROUP = 4
Q_DIM = 1280
KV_DIM = 640
QKV_DIM = 1920
TOK_DEV = 256
PAGE = 64
PAGES_DEV = 4
ROWS = 32
PIECE = 30
ROPE_BASE = 10000.0
SUMS = Q_DIM + 128
BF = jnp.bfloat16
F32 = jnp.float32
HIDDEN_BIAS = -1e30
EXP2_SCALE = HEAD ** (-0.5) * math.log2(math.e)

VM = pl.BlockSpec(memory_space=pltpu.VMEM)
SM = pl.BlockSpec(memory_space=pltpu.SMEM)


def call(body, out_shape, in_specs, name, scratch=()):
    many = isinstance(out_shape, tuple)
    return pl.pallas_call(
        body,
        out_shape=out_shape,
        in_specs=in_specs,
        out_specs=(VM,) * len(out_shape) if many else VM,
        scratch_shapes=list(scratch),
        compiler_params=pltpu.CompilerParams(vmem_limit_bytes=48 << 20),
        name=name,
    )


def project_body(flip, place, gain, weight, here, one, two, three, out):
    core = place[3] if not flip else 1 - place[3]
    x = place[5]
    lane = lax.broadcasted_iota(jnp.int32, (128, 128), 1)
    for step, hidden in enumerate((here, one, two, three)):
        rows = [hidden[p, yl, core].astype(F32) for yl in range(4) for p in range(PAGES_DEV)]
        values = jnp.concatenate(rows, axis=0)
        scaled = (values * gain[...].astype(F32)).astype(BF)
        product = lax.dot_general(
            scaled, weight[...], (((1,), (1,)), ((), ())), preferred_element_type=F32
        )
        squares = jnp.sum(values * values, axis=1, keepdims=True)
        owner = lax.rem(x + 4 - step, 4)
        out[pl.ds(owner, 1), :, :128] = jnp.where(lane == 30, squares, product[:, :128])[None]
        out[pl.ds(owner, 1), :, 128:] = product[None, :, 128:]


def rotate_body(table, parts, cosine, sine, q_gain, k_gain, queries, kv, cache):
    lane = lax.broadcasted_iota(jnp.int32, (ROWS, 128), 1)
    upper_head = lane >= HEAD
    lower_part = (lane % HEAD) < HEAD // 2

    def summed(x, tile):
        at = pl.ds(tile * 128, 128)
        low, high = parts[4 * x, :, at] + parts[4 * x + 1, :, at], parts[4 * x + 2, :, at]
        return low + (high + parts[4 * x + 3, :, at])

    tiles = [None] * 15
    inverse = None
    for tile in range(4):
        for x in range(4):
            source = summed(x, tile)
            if x == 0 and tile == 0:
                inverse = lax.rsqrt(source[:, 30:31] / D + 1e-06)
            for piece in range(4):
                yh, z = divmod(tile * 4 + piece, 8)
                start = PIECE * (yh * 32 + z * 4 + x)
                moved = pltpu.roll(source, (start - piece * 32) % 128, 1)
                for place_at in range(start // 128, (start + PIECE - 1) // 128 + 1):
                    first, last = start - place_at * 128, start + PIECE - place_at * 128
                    inside = (lane >= first) & (lane < last)
                    old = tiles[place_at]
                    tiles[place_at] = jnp.where(inside, moved, 0.0 if old is None else old)
    cos = cosine[...]
    sin = jnp.where(lower_part, -sine[...], sine[...])

    def turned(u, gain):
        square = u * u
        both = jnp.sum(jnp.where(upper_head, 0.0, square), axis=1, keepdims=True)
        other = jnp.sum(jnp.where(upper_head, square, 0.0), axis=1, keepdims=True)
        mean = jnp.where(upper_head, other, both) * (1.0 / HEAD)
        w = u * lax.rsqrt(mean + 1e-06) * gain
        partner = jnp.where(lower_part, pltpu.roll(w, 96, 1), pltpu.roll(w, 32, 1))
        return w * cos + partner * sin

    for tile in range(10):
        u = tiles[tile] * inverse
        queries[:, tile * 128 : tile * 128 + 128] = turned(u, q_gain[...]).astype(BF)
    for tile in range(10, 15):
        u = tiles[tile] * inverse
        if tile == 12:
            u = jnp.where(upper_head, u, turned(u, k_gain[...]))
        elif tile < 12:
            u = turned(u, k_gain[...])
        kv[:, (tile - 10) * 128 : (tile - 9) * 128] = u.astype(BF)
    for p in range(PAGES_DEV):
        cache[pl.ds(table[p], 1)] = kv[p * 8 : p * 8 + 8, :].reshape(1, 8, KV_DIM)


def attend_body(flip, place, lengths, q, blocks, far, out, bias, bias_far):
    yh, index, wide, narrow, yl = place[0], place[1], place[2], place[4], place[6]
    core = place[3] if not flip else 1 - place[3]
    row = lax.broadcasted_iota(jnp.int32, (128, 1), 0)
    owner = ((yl + 4 - row // ROWS) & 3) * 2 + core
    token = wide * TOK_DEV + (row % ROWS) // 8 * PAGE + owner * 8 + row % 8
    begin = jnp.zeros_like(token)
    end = jnp.int32(0)
    for s in range(3):
        end = end + lengths[s]
        begin = jnp.where(token >= end, end, begin)

    def hide(first_block, lanes, fixed):
        lane = lax.broadcasted_iota(jnp.int32, (1, lanes), 1)
        block = first_block + lane // ROWS
        if fixed:
            source = (1 - yh) * 32 + block
        else:
            source = jnp.where(block <= index, yh, 1 - yh) * 32 + block
        key = source * TOK_DEV + (lane % ROWS) // 8 * PAGE + narrow * 8 + lane % 8
        return jnp.where((key <= token) & (key >= begin), 0.0, HIDDEN_BIAS)

    for chunk in range(4):
        bias[chunk] = hide(chunk * 8, 256, False)
    bias_far[...] = hide(index, ROWS, True)
    half = q[...].reshape(128, Q_DIM)
    owners = [(yl + 4 - k) & 3 for k in range(4)]
    out[:, :, Q_DIM:] = jnp.zeros((4, ROWS, 128), F32)
    for g in range(KV_HEADS):
        heads = [
            half[:, (g * GROUP + h) * HEAD : (g * GROUP + h + 1) * HEAD] for h in range(GROUP)
        ]
        stacked = jnp.concatenate(heads, axis=0)
        denominator = None
        numerator = None
        tail = None
        for chunk in range(5):
            if chunk < 4:
                keys = blocks[chunk * 8 : chunk * 8 + 8, :, g * HEAD : (g + 1) * HEAD]
                keys = keys.reshape(256, HEAD)
                values = blocks[chunk * 8 : chunk * 8 + 8, :, 320 + g * HEAD : 320 + (g + 1) * HEAD]
                values = values.reshape(256, HEAD)
                shade = bias[chunk]
            else:
                keys = far[:, g * HEAD : (g + 1) * HEAD]
                values = far[:, 320 + g * HEAD : 320 + (g + 1) * HEAD]
                shade = bias_far[...]
            scores = lax.dot_general(
                stacked, keys, (((1,), (1,)), ((), ())), preferred_element_type=F32
            )
            wide_scores = scores.reshape(GROUP, 128, keys.shape[0]) * EXP2_SCALE + shade[None]
            weight = jnp.exp2(wide_scores).reshape(GROUP * 128, keys.shape[0])
            product = jnp.dot(weight.astype(BF), values, preferred_element_type=F32)
            numerator = product if numerator is None else numerator + product
            if chunk < 4:
                folded = weight[:, :128] + weight[:, 128:]
                denominator = folded if denominator is None else denominator + folded
            else:
                tail = jnp.sum(weight, axis=1, keepdims=True)
        denominator = jnp.sum(denominator, axis=1, keepdims=True) + tail
        for h in range(GROUP):
            head = g * GROUP + h
            for k in range(4):
                at = slice(h * 128 + k * ROWS, h * 128 + (k + 1) * ROWS)
                to = pl.ds(owners[k], 1)
                out[to, :, head * HEAD : (head + 1) * HEAD] = numerator[at][None]
                out[to, :, Q_DIM + head : Q_DIM + head + 1] = denominator[at][None]


def divide_body(parts, out):
    upper_head = lax.broadcasted_iota(jnp.int32, (ROWS, 128), 1) >= HEAD

    def total(tile):
        at = pl.ds(tile * 128, 128)
        return (parts[0, :, at] + parts[1, :, at]) + (parts[2, :, at] + parts[3, :, at])

    under = total(10)
    for tile in range(10):
        low, high = under[:, 2 * tile : 2 * tile + 1], under[:, 2 * tile + 1 : 2 * tile + 2]
        out[:, tile * 128 : tile * 128 + 128] = (
            total(tile) / jnp.where(upper_head, high, low)
        ).astype(BF)


def mix_body(attended, weight, hidden, out):
    mixed = jnp.dot(attended[...], weight[...], preferred_element_type=F32)
    for n in range(8):
        for p in range(PAGES_DEV):
            at = (n * PAGES_DEV + p) * 8
            out[p, n] = (hidden[p, n].astype(F32) + mixed[at : at + 8]).astype(BF)


def order_body(place, blocks, out):
    x, z = place[5], place[1] // 4
    for i in range(4):
        for k in range(8):
            at = ((z + 8 - k) & 7) * 4 + ((x + 4 - i) & 3)
            for yh in range(2):
                out[pl.ds(yh * 32 + at, 1)] = blocks[i, k, yh][None]


def spread(x, axes, count):
    return lax.all_to_all(jnp.broadcast_to(x[None], (count,) + x.shape), axes, 0, 0)


def on_device(hidden_in, attn_gain, qkv_weight, q_gain, k_gain, out_weight, lengths, page_table):
    yh, z, x = lax.axis_index("yh"), lax.axis_index("z"), lax.axis_index("x")
    yl, core = lax.axis_index("yl"), lax.axis_index("c")
    index = z * 4 + x
    wide = yh * 32 + index
    narrow = yl * 2 + core
    place = jnp.stack([yh, index, wide, core, narrow, x, yl]).astype(jnp.int32)
    swap = [(0, 1), (1, 0)]

    def shift(value, axis, count, step):
        return lax.ppermute(value, axis, [(i, (i + step) % count) for i in range(count)])

    def gather(value, axis, count):
        step = 1
        while step < count:
            value = jnp.concatenate([value, shift(value, axis, count, step)], axis=0)
            step *= 2
        return value

    hidden = [hidden_in] + [shift(hidden_in, "x", 4, step) for step in range(1, 4)]
    columns = jnp.pad(qkv_weight.T, ((0, 2), (0, 0)))
    weight = spread(columns, ("yh", "z"), 16).reshape(512, TOK_DEV)
    other = lax.ppermute(out_weight, "yh", swap)
    weight, other = lax.optimization_barrier((weight, other))
    mixing = jnp.where(yh == 0, jnp.stack([out_weight, other]), jnp.stack([other, out_weight]))
    hidden = [h.reshape(PAGES_DEV, 4, 2, 8, 256) for h in hidden]
    gain = attn_gain.reshape(1, 256)
    half_shape = jax.ShapeDtypeStruct((4, 128, 512), F32)

    def project(flip):
        return call(
            functools.partial(project_body, flip), half_shape, [SM] + [VM] * 6, f"project{flip}"
        )(place, gain, weight, *hidden)

    sent = project(1)
    arrived = lax.ppermute(sent, "c", swap)
    partial = (project(0) + arrived).reshape(16, ROWS, 512)
    mixing, partial = lax.optimization_barrier((mixing, partial))
    parts = lax.all_to_all(partial, ("x", "yl"), 0, 0)
    mixing = gather(mixing[None], "z", 8)
    mixing, parts = lax.optimization_barrier((mixing, parts))

    row = jnp.arange(ROWS, dtype=jnp.int32)
    own = wide * TOK_DEV + row // 8 * PAGE + narrow * 8 + row % 8
    ends = jnp.cumsum(lengths)
    begin = jnp.max(jnp.where(own[:, None] >= ends[None, :], ends[None, :], 0), axis=1)
    position = own - begin
    half = HEAD // 2
    frequency = jnp.exp(jnp.arange(half, dtype=F32) * (-2.0 * math.log(ROPE_BASE) / HEAD))
    angles = position.astype(F32)[:, None] * jnp.tile(frequency, 4)[None, :]
    queries, kv, cache = call(
        rotate_body,
        (
            jax.ShapeDtypeStruct((ROWS, Q_DIM), BF),
            jax.ShapeDtypeStruct((ROWS, KV_DIM), BF),
            jax.ShapeDtypeStruct((PAGES_DEV, 8, KV_DIM), BF),
        ),
        [SM] + [VM] * 5,
        "rotate",
    )(
        page_table,
        parts,
        jnp.cos(angles),
        jnp.sin(angles),
        jnp.tile(q_gain.astype(F32), 2)[None, :],
        jnp.tile(k_gain.astype(F32), 2)[None, :],
    )

    far = lax.ppermute(kv, "yh", swap)
    kept = gather(queries[None], "yl", 4)
    given = lax.ppermute(kept, "c", swap)
    mixing = call(order_body, jax.ShapeDtypeStruct((64, 20, 256), BF), [SM, VM], "order")(
        place, gather(mixing[None], "x", 4)
    ).reshape(Q_DIM, 256)
    target = jnp.arange(32, dtype=jnp.int32)[:, None, None]
    blocks = lax.all_to_all(jnp.where(target >= index, kv[None], far[None]), ("z", "x"), 0, 0)

    blocks, mixing, kept, given = lax.optimization_barrier((blocks, mixing, kept, given))

    def attend(flip):
        return call(
            functools.partial(attend_body, flip),
            jax.ShapeDtypeStruct((4, ROWS, SUMS), F32),
            [SM, SM] + [VM] * 3,
            f"attend{flip}",
            [pltpu.VMEM((4, 128, 256), F32), pltpu.VMEM((128, ROWS), F32)],
        )(place, lengths, given if flip else kept, blocks, far)

    sent = attend(1)
    arrived = lax.ppermute(sent, "c", swap)
    parts = lax.all_to_all(attend(0) + arrived, "yl", 0, 0)
    attended = call(divide_body, jax.ShapeDtypeStruct((ROWS, Q_DIM), BF), [VM], "divide")(parts)
    attended = lax.all_gather(attended, ("yl", "c"), axis=0, tiled=True)
    hidden_out = call(
        mix_body, jax.ShapeDtypeStruct((PAGES_DEV, 8, 8, 256), BF), [VM] * 3, "mix"
    )(attended, mixing, hidden_in.reshape(PAGES_DEV, 8, 8, 256))
    return (hidden_out.reshape(TOK_DEV, 256), cache)


def solution(mesh):
    fine = Mesh(mesh.devices.reshape(2, 8, 4, 4, 2), ("yh", "z", "x", "yl", "c"))
    rows, columns = ("yh", "z", "x"), ("yl", "c")
    return jax.shard_map(
        on_device,
        mesh=fine,
        in_specs=(
            P(rows, columns),
            P(columns),
            P(columns, rows),
            P(),
            P(),
            P(rows, columns),
            P(),
            P(rows),
        ),
        out_specs=(P(rows, columns), P(rows, columns, None)),
        check_vma=False,
    )
```

```python
import functools
import math

import jax
import jax.numpy as jnp
from jax import lax
from jax.experimental import pallas as pl
from jax.experimental.pallas import tpu as pltpu
from jax.sharding import Mesh, PartitionSpec as P

D = 2048
HEADS = 20
KV_HEADS = 5
HEAD = 64
GROUP = 4
Q_DIM = 1280
KV_DIM = 640
QKV_DIM = 1920
TOK_DEV = 256
PAGE = 64
PAGES_DEV = 4
ROWS = 32
PIECE = 30
ROPE_BASE = 10000.0
SUMS = Q_DIM + 128
BF = jnp.bfloat16
F32 = jnp.float32
HIDDEN_BIAS = -1e30
EXP2_SCALE = HEAD ** (-0.5) * math.log2(math.e)

VM = pl.BlockSpec(memory_space=pltpu.VMEM)
SM = pl.BlockSpec(memory_space=pltpu.SMEM)


def call(body, out_shape, in_specs, name, scratch=()):
    many = isinstance(out_shape, tuple)
    return pl.pallas_call(
        body,
        out_shape=out_shape,
        in_specs=in_specs,
        out_specs=(VM,) * len(out_shape) if many else VM,
        scratch_shapes=list(scratch),
        compiler_params=pltpu.CompilerParams(vmem_limit_bytes=48 << 20),
        name=name,
    )


def project_body(flip, place, gain, weight, hidden, out):
    core = place[3] if not flip else 1 - place[3]
    x = place[5]
    lane = lax.broadcasted_iota(jnp.int32, (128, 128), 1)
    for step in range(4):
        rows = [hidden[step, p, yl, core].astype(F32) for yl in range(4) for p in range(PAGES_DEV)]
        values = jnp.concatenate(rows, axis=0)
        scaled = (values * gain[...].astype(F32)).astype(BF)
        product = lax.dot_general(
            scaled, weight[...], (((1,), (1,)), ((), ())), preferred_element_type=F32
        )
        squares = jnp.sum(values * values, axis=1, keepdims=True)
        owner = lax.rem(x + 4 - step, 4)
        out[pl.ds(owner, 1), :, :128] = jnp.where(lane == 30, squares, product[:, :128])[None]
        out[pl.ds(owner, 1), :, 128:] = product[None, :, 128:]


def rotate_body(table, parts, cosine, sine, q_gain, k_gain, queries, kv, cache):
    lane = lax.broadcasted_iota(jnp.int32, (ROWS, 128), 1)
    upper_head = lane >= HEAD
    lower_part = (lane % HEAD) < HEAD // 2

    def summed(x, tile):
        at = pl.ds(tile * 128, 128)
        low, high = parts[4 * x, :, at] + parts[4 * x + 1, :, at], parts[4 * x + 2, :, at]
        return low + (high + parts[4 * x + 3, :, at])

    tiles = [None] * 15
    inverse = None
    for tile in range(4):
        for x in range(4):
            source = summed(x, tile)
            if x == 0 and tile == 0:
                inverse = lax.rsqrt(source[:, 30:31] / D + 1e-06)
            for piece in range(4):
                yh, z = divmod(tile * 4 + piece, 8)
                start = PIECE * (yh * 32 + z * 4 + x)
                moved = pltpu.roll(source, (start - piece * 32) % 128, 1)
                for place_at in range(start // 128, (start + PIECE - 1) // 128 + 1):
                    first, last = start - place_at * 128, start + PIECE - place_at * 128
                    inside = (lane >= first) & (lane < last)
                    old = tiles[place_at]
                    tiles[place_at] = jnp.where(inside, moved, 0.0 if old is None else old)
    cos = cosine[...]
    sin = jnp.where(lower_part, -sine[...], sine[...])

    def turned(u, gain):
        square = u * u
        both = jnp.sum(jnp.where(upper_head, 0.0, square), axis=1, keepdims=True)
        other = jnp.sum(jnp.where(upper_head, square, 0.0), axis=1, keepdims=True)
        mean = jnp.where(upper_head, other, both) * (1.0 / HEAD)
        w = u * lax.rsqrt(mean + 1e-06) * gain
        partner = jnp.where(lower_part, pltpu.roll(w, 96, 1), pltpu.roll(w, 32, 1))
        return w * cos + partner * sin

    for tile in range(10):
        u = tiles[tile] * inverse
        queries[:, tile * 128 : tile * 128 + 128] = turned(u, q_gain[...]).astype(BF)
    for tile in range(10, 15):
        u = tiles[tile] * inverse
        if tile == 12:
            u = jnp.where(upper_head, u, turned(u, k_gain[...]))
        elif tile < 12:
            u = turned(u, k_gain[...])
        kv[:, (tile - 10) * 128 : (tile - 9) * 128] = u.astype(BF)
    for p in range(PAGES_DEV):
        cache[pl.ds(table[p], 1)] = kv[p * 8 : p * 8 + 8, :].reshape(1, 8, KV_DIM)


def attend_body(flip, place, lengths, q, blocks, far, out, bias, bias_far):
    yh, index, wide, narrow, yl = place[0], place[1], place[2], place[4], place[6]
    core = place[3] if not flip else 1 - place[3]
    row = lax.broadcasted_iota(jnp.int32, (128, 1), 0)
    owner = ((yl + 4 - row // ROWS) & 3) * 2 + core
    token = wide * TOK_DEV + (row % ROWS) // 8 * PAGE + owner * 8 + row % 8
    begin = jnp.zeros_like(token)
    end = jnp.int32(0)
    for s in range(3):
        end = end + lengths[s]
        begin = jnp.where(token >= end, end, begin)

    def hide(first_block, lanes, fixed):
        lane = lax.broadcasted_iota(jnp.int32, (1, lanes), 1)
        block = first_block + lane // ROWS
        if fixed:
            source = (1 - yh) * 32 + block
        else:
            source = jnp.where(block <= index, yh, 1 - yh) * 32 + block
        key = source * TOK_DEV + (lane % ROWS) // 8 * PAGE + narrow * 8 + lane % 8
        return jnp.where((key <= token) & (key >= begin), 0.0, HIDDEN_BIAS)

    for chunk in range(4):
        bias[chunk] = hide(chunk * 8, 256, False)
    bias_far[...] = hide(index, ROWS, True)
    half = q[...].reshape(128, Q_DIM)
    owners = [(yl + 4 - k) & 3 for k in range(4)]
    out[:, :, Q_DIM:] = jnp.zeros((4, ROWS, 128), F32)
    for g in range(KV_HEADS):
        heads = [
            half[:, (g * GROUP + h) * HEAD : (g * GROUP + h + 1) * HEAD] for h in range(GROUP)
        ]
        stacked = jnp.concatenate(heads, axis=0)
        denominator = None
        numerator = None
        tail = None
        for chunk in range(5):
            if chunk < 4:
                keys = blocks[chunk * 8 : chunk * 8 + 8, :, g * HEAD : (g + 1) * HEAD]
                keys = keys.reshape(256, HEAD)
                values = blocks[chunk * 8 : chunk * 8 + 8, :, 320 + g * HEAD : 320 + (g + 1) * HEAD]
                values = values.reshape(256, HEAD)
                shade = bias[chunk]
            else:
                keys = far[:, g * HEAD : (g + 1) * HEAD]
                values = far[:, 320 + g * HEAD : 320 + (g + 1) * HEAD]
                shade = bias_far[...]
            scores = lax.dot_general(
                stacked, keys, (((1,), (1,)), ((), ())), preferred_element_type=F32
            )
            wide_scores = scores.reshape(GROUP, 128, keys.shape[0]) * EXP2_SCALE + shade[None]
            weight = jnp.exp2(wide_scores).reshape(GROUP * 128, keys.shape[0])
            product = jnp.dot(weight.astype(BF), values, preferred_element_type=F32)
            numerator = product if numerator is None else numerator + product
            if chunk < 4:
                folded = weight[:, :128] + weight[:, 128:]
                denominator = folded if denominator is None else denominator + folded
            else:
                tail = jnp.sum(weight, axis=1, keepdims=True)
        denominator = jnp.sum(denominator, axis=1, keepdims=True) + tail
        for h in range(GROUP):
            head = g * GROUP + h
            for k in range(4):
                at = slice(h * 128 + k * ROWS, h * 128 + (k + 1) * ROWS)
                to = pl.ds(owners[k], 1)
                out[to, :, head * HEAD : (head + 1) * HEAD] = numerator[at][None]
                out[to, :, Q_DIM + head : Q_DIM + head + 1] = denominator[at][None]


def divide_body(parts, out):
    upper_head = lax.broadcasted_iota(jnp.int32, (ROWS, 128), 1) >= HEAD

    def total(tile):
        at = pl.ds(tile * 128, 128)
        return (parts[0, :, at] + parts[1, :, at]) + (parts[2, :, at] + parts[3, :, at])

    under = total(10)
    for tile in range(10):
        low, high = under[:, 2 * tile : 2 * tile + 1], under[:, 2 * tile + 1 : 2 * tile + 2]
        out[:, tile * 128 : tile * 128 + 128] = (
            total(tile) / jnp.where(upper_head, high, low)
        ).astype(BF)


def mix_body(attended, weight, hidden, out):
    mixed = jnp.dot(attended[...], weight[...], preferred_element_type=F32)
    for n in range(8):
        for p in range(PAGES_DEV):
            at = (n * PAGES_DEV + p) * 8
            out[p, n] = (hidden[p, n].astype(F32) + mixed[at : at + 8]).astype(BF)


def order_body(place, blocks, out):
    x, z = place[5], place[1] // 4
    for i in range(4):
        for k in range(8):
            at = ((z + 8 - k) & 7) * 4 + ((x + 4 - i) & 3)
            for yh in range(2):
                out[pl.ds(yh * 32 + at, 1)] = blocks[i, k, yh][None]


def spread(x, axes, count):
    return lax.all_to_all(jnp.broadcast_to(x[None], (count,) + x.shape), axes, 0, 0)


def on_device(hidden_in, attn_gain, qkv_weight, q_gain, k_gain, out_weight, lengths, page_table):
    yh, z, x = lax.axis_index("yh"), lax.axis_index("z"), lax.axis_index("x")
    yl, core = lax.axis_index("yl"), lax.axis_index("c")
    index = z * 4 + x
    wide = yh * 32 + index
    narrow = yl * 2 + core
    place = jnp.stack([yh, index, wide, core, narrow, x, yl]).astype(jnp.int32)
    swap = [(0, 1), (1, 0)]

    def shift(value, axis, count, step):
        return lax.ppermute(value, axis, [(i, (i + step) % count) for i in range(count)])

    def gather(value, axis, size, count):
        step = 1
        while step < count:
            value = jnp.concatenate([value, shift(value, axis, size, step)], axis=0)
            step *= 2
        return value

    hidden = gather(hidden_in[None], "x", 4, 2)
    columns = jnp.pad(qkv_weight.T, ((0, 2), (0, 0)))
    other = lax.ppermute(out_weight, "yh", swap)
    hidden, columns, other = lax.optimization_barrier((hidden, columns, other))
    mixing = jnp.where(yh == 0, jnp.stack([out_weight, other]), jnp.stack([other, out_weight]))
    weight = spread(columns, ("yh", "z"), 16).reshape(512, TOK_DEV)
    hidden = jnp.concatenate([hidden, shift(hidden, "x", 4, 2)], axis=0)
    hidden = hidden.reshape(4, PAGES_DEV, 4, 2, 8, 256)
    gain = attn_gain.reshape(1, 256)
    half_shape = jax.ShapeDtypeStruct((4, 128, 512), F32)

    def project(flip):
        return call(
            functools.partial(project_body, flip), half_shape, [SM] + [VM] * 3, f"project{flip}"
        )(place, gain, weight, hidden)

    sent = project(1)
    arrived = lax.ppermute(sent, "c", swap)
    partial = (project(0) + arrived).reshape(16, ROWS, 512)
    mixing, partial = lax.optimization_barrier((mixing, partial))
    parts = lax.all_to_all(partial, ("x", "yl"), 0, 0)
    mixing = gather(mixing[None], "z", 8, 4)
    mixing, parts = lax.optimization_barrier((mixing, parts))

    row = jnp.arange(ROWS, dtype=jnp.int32)
    own = wide * TOK_DEV + row // 8 * PAGE + narrow * 8 + row % 8
    ends = jnp.cumsum(lengths)
    begin = jnp.max(jnp.where(own[:, None] >= ends[None, :], ends[None, :], 0), axis=1)
    position = own - begin
    half = HEAD // 2
    frequency = jnp.exp(jnp.arange(half, dtype=F32) * (-2.0 * math.log(ROPE_BASE) / HEAD))
    angles = position.astype(F32)[:, None] * jnp.tile(frequency, 4)[None, :]
    queries, kv, cache = call(
        rotate_body,
        (
            jax.ShapeDtypeStruct((ROWS, Q_DIM), BF),
            jax.ShapeDtypeStruct((ROWS, KV_DIM), BF),
            jax.ShapeDtypeStruct((PAGES_DEV, 8, KV_DIM), BF),
        ),
        [SM] + [VM] * 5,
        "rotate",
    )(
        page_table,
        parts,
        jnp.cos(angles),
        jnp.sin(angles),
        jnp.tile(q_gain.astype(F32), 2)[None, :],
        jnp.tile(k_gain.astype(F32), 2)[None, :],
    )

    far = lax.ppermute(kv, "yh", swap)
    kept = gather(queries[None], "yl", 4, 4)
    given = lax.ppermute(kept, "c", swap)
    mixing = jnp.concatenate([mixing, shift(mixing, "z", 8, 4)], axis=0)
    target = jnp.arange(32, dtype=jnp.int32)[:, None, None]
    blocks = lax.all_to_all(jnp.where(target >= index, kv[None], far[None]), ("z", "x"), 0, 0)

    blocks, mixing, kept, given = lax.optimization_barrier((blocks, mixing, kept, given))

    def attend(flip):
        return call(
            functools.partial(attend_body, flip),
            jax.ShapeDtypeStruct((4, ROWS, SUMS), F32),
            [SM, SM] + [VM] * 3,
            f"attend{flip}",
            [pltpu.VMEM((4, 128, 256), F32), pltpu.VMEM((128, ROWS), F32)],
        )(place, lengths, given if flip else kept, blocks, far)

    sent = attend(1)
    arrived = lax.ppermute(sent, "c", swap)
    parts = lax.all_to_all(attend(0) + arrived, "yl", 0, 0)
    mixing = call(order_body, jax.ShapeDtypeStruct((64, 20, 256), BF), [SM, VM], "order")(
        place, gather(mixing[None], "x", 4, 4)
    ).reshape(Q_DIM, 256)
    attended = call(divide_body, jax.ShapeDtypeStruct((ROWS, Q_DIM), BF), [VM], "divide")(parts)
    attended = lax.all_gather(attended, ("yl", "c"), axis=0, tiled=True)
    hidden_out = call(
        mix_body, jax.ShapeDtypeStruct((PAGES_DEV, 8, 8, 256), BF), [VM] * 3, "mix"
    )(attended, mixing, hidden_in.reshape(PAGES_DEV, 8, 8, 256))
    return (hidden_out.reshape(TOK_DEV, 256), cache)


def solution(mesh):
    fine = Mesh(mesh.devices.reshape(2, 8, 4, 4, 2), ("yh", "z", "x", "yl", "c"))
    rows, columns = ("yh", "z", "x"), ("yl", "c")
    return jax.shard_map(
        on_device,
        mesh=fine,
        in_specs=(
            P(rows, columns),
            P(columns),
            P(columns, rows),
            P(),
            P(),
            P(rows, columns),
            P(),
            P(rows),
        ),
        out_specs=(P(rows, columns), P(rows, columns, None)),
        check_vma=False,
    )
```

```python
import functools
import math

import jax
import jax.numpy as jnp
from jax import lax
from jax.experimental import pallas as pl
from jax.experimental.pallas import tpu as pltpu
from jax.sharding import Mesh, PartitionSpec as P

D = 2048
HEADS = 20
KV_HEADS = 5
HEAD = 64
GROUP = 4
Q_DIM = 1280
KV_DIM = 640
QKV_DIM = 1920
TOK_DEV = 256
PAGE = 64
PAGES_DEV = 4
ROWS = 32
PIECE = 30
ROPE_BASE = 10000.0
SUMS = Q_DIM + 128
BF = jnp.bfloat16
F32 = jnp.float32
HIDDEN_BIAS = -1e30
EXP2_SCALE = HEAD ** (-0.5) * math.log2(math.e)

VM = pl.BlockSpec(memory_space=pltpu.VMEM)
SM = pl.BlockSpec(memory_space=pltpu.SMEM)


def call(body, out_shape, in_specs, name, scratch=()):
    many = isinstance(out_shape, tuple)
    return pl.pallas_call(
        body,
        out_shape=out_shape,
        in_specs=in_specs,
        out_specs=(VM,) * len(out_shape) if many else VM,
        scratch_shapes=list(scratch),
        compiler_params=pltpu.CompilerParams(vmem_limit_bytes=48 << 20),
        name=name,
    )


def project_body(flip, place, gain, weight, here, one, two, three, out):
    core = place[3] if not flip else 1 - place[3]
    x = place[5]
    lane = lax.broadcasted_iota(jnp.int32, (128, 128), 1)
    for step, hidden in enumerate((here, one, two, three)):
        rows = [hidden[p, yl, core].astype(F32) for yl in range(4) for p in range(PAGES_DEV)]
        values = jnp.concatenate(rows, axis=0)
        scaled = (values * gain[...].astype(F32)).astype(BF)
        product = lax.dot_general(
            scaled, weight[...], (((1,), (1,)), ((), ())), preferred_element_type=F32
        )
        squares = jnp.sum(values * values, axis=1, keepdims=True)
        owner = lax.rem(x + 4 - step, 4)
        out[pl.ds(owner, 1), :, :128] = jnp.where(lane == 30, squares, product[:, :128])[None]
        out[pl.ds(owner, 1), :, 128:] = product[None, :, 128:]


def pieces_in_order(parts, first_tile, count):
    lane = lax.broadcasted_iota(jnp.int32, (ROWS, 128), 1)

    def summed(x, tile):
        at = pl.ds(tile * 128, 128)
        low, high = parts[4 * x, :, at] + parts[4 * x + 1, :, at], parts[4 * x + 2, :, at]
        return low + (high + parts[4 * x + 3, :, at])

    inverse = lax.rsqrt(summed(0, 0)[:, 30:31] / D + 1e-06)
    tiles = [None] * count
    for tile in range(4):
        for x in range(4):
            source = None
            for piece in range(4):
                yh, z = divmod(tile * 4 + piece, 8)
                start = PIECE * (yh * 32 + z * 4 + x) - 128 * first_tile
                touched = range(start // 128, (start + PIECE - 1) // 128 + 1)
                touched = [t for t in touched if 0 <= t < count]
                if not touched:
                    continue
                source = summed(x, tile) if source is None else source
                moved = pltpu.roll(source, (start - piece * 32) % 128, 1)
                for t in touched:
                    inside = (lane >= start - t * 128) & (lane < start + PIECE - t * 128)
                    tiles[t] = jnp.where(inside, moved, 0.0 if tiles[t] is None else tiles[t])
    return [u * inverse for u in tiles]


def turn(u, cosine, sine, gain):
    lane = lax.broadcasted_iota(jnp.int32, (ROWS, 128), 1)
    upper_head = lane >= HEAD
    lower_part = (lane % HEAD) < HEAD // 2
    square = u * u
    both = jnp.sum(jnp.where(upper_head, 0.0, square), axis=1, keepdims=True)
    other = jnp.sum(jnp.where(upper_head, square, 0.0), axis=1, keepdims=True)
    mean = jnp.where(upper_head, other, both) * (1.0 / HEAD)
    w = u * lax.rsqrt(mean + 1e-06) * gain[...]
    partner = jnp.where(lower_part, pltpu.roll(w, 96, 1), pltpu.roll(w, 32, 1))
    return w * cosine[...] + partner * jnp.where(lower_part, -sine[...], sine[...])


def rotate_queries_body(parts, cosine, sine, gain, queries):
    for tile, u in enumerate(pieces_in_order(parts, 0, 10)):
        queries[:, tile * 128 : tile * 128 + 128] = turn(u, cosine, sine, gain).astype(BF)


def rotate_keys_body(table, parts, cosine, sine, gain, kv, cache):
    upper_head = lax.broadcasted_iota(jnp.int32, (ROWS, 128), 1) >= HEAD
    for tile, u in enumerate(pieces_in_order(parts, 10, 5)):
        if tile == 2:
            u = jnp.where(upper_head, u, turn(u, cosine, sine, gain))
        elif tile < 2:
            u = turn(u, cosine, sine, gain)
        kv[:, tile * 128 : tile * 128 + 128] = u.astype(BF)
    for p in range(PAGES_DEV):
        cache[pl.ds(table[p], 1)] = kv[p * 8 : p * 8 + 8, :].reshape(1, 8, KV_DIM)


def attend_body(flip, place, lengths, q, blocks, far, out, bias, bias_far):
    yh, index, wide, narrow, yl = place[0], place[1], place[2], place[4], place[6]
    core = place[3] if not flip else 1 - place[3]
    row = lax.broadcasted_iota(jnp.int32, (128, 1), 0)
    owner = ((yl + 4 - row // ROWS) & 3) * 2 + core
    token = wide * TOK_DEV + (row % ROWS) // 8 * PAGE + owner * 8 + row % 8
    begin = jnp.zeros_like(token)
    end = jnp.int32(0)
    for s in range(3):
        end = end + lengths[s]
        begin = jnp.where(token >= end, end, begin)

    def hide(first_block, lanes, fixed):
        lane = lax.broadcasted_iota(jnp.int32, (1, lanes), 1)
        block = first_block + lane // ROWS
        if fixed:
            source = (1 - yh) * 32 + block
        else:
            source = jnp.where(block <= index, yh, 1 - yh) * 32 + block
        key = source * TOK_DEV + (lane % ROWS) // 8 * PAGE + narrow * 8 + lane % 8
        return jnp.where((key <= token) & (key >= begin), 0.0, HIDDEN_BIAS)

    for chunk in range(4):
        bias[chunk] = hide(chunk * 8, 256, False)
    bias_far[...] = hide(index, ROWS, True)
    half = q[...].reshape(128, Q_DIM)
    owners = [(yl + 4 - k) & 3 for k in range(4)]
    out[:, :, Q_DIM:] = jnp.zeros((4, ROWS, 128), F32)
    for g in range(KV_HEADS):
        heads = [
            half[:, (g * GROUP + h) * HEAD : (g * GROUP + h + 1) * HEAD] for h in range(GROUP)
        ]
        stacked = jnp.concatenate(heads, axis=0)
        denominator = None
        numerator = None
        tail = None
        for chunk in range(5):
            if chunk < 4:
                keys = blocks[chunk * 8 : chunk * 8 + 8, :, g * HEAD : (g + 1) * HEAD]
                keys = keys.reshape(256, HEAD)
                values = blocks[chunk * 8 : chunk * 8 + 8, :, 320 + g * HEAD : 320 + (g + 1) * HEAD]
                values = values.reshape(256, HEAD)
                shade = bias[chunk]
            else:
                keys = far[:, g * HEAD : (g + 1) * HEAD]
                values = far[:, 320 + g * HEAD : 320 + (g + 1) * HEAD]
                shade = bias_far[...]
            scores = lax.dot_general(
                stacked, keys, (((1,), (1,)), ((), ())), preferred_element_type=F32
            )
            wide_scores = scores.reshape(GROUP, 128, keys.shape[0]) * EXP2_SCALE + shade[None]
            weight = jnp.exp2(wide_scores).reshape(GROUP * 128, keys.shape[0])
            product = jnp.dot(weight.astype(BF), values, preferred_element_type=F32)
            numerator = product if numerator is None else numerator + product
            if chunk < 4:
                folded = weight[:, :128] + weight[:, 128:]
                denominator = folded if denominator is None else denominator + folded
            else:
                tail = jnp.sum(weight, axis=1, keepdims=True)
        denominator = jnp.sum(denominator, axis=1, keepdims=True) + tail
        for h in range(GROUP):
            head = g * GROUP + h
            for k in range(4):
                at = slice(h * 128 + k * ROWS, h * 128 + (k + 1) * ROWS)
                to = pl.ds(owners[k], 1)
                out[to, :, head * HEAD : (head + 1) * HEAD] = numerator[at][None]
                out[to, :, Q_DIM + head : Q_DIM + head + 1] = denominator[at][None]


def divide_body(parts, out):
    upper_head = lax.broadcasted_iota(jnp.int32, (ROWS, 128), 1) >= HEAD

    def total(tile):
        at = pl.ds(tile * 128, 128)
        return (parts[0, :, at] + parts[1, :, at]) + (parts[2, :, at] + parts[3, :, at])

    under = total(10)
    for tile in range(10):
        low, high = under[:, 2 * tile : 2 * tile + 1], under[:, 2 * tile + 1 : 2 * tile + 2]
        out[:, tile * 128 : tile * 128 + 128] = (
            total(tile) / jnp.where(upper_head, high, low)
        ).astype(BF)


def mix_body(attended, weight, hidden, out):
    mixed = jnp.dot(attended[...], weight[...], preferred_element_type=F32)
    for n in range(8):
        for p in range(PAGES_DEV):
            at = (n * PAGES_DEV + p) * 8
            out[p, n] = (hidden[p, n].astype(F32) + mixed[at : at + 8]).astype(BF)


def order_body(place, blocks, out):
    x, z = place[5], place[1] // 4
    for i in range(4):
        for k in range(8):
            at = ((z + 8 - k) & 7) * 4 + ((x + 4 - i) & 3)
            for yh in range(2):
                out[pl.ds(yh * 32 + at, 1)] = blocks[i, yh, k][None]


def spread(x, axes, count):
    return lax.all_to_all(jnp.broadcast_to(x[None], (count,) + x.shape), axes, 0, 0)


def on_device(hidden_in, attn_gain, qkv_weight, q_gain, k_gain, out_weight, lengths, page_table):
    yh, z, x = lax.axis_index("yh"), lax.axis_index("z"), lax.axis_index("x")
    yl, core = lax.axis_index("yl"), lax.axis_index("c")
    index = z * 4 + x
    wide = yh * 32 + index
    narrow = yl * 2 + core
    place = jnp.stack([yh, index, wide, core, narrow, x, yl]).astype(jnp.int32)
    swap = [(0, 1), (1, 0)]

    def shift(value, axis, count, step):
        return lax.ppermute(value, axis, [(i, (i + step) % count) for i in range(count)])

    def gather(value, axis, size, count):
        step = 1
        while step < count:
            value = jnp.concatenate([value, shift(value, axis, size, step)], axis=0)
            step *= 2
        return value

    columns = jnp.pad(qkv_weight.T, ((0, 2), (0, 0)))
    weight = spread(columns, ("yh", "z"), 16).reshape(512, TOK_DEV)
    hidden = [hidden_in] + [shift(hidden_in, "x", 4, step) for step in range(1, 4)]
    hidden = [h.reshape(PAGES_DEV, 4, 2, 8, 256) for h in hidden]
    gain = attn_gain.reshape(1, 256)
    half_shape = jax.ShapeDtypeStruct((4, 128, 512), F32)

    def project(flip):
        return call(
            functools.partial(project_body, flip), half_shape, [SM] + [VM] * 6, f"project{flip}"
        )(place, gain, weight, *hidden)

    sent = project(1)
    arrived = lax.ppermute(sent, "c", swap)
    partial = (project(0) + arrived).reshape(16, ROWS, 512)
    mixing, partial = lax.optimization_barrier((out_weight[None], partial))
    parts = lax.all_to_all(partial, ("x", "yl"), 0, 0)
    mixing = gather(mixing, "z", 8, 8)
    mixing, parts = lax.optimization_barrier((mixing, parts))

    row = jnp.arange(ROWS, dtype=jnp.int32)
    own = wide * TOK_DEV + row // 8 * PAGE + narrow * 8 + row % 8
    ends = jnp.cumsum(lengths)
    begin = jnp.max(jnp.where(own[:, None] >= ends[None, :], ends[None, :], 0), axis=1)
    position = own - begin
    half = HEAD // 2
    frequency = jnp.exp(jnp.arange(half, dtype=F32) * (-2.0 * math.log(ROPE_BASE) / HEAD))
    angles = position.astype(F32)[:, None] * jnp.tile(frequency, 4)[None, :]
    tables = (jnp.cos(angles), jnp.sin(angles))
    gains = [jnp.tile(g.astype(F32), 2)[None, :] for g in (q_gain, k_gain)]
    kv, cache = call(
        rotate_keys_body,
        (
            jax.ShapeDtypeStruct((ROWS, KV_DIM), BF),
            jax.ShapeDtypeStruct((PAGES_DEV, 8, KV_DIM), BF),
        ),
        [SM] + [VM] * 4,
        "rotate_keys",
    )(page_table, parts, *tables, gains[1])
    far = lax.ppermute(kv, "yh", swap)
    queries = call(
        rotate_queries_body, jax.ShapeDtypeStruct((ROWS, Q_DIM), BF), [VM] * 4, "rotate_queries"
    )(parts, *tables, gains[0])
    far, queries = lax.optimization_barrier((far, queries))
    kept = gather(queries[None], "yl", 4, 4)
    given = lax.ppermute(kept, "c", swap)
    other = lax.ppermute(mixing, "yh", swap)
    mixing = jnp.where(yh == 0, jnp.stack([mixing, other]), jnp.stack([other, mixing]))
    target = jnp.arange(32, dtype=jnp.int32)[:, None, None]
    blocks = lax.all_to_all(jnp.where(target >= index, kv[None], far[None]), ("z", "x"), 0, 0)

    blocks, mixing, kept, given = lax.optimization_barrier((blocks, mixing, kept, given))

    def attend(flip):
        return call(
            functools.partial(attend_body, flip),
            jax.ShapeDtypeStruct((4, ROWS, SUMS), F32),
            [SM, SM] + [VM] * 3,
            f"attend{flip}",
            [pltpu.VMEM((4, 128, 256), F32), pltpu.VMEM((128, ROWS), F32)],
        )(place, lengths, given if flip else kept, blocks, far)

    sent = attend(1)
    arrived = lax.ppermute(sent, "c", swap)
    parts = lax.all_to_all(attend(0) + arrived, "yl", 0, 0)
    mixing = gather(mixing[None], "x", 4, 2)
    mixing, parts = lax.optimization_barrier((mixing, parts))
    mixing = jnp.concatenate([mixing, shift(mixing, "x", 4, 2)], axis=0)
    attended = call(divide_body, jax.ShapeDtypeStruct((ROWS, Q_DIM), BF), [VM], "divide")(parts)
    attended = lax.all_gather(attended, ("yl", "c"), axis=0, tiled=True)
    attended, mixing = lax.optimization_barrier((attended, mixing))
    mixing = call(order_body, jax.ShapeDtypeStruct((64, 20, 256), BF), [SM, VM], "order")(
        place, mixing
    ).reshape(Q_DIM, 256)
    hidden_out = call(
        mix_body, jax.ShapeDtypeStruct((PAGES_DEV, 8, 8, 256), BF), [VM] * 3, "mix"
    )(attended, mixing, hidden_in.reshape(PAGES_DEV, 8, 8, 256))
    return (hidden_out.reshape(TOK_DEV, 256), cache)


def solution(mesh):
    fine = Mesh(mesh.devices.reshape(2, 8, 4, 4, 2), ("yh", "z", "x", "yl", "c"))
    rows, columns = ("yh", "z", "x"), ("yl", "c")
    return jax.shard_map(
        on_device,
        mesh=fine,
        in_specs=(
            P(rows, columns),
            P(columns),
            P(columns, rows),
            P(),
            P(),
            P(rows, columns),
            P(),
            P(rows),
        ),
        out_specs=(P(rows, columns), P(rows, columns, None)),
        check_vma=False,
    )
```

```python
import functools
import math

import jax
import jax.numpy as jnp
from jax import lax
from jax.experimental import pallas as pl
from jax.experimental.pallas import tpu as pltpu
from jax.sharding import Mesh, PartitionSpec as P

D = 2048
HEADS = 20
KV_HEADS = 5
HEAD = 64
GROUP = 4
Q_DIM = 1280
KV_DIM = 640
QKV_DIM = 1920
TOK_DEV = 256
PAGE = 64
PAGES_DEV = 4
ROWS = 32
PIECE = 30
ROPE_BASE = 10000.0
SUMS = Q_DIM + 128
BF = jnp.bfloat16
F32 = jnp.float32
HIDDEN_BIAS = -1e30
EXP2_SCALE = HEAD ** (-0.5) * math.log2(math.e)

VM = pl.BlockSpec(memory_space=pltpu.VMEM)
SM = pl.BlockSpec(memory_space=pltpu.SMEM)


def call(body, out_shape, in_specs, name, scratch=()):
    many = isinstance(out_shape, tuple)
    return pl.pallas_call(
        body,
        out_shape=out_shape,
        in_specs=in_specs,
        out_specs=(VM,) * len(out_shape) if many else VM,
        scratch_shapes=list(scratch),
        compiler_params=pltpu.CompilerParams(vmem_limit_bytes=48 << 20),
        name=name,
    )


def project_body(flip, place, gain, weight, here, one, two, three, out):
    core = place[3] if not flip else 1 - place[3]
    x = place[5]
    lane = lax.broadcasted_iota(jnp.int32, (128, 128), 1)
    for step, hidden in enumerate((here, one, two, three)):
        rows = [hidden[p, yl, core].astype(F32) for yl in range(4) for p in range(PAGES_DEV)]
        values = jnp.concatenate(rows, axis=0)
        scaled = (values * gain[...].astype(F32)).astype(BF)
        product = lax.dot_general(
            scaled, weight[...], (((1,), (1,)), ((), ())), preferred_element_type=F32
        )
        squares = jnp.sum(values * values, axis=1, keepdims=True)
        owner = lax.rem(x + 4 - step, 4)
        out[pl.ds(owner, 1), :, :128] = jnp.where(lane == 30, squares, product[:, :128])[None]
        out[pl.ds(owner, 1), :, 128:] = product[None, :, 128:]


def pieces_in_order(parts, first_tile, count):
    lane = lax.broadcasted_iota(jnp.int32, (ROWS, 128), 1)

    def summed(x, tile):
        at = pl.ds(tile * 128, 128)
        low, high = parts[4 * x, :, at] + parts[4 * x + 1, :, at], parts[4 * x + 2, :, at]
        return low + (high + parts[4 * x + 3, :, at])

    inverse = lax.rsqrt(summed(0, 0)[:, 30:31] / D + 1e-06)
    tiles = [None] * count
    for tile in range(4):
        for x in range(4):
            source = None
            for piece in range(4):
                yh, z = divmod(tile * 4 + piece, 8)
                start = PIECE * (yh * 32 + z * 4 + x) - 128 * first_tile
                touched = range(start // 128, (start + PIECE - 1) // 128 + 1)
                touched = [t for t in touched if 0 <= t < count]
                if not touched:
                    continue
                source = summed(x, tile) if source is None else source
                moved = pltpu.roll(source, (start - piece * 32) % 128, 1)
                for t in touched:
                    inside = (lane >= start - t * 128) & (lane < start + PIECE - t * 128)
                    tiles[t] = jnp.where(inside, moved, 0.0 if tiles[t] is None else tiles[t])
    return [u * inverse for u in tiles]


def turn(u, cosine, sine, gain):
    lane = lax.broadcasted_iota(jnp.int32, (ROWS, 128), 1)
    upper_head = lane >= HEAD
    lower_part = (lane % HEAD) < HEAD // 2
    square = u * u
    both = jnp.sum(jnp.where(upper_head, 0.0, square), axis=1, keepdims=True)
    other = jnp.sum(jnp.where(upper_head, square, 0.0), axis=1, keepdims=True)
    mean = jnp.where(upper_head, other, both) * (1.0 / HEAD)
    w = u * lax.rsqrt(mean + 1e-06) * gain[...]
    partner = jnp.where(lower_part, pltpu.roll(w, 96, 1), pltpu.roll(w, 32, 1))
    return w * cosine[...] + partner * jnp.where(lower_part, -sine[...], sine[...])


def rotate_queries_body(parts, cosine, sine, gain, queries):
    for tile, u in enumerate(pieces_in_order(parts, 0, 10)):
        queries[:, tile * 128 : tile * 128 + 128] = turn(u, cosine, sine, gain).astype(BF)


def rotate_keys_body(table, parts, cosine, sine, gain, kv, cache):
    upper_head = lax.broadcasted_iota(jnp.int32, (ROWS, 128), 1) >= HEAD
    for tile, u in enumerate(pieces_in_order(parts, 10, 5)):
        if tile == 2:
            u = jnp.where(upper_head, u, turn(u, cosine, sine, gain))
        elif tile < 2:
            u = turn(u, cosine, sine, gain)
        kv[:, tile * 128 : tile * 128 + 128] = u.astype(BF)
    for p in range(PAGES_DEV):
        cache[pl.ds(table[p], 1)] = kv[p * 8 : p * 8 + 8, :].reshape(1, 8, KV_DIM)


def attend_body(flip, place, lengths, q, blocks, far, out, bias, bias_far):
    yh, index, wide, narrow, yl = place[0], place[1], place[2], place[4], place[6]
    core = place[3] if not flip else 1 - place[3]
    row = lax.broadcasted_iota(jnp.int32, (128, 1), 0)
    owner = ((yl + 4 - row // ROWS) & 3) * 2 + core
    token = wide * TOK_DEV + (row % ROWS) // 8 * PAGE + owner * 8 + row % 8
    begin = jnp.zeros_like(token)
    end = jnp.int32(0)
    for s in range(3):
        end = end + lengths[s]
        begin = jnp.where(token >= end, end, begin)

    def hide(first_block, lanes, fixed):
        lane = lax.broadcasted_iota(jnp.int32, (1, lanes), 1)
        block = first_block + lane // ROWS
        if fixed:
            source = (1 - yh) * 32 + block
        else:
            source = jnp.where(block <= index, yh, 1 - yh) * 32 + block
        key = source * TOK_DEV + (lane % ROWS) // 8 * PAGE + narrow * 8 + lane % 8
        return jnp.where((key <= token) & (key >= begin), 0.0, HIDDEN_BIAS)

    for chunk in range(4):
        bias[chunk] = hide(chunk * 8, 256, False)
    bias_far[...] = hide(index, ROWS, True)
    half = q[...].reshape(128, Q_DIM)
    owners = [(yl + 4 - k) & 3 for k in range(4)]
    out[:, :, Q_DIM:] = jnp.zeros((4, ROWS, 128), F32)
    for g in range(KV_HEADS):
        heads = [
            half[:, (g * GROUP + h) * HEAD : (g * GROUP + h + 1) * HEAD] for h in range(GROUP)
        ]
        stacked = jnp.concatenate(heads, axis=0)
        denominator = None
        numerator = None
        tail = None
        for chunk in range(5):
            if chunk < 4:
                keys = blocks[chunk * 8 : chunk * 8 + 8, :, g * HEAD : (g + 1) * HEAD]
                keys = keys.reshape(256, HEAD)
                values = blocks[chunk * 8 : chunk * 8 + 8, :, 320 + g * HEAD : 320 + (g + 1) * HEAD]
                values = values.reshape(256, HEAD)
                shade = bias[chunk]
            else:
                keys = far[:, g * HEAD : (g + 1) * HEAD]
                values = far[:, 320 + g * HEAD : 320 + (g + 1) * HEAD]
                shade = bias_far[...]
            scores = lax.dot_general(
                stacked, keys, (((1,), (1,)), ((), ())), preferred_element_type=F32
            )
            wide_scores = scores.reshape(GROUP, 128, keys.shape[0]) * EXP2_SCALE + shade[None]
            weight = jnp.exp2(wide_scores).reshape(GROUP * 128, keys.shape[0])
            product = jnp.dot(weight.astype(BF), values, preferred_element_type=F32)
            numerator = product if numerator is None else numerator + product
            if chunk < 4:
                folded = weight[:, :128] + weight[:, 128:]
                denominator = folded if denominator is None else denominator + folded
            else:
                tail = jnp.sum(weight, axis=1, keepdims=True)
        denominator = jnp.sum(denominator, axis=1, keepdims=True) + tail
        for h in range(GROUP):
            head = g * GROUP + h
            for k in range(4):
                at = slice(h * 128 + k * ROWS, h * 128 + (k + 1) * ROWS)
                to = pl.ds(owners[k], 1)
                out[to, :, head * HEAD : (head + 1) * HEAD] = numerator[at][None]
                for lane in (Q_DIM + head, Q_DIM + HEAD + head):
                    out[to, :, lane : lane + 1] = denominator[at][None]


def pack_body(here, there, out):
    lane = lax.broadcasted_iota(jnp.int32, (ROWS, 128), 1)
    for k in range(4):
        for tile in range(11):
            at = pl.ds(tile * 128, 128)
            total = here[k, :, at] + there[k, :, at]
            low = total.astype(BF)
            if tile == 10:
                rest = total - low.astype(F32)
                low = jnp.where(lane < HEAD, low.astype(F32), rest).astype(BF)
            out[k, :, at] = low


def divide_body(parts, out):
    upper_head = lax.broadcasted_iota(jnp.int32, (ROWS, 128), 1) >= HEAD

    def total(tile):
        at = pl.ds(tile * 128, 128)
        four = [parts[k, :, at].astype(F32) for k in range(4)]
        return (four[0] + four[1]) + (four[2] + four[3])

    under = total(10)
    under = under + pltpu.roll(under, HEAD, 1)
    for tile in range(10):
        low, high = under[:, 2 * tile : 2 * tile + 1], under[:, 2 * tile + 1 : 2 * tile + 2]
        out[:, tile * 128 : tile * 128 + 128] = (
            total(tile) / jnp.where(upper_head, high, low)
        ).astype(BF)


def mix_body(attended, weight, hidden, out):
    mixed = jnp.dot(attended[...], weight[...], preferred_element_type=F32)
    for n in range(8):
        for p in range(PAGES_DEV):
            at = (n * PAGES_DEV + p) * 8
            out[p, n] = (hidden[p, n].astype(F32) + mixed[at : at + 8]).astype(BF)


def order_body(place, blocks, out):
    x, z = place[5], place[1] // 4
    for i in range(4):
        for k in range(8):
            at = ((z + 8 - k) & 7) * 4 + ((x + 4 - i) & 3)
            for yh in range(2):
                out[pl.ds(yh * 32 + at, 1)] = blocks[i, yh, k][None]


def spread(x, axes, count):
    return lax.all_to_all(jnp.broadcast_to(x[None], (count,) + x.shape), axes, 0, 0)


def on_device(hidden_in, attn_gain, qkv_weight, q_gain, k_gain, out_weight, lengths, page_table):
    yh, z, x = lax.axis_index("yh"), lax.axis_index("z"), lax.axis_index("x")
    yl, core = lax.axis_index("yl"), lax.axis_index("c")
    index = z * 4 + x
    wide = yh * 32 + index
    narrow = yl * 2 + core
    place = jnp.stack([yh, index, wide, core, narrow, x, yl]).astype(jnp.int32)
    swap = [(0, 1), (1, 0)]

    def shift(value, axis, count, step):
        return lax.ppermute(value, axis, [(i, (i + step) % count) for i in range(count)])

    def gather(value, axis, size, count):
        step = 1
        while step < count:
            value = jnp.concatenate([value, shift(value, axis, size, step)], axis=0)
            step *= 2
        return value

    columns = jnp.pad(qkv_weight.T, ((0, 2), (0, 0)))
    weight = spread(columns, ("yh", "z"), 16).reshape(512, TOK_DEV)
    hidden = [hidden_in] + [shift(hidden_in, "x", 4, step) for step in range(1, 4)]
    hidden = [h.reshape(PAGES_DEV, 4, 2, 8, 256) for h in hidden]
    gain = attn_gain.reshape(1, 256)
    half_shape = jax.ShapeDtypeStruct((4, 128, 512), F32)

    def project(flip):
        return call(
            functools.partial(project_body, flip), half_shape, [SM] + [VM] * 6, f"project{flip}"
        )(place, gain, weight, *hidden)

    sent = project(1)
    arrived = lax.ppermute(sent, "c", swap)
    partial = (project(0) + arrived).reshape(16, ROWS, 512)
    mixing, partial = lax.optimization_barrier((out_weight[None], partial))
    parts = lax.all_to_all(partial, ("x", "yl"), 0, 0)
    mixing = gather(mixing, "z", 8, 8)
    mixing, parts = lax.optimization_barrier((mixing, parts))

    row = jnp.arange(ROWS, dtype=jnp.int32)
    own = wide * TOK_DEV + row // 8 * PAGE + narrow * 8 + row % 8
    ends = jnp.cumsum(lengths)
    begin = jnp.max(jnp.where(own[:, None] >= ends[None, :], ends[None, :], 0), axis=1)
    position = own - begin
    half = HEAD // 2
    frequency = jnp.exp(jnp.arange(half, dtype=F32) * (-2.0 * math.log(ROPE_BASE) / HEAD))
    angles = position.astype(F32)[:, None] * jnp.tile(frequency, 4)[None, :]
    tables = (jnp.cos(angles), jnp.sin(angles))
    gains = [jnp.tile(g.astype(F32), 2)[None, :] for g in (q_gain, k_gain)]
    kv, cache = call(
        rotate_keys_body,
        (
            jax.ShapeDtypeStruct((ROWS, KV_DIM), BF),
            jax.ShapeDtypeStruct((PAGES_DEV, 8, KV_DIM), BF),
        ),
        [SM] + [VM] * 4,
        "rotate_keys",
    )(page_table, parts, *tables, gains[1])
    far = lax.ppermute(kv, "yh", swap)
    queries = call(
        rotate_queries_body, jax.ShapeDtypeStruct((ROWS, Q_DIM), BF), [VM] * 4, "rotate_queries"
    )(parts, *tables, gains[0])
    far, queries = lax.optimization_barrier((far, queries))
    kept = gather(queries[None], "yl", 4, 2)
    other = lax.ppermute(mixing, "yh", swap)
    kept, other = lax.optimization_barrier((kept, other))
    mixing = jnp.where(yh == 0, jnp.stack([mixing, other]), jnp.stack([other, mixing]))
    kept = jnp.concatenate([kept, shift(kept, "yl", 4, 2)], axis=0)
    mixing = gather(mixing[None], "x", 4, 2)
    kept, mixing = lax.optimization_barrier((kept, mixing))
    given = lax.ppermute(kept, "c", swap)
    target = jnp.arange(32, dtype=jnp.int32)[:, None, None]
    blocks = lax.all_to_all(jnp.where(target >= index, kv[None], far[None]), ("z", "x"), 0, 0)

    blocks, mixing, kept, given = lax.optimization_barrier((blocks, mixing, kept, given))

    def attend(flip):
        return call(
            functools.partial(attend_body, flip),
            jax.ShapeDtypeStruct((4, ROWS, SUMS), F32),
            [SM, SM] + [VM] * 3,
            f"attend{flip}",
            [pltpu.VMEM((4, 128, 256), F32), pltpu.VMEM((128, ROWS), F32)],
        )(place, lengths, given if flip else kept, blocks, far)

    sent = attend(1)
    arrived = lax.ppermute(sent, "c", swap)
    packed = call(pack_body, jax.ShapeDtypeStruct((4, ROWS, SUMS), BF), [VM, VM], "pack")(
        attend(0), arrived
    )
    mixing, packed = lax.optimization_barrier((mixing, packed))
    parts = lax.all_to_all(packed, "yl", 0, 0)
    mixing = jnp.concatenate([mixing, shift(mixing, "x", 4, 2)], axis=0)
    mixing = call(order_body, jax.ShapeDtypeStruct((64, 20, 256), BF), [SM, VM], "order")(
        place, mixing
    ).reshape(Q_DIM, 256)
    attended = call(divide_body, jax.ShapeDtypeStruct((ROWS, Q_DIM), BF), [VM], "divide")(parts)
    attended = lax.all_gather(attended, ("yl", "c"), axis=0, tiled=True)
    hidden_out = call(
        mix_body, jax.ShapeDtypeStruct((PAGES_DEV, 8, 8, 256), BF), [VM] * 3, "mix"
    )(attended, mixing, hidden_in.reshape(PAGES_DEV, 8, 8, 256))
    return (hidden_out.reshape(TOK_DEV, 256), cache)


def solution(mesh):
    fine = Mesh(mesh.devices.reshape(2, 8, 4, 4, 2), ("yh", "z", "x", "yl", "c"))
    rows, columns = ("yh", "z", "x"), ("yl", "c")
    return jax.shard_map(
        on_device,
        mesh=fine,
        in_specs=(
            P(rows, columns),
            P(columns),
            P(columns, rows),
            P(),
            P(),
            P(rows, columns),
            P(),
            P(rows),
        ),
        out_specs=(P(rows, columns), P(rows, columns, None)),
        check_vma=False,
    )
```

```python
import functools
import math

import jax
import jax.numpy as jnp
from jax import lax
from jax.experimental import pallas as pl
from jax.experimental.pallas import tpu as pltpu
from jax.sharding import Mesh, PartitionSpec as P

D = 2048
HEADS = 20
KV_HEADS = 5
HEAD = 64
GROUP = 4
Q_DIM = 1280
KV_DIM = 640
QKV_DIM = 1920
TOK_DEV = 256
PAGE = 64
PAGES_DEV = 4
ROWS = 32
PIECE = 30
ROPE_BASE = 10000.0
SUMS = Q_DIM + 128
BF = jnp.bfloat16
F32 = jnp.float32
HIDDEN_BIAS = -1e30
EXP2_SCALE = HEAD ** (-0.5) * math.log2(math.e)

VM = pl.BlockSpec(memory_space=pltpu.VMEM)
SM = pl.BlockSpec(memory_space=pltpu.SMEM)


def call(body, out_shape, in_specs, name, scratch=()):
    many = isinstance(out_shape, tuple)
    return pl.pallas_call(
        body,
        out_shape=out_shape,
        in_specs=in_specs,
        out_specs=(VM,) * len(out_shape) if many else VM,
        scratch_shapes=list(scratch),
        compiler_params=pltpu.CompilerParams(vmem_limit_bytes=48 << 20),
        name=name,
    )


def project_body(flip, place, gain, weight, here, one, two, three, out):
    core = place[3] if not flip else 1 - place[3]
    x = place[5]
    columns = weight[:, :32, :].reshape(512, 256)
    lane = lax.broadcasted_iota(jnp.int32, (128, 128), 1)
    for step, hidden in enumerate((here, one, two, three)):
        rows = [hidden[p, yl, core].astype(F32) for yl in range(4) for p in range(PAGES_DEV)]
        values = jnp.concatenate(rows, axis=0)
        scaled = (values * gain[...].astype(F32)).astype(BF)
        product = lax.dot_general(
            scaled, columns, (((1,), (1,)), ((), ())), preferred_element_type=F32
        )
        squares = jnp.sum(values * values, axis=1, keepdims=True)
        owner = lax.rem(x + 4 - step, 4)
        out[pl.ds(owner, 1), :, :128] = jnp.where(lane == 30, squares, product[:, :128])[None]
        out[pl.ds(owner, 1), :, 128:] = product[None, :, 128:]


def pieces_in_order(parts, first_tile, count):
    lane = lax.broadcasted_iota(jnp.int32, (ROWS, 128), 1)

    def summed(x, tile):
        at = pl.ds(tile * 128, 128)
        low, high = parts[4 * x, :, at] + parts[4 * x + 1, :, at], parts[4 * x + 2, :, at]
        return low + (high + parts[4 * x + 3, :, at])

    inverse = lax.rsqrt(summed(0, 0)[:, 30:31] / D + 1e-06)
    tiles = [None] * count
    for tile in range(4):
        for x in range(4):
            source = None
            for piece in range(4):
                yh, z = divmod(tile * 4 + piece, 8)
                start = PIECE * (yh * 32 + z * 4 + x) - 128 * first_tile
                touched = range(start // 128, (start + PIECE - 1) // 128 + 1)
                touched = [t for t in touched if 0 <= t < count]
                if not touched:
                    continue
                source = summed(x, tile) if source is None else source
                moved = pltpu.roll(source, (start - piece * 32) % 128, 1)
                for t in touched:
                    inside = (lane >= start - t * 128) & (lane < start + PIECE - t * 128)
                    tiles[t] = jnp.where(inside, moved, 0.0 if tiles[t] is None else tiles[t])
    return [u * inverse for u in tiles]


def turn(u, cosine, sine, gain):
    lane = lax.broadcasted_iota(jnp.int32, (ROWS, 128), 1)
    upper_head = lane >= HEAD
    lower_part = (lane % HEAD) < HEAD // 2
    square = u * u
    both = jnp.sum(jnp.where(upper_head, 0.0, square), axis=1, keepdims=True)
    other = jnp.sum(jnp.where(upper_head, square, 0.0), axis=1, keepdims=True)
    mean = jnp.where(upper_head, other, both) * (1.0 / HEAD)
    w = u * lax.rsqrt(mean + 1e-06) * gain[...]
    partner = jnp.where(lower_part, pltpu.roll(w, 96, 1), pltpu.roll(w, 32, 1))
    return w * cosine[...] + partner * jnp.where(lower_part, -sine[...], sine[...])


def rotate_queries_body(parts, cosine, sine, gain, queries):
    for tile, u in enumerate(pieces_in_order(parts, 0, 10)):
        queries[:, tile * 128 : tile * 128 + 128] = turn(u, cosine, sine, gain).astype(BF)


def rotate_keys_body(table, parts, cosine, sine, gain, kv, cache):
    upper_head = lax.broadcasted_iota(jnp.int32, (ROWS, 128), 1) >= HEAD
    for tile, u in enumerate(pieces_in_order(parts, 10, 5)):
        if tile == 2:
            u = jnp.where(upper_head, u, turn(u, cosine, sine, gain))
        elif tile < 2:
            u = turn(u, cosine, sine, gain)
        kv[:, tile * 128 : tile * 128 + 128] = u.astype(BF)
    for p in range(PAGES_DEV):
        cache[pl.ds(table[p], 1)] = kv[p * 8 : p * 8 + 8, :].reshape(1, 8, KV_DIM)


def attend_body(flip, place, lengths, q, blocks, far, out, bias, bias_far):
    yh, index, wide, narrow, yl = place[0], place[1], place[2], place[4], place[6]
    core = place[3] if not flip else 1 - place[3]
    row = lax.broadcasted_iota(jnp.int32, (128, 1), 0)
    owner = ((yl + 4 - row // ROWS) & 3) * 2 + core
    token = wide * TOK_DEV + (row % ROWS) // 8 * PAGE + owner * 8 + row % 8
    begin = jnp.zeros_like(token)
    end = jnp.int32(0)
    for s in range(3):
        end = end + lengths[s]
        begin = jnp.where(token >= end, end, begin)

    def hide(first_block, lanes, fixed):
        lane = lax.broadcasted_iota(jnp.int32, (1, lanes), 1)
        block = first_block + lane // ROWS
        if fixed:
            source = (1 - yh) * 32 + block
        else:
            source = jnp.where(block <= index, yh, 1 - yh) * 32 + block
        key = source * TOK_DEV + (lane % ROWS) // 8 * PAGE + narrow * 8 + lane % 8
        return jnp.where((key <= token) & (key >= begin), 0.0, HIDDEN_BIAS)

    for chunk in range(4):
        bias[chunk] = hide(chunk * 8, 256, False)
    bias_far[...] = hide(index, ROWS, True)
    half = q[...].reshape(128, Q_DIM)
    owners = [(yl + 4 - k) & 3 for k in range(4)]
    out[:, :, Q_DIM:] = jnp.zeros((4, ROWS, 128), F32)
    for g in range(KV_HEADS):
        heads = [
            half[:, (g * GROUP + h) * HEAD : (g * GROUP + h + 1) * HEAD] for h in range(GROUP)
        ]
        stacked = jnp.concatenate(heads, axis=0)
        denominator = None
        numerator = None
        tail = None
        for chunk in range(5):
            if chunk < 4:
                keys = blocks[chunk * 8 : chunk * 8 + 8, :, g * HEAD : (g + 1) * HEAD]
                keys = keys.reshape(256, HEAD)
                values = blocks[chunk * 8 : chunk * 8 + 8, :, 320 + g * HEAD : 320 + (g + 1) * HEAD]
                values = values.reshape(256, HEAD)
                shade = bias[chunk]
            else:
                keys = far[:, g * HEAD : (g + 1) * HEAD]
                values = far[:, 320 + g * HEAD : 320 + (g + 1) * HEAD]
                shade = bias_far[...]
            scores = lax.dot_general(
                stacked, keys, (((1,), (1,)), ((), ())), preferred_element_type=F32
            )
            wide_scores = scores.reshape(GROUP, 128, keys.shape[0]) * EXP2_SCALE + shade[None]
            weight = jnp.exp2(wide_scores).reshape(GROUP * 128, keys.shape[0])
            product = jnp.dot(weight.astype(BF), values, preferred_element_type=F32)
            numerator = product if numerator is None else numerator + product
            if chunk < 4:
                folded = weight[:, :128] + weight[:, 128:]
                denominator = folded if denominator is None else denominator + folded
            else:
                tail = jnp.sum(weight, axis=1, keepdims=True)
        denominator = jnp.sum(denominator, axis=1, keepdims=True) + tail
        for h in range(GROUP):
            head = g * GROUP + h
            for k in range(4):
                at = slice(h * 128 + k * ROWS, h * 128 + (k + 1) * ROWS)
                to = pl.ds(owners[k], 1)
                out[to, :, head * HEAD : (head + 1) * HEAD] = numerator[at][None]
                for lane in (Q_DIM + head, Q_DIM + HEAD + head):
                    out[to, :, lane : lane + 1] = denominator[at][None]


def pack_body(here, there, out):
    lane = lax.broadcasted_iota(jnp.int32, (ROWS, 128), 1)
    for k in range(4):
        for tile in range(11):
            at = pl.ds(tile * 128, 128)
            total = here[k, :, at] + there[k, :, at]
            low = total.astype(BF)
            if tile == 10:
                rest = total - low.astype(F32)
                low = jnp.where(lane < HEAD, low.astype(F32), rest).astype(BF)
            out[k, :, at] = low


def divide_body(parts, out):
    upper_head = lax.broadcasted_iota(jnp.int32, (ROWS, 128), 1) >= HEAD

    def total(tile):
        at = pl.ds(tile * 128, 128)
        four = [parts[k, :, at].astype(F32) for k in range(4)]
        return (four[0] + four[1]) + (four[2] + four[3])

    under = total(10)
    under = under + pltpu.roll(under, HEAD, 1)
    for tile in range(10):
        low, high = under[:, 2 * tile : 2 * tile + 1], under[:, 2 * tile + 1 : 2 * tile + 2]
        out[:, tile * 128 : tile * 128 + 128] = (
            total(tile) / jnp.where(upper_head, high, low)
        ).astype(BF)


def mix_body(attended, weight, hidden, out):
    mixed = jnp.dot(attended[...], weight[...], preferred_element_type=F32)
    for n in range(8):
        for p in range(PAGES_DEV):
            at = (n * PAGES_DEV + p) * 8
            out[p, n] = (hidden[p, n].astype(F32) + mixed[at : at + 8]).astype(BF)


def order_body(place, blocks, out):
    for i in range(4):
        x = (place[5] + 4 - i) & 3
        for k in range(16):
            out[pl.ds(k * 4 + x, 1)] = blocks[i, k, :20][None]


def spread(x, axes, count):
    return lax.all_to_all(jnp.broadcast_to(x[None], (count,) + x.shape), axes, 0, 0)


def on_device(hidden_in, attn_gain, qkv_weight, q_gain, k_gain, out_weight, lengths, page_table):
    yh, z, x = lax.axis_index("yh"), lax.axis_index("z"), lax.axis_index("x")
    yl, core = lax.axis_index("yl"), lax.axis_index("c")
    index = z * 4 + x
    wide = yh * 32 + index
    narrow = yl * 2 + core
    place = jnp.stack([yh, index, wide, core, narrow, x, yl]).astype(jnp.int32)
    swap = [(0, 1), (1, 0)]

    def shift(value, axis, count, step):
        return lax.ppermute(value, axis, [(i, (i + step) % count) for i in range(count)])

    def gather(value, axis, size, count):
        step = 1
        while step < count:
            value = jnp.concatenate([value, shift(value, axis, size, step)], axis=0)
            step *= 2
        return value

    own = [jnp.pad(qkv_weight.T, ((0, 2), (0, 0))), jnp.pad(out_weight, ((0, 4), (0, 0)))]
    weight = spread(jnp.concatenate(own, axis=0), ("yh", "z"), 16)
    hidden = [hidden_in] + [shift(hidden_in, "x", 4, step) for step in range(1, 4)]
    hidden = [h.reshape(PAGES_DEV, 4, 2, 8, 256) for h in hidden]
    gain = attn_gain.reshape(1, 256)
    half_shape = jax.ShapeDtypeStruct((4, 128, 512), F32)

    def project(flip):
        return call(
            functools.partial(project_body, flip), half_shape, [SM] + [VM] * 6, f"project{flip}"
        )(place, gain, weight, *hidden)

    sent = project(1)
    arrived = lax.ppermute(sent, "c", swap)
    partial = (project(0) + arrived).reshape(16, ROWS, 512)
    mixing, partial = lax.optimization_barrier((weight[None, :, 32:], partial))
    parts = lax.all_to_all(partial, ("x", "yl"), 0, 0)
    mixing = gather(mixing, "x", 4, 2)
    mixing, parts = lax.optimization_barrier((mixing, parts))

    row = jnp.arange(ROWS, dtype=jnp.int32)
    own = wide * TOK_DEV + row // 8 * PAGE + narrow * 8 + row % 8
    ends = jnp.cumsum(lengths)
    begin = jnp.max(jnp.where(own[:, None] >= ends[None, :], ends[None, :], 0), axis=1)
    position = own - begin
    half = HEAD // 2
    frequency = jnp.exp(jnp.arange(half, dtype=F32) * (-2.0 * math.log(ROPE_BASE) / HEAD))
    angles = position.astype(F32)[:, None] * jnp.tile(frequency, 4)[None, :]
    tables = (jnp.cos(angles), jnp.sin(angles))
    gains = [jnp.tile(g.astype(F32), 2)[None, :] for g in (q_gain, k_gain)]
    kv, cache = call(
        rotate_keys_body,
        (
            jax.ShapeDtypeStruct((ROWS, KV_DIM), BF),
            jax.ShapeDtypeStruct((PAGES_DEV, 8, KV_DIM), BF),
        ),
        [SM] + [VM] * 4,
        "rotate_keys",
    )(page_table, parts, *tables, gains[1])
    far = lax.ppermute(kv, "yh", swap)
    queries = call(
        rotate_queries_body, jax.ShapeDtypeStruct((ROWS, Q_DIM), BF), [VM] * 4, "rotate_queries"
    )(parts, *tables, gains[0])
    far, queries = lax.optimization_barrier((far, queries))
    kept = gather(queries[None], "yl", 4, 4)
    mixing = jnp.concatenate([mixing, shift(mixing, "x", 4, 2)], axis=0)
    given = lax.ppermute(kept, "c", swap)
    target = jnp.arange(32, dtype=jnp.int32)[:, None, None]
    blocks = lax.all_to_all(jnp.where(target >= index, kv[None], far[None]), ("z", "x"), 0, 0)

    blocks, mixing, kept, given = lax.optimization_barrier((blocks, mixing, kept, given))

    def attend(flip):
        return call(
            functools.partial(attend_body, flip),
            jax.ShapeDtypeStruct((4, ROWS, SUMS), F32),
            [SM, SM] + [VM] * 3,
            f"attend{flip}",
            [pltpu.VMEM((4, 128, 256), F32), pltpu.VMEM((128, ROWS), F32)],
        )(place, lengths, given if flip else kept, blocks, far)

    sent = attend(1)
    arrived = lax.ppermute(sent, "c", swap)
    packed = call(pack_body, jax.ShapeDtypeStruct((4, ROWS, SUMS), BF), [VM, VM], "pack")(
        attend(0), arrived
    )
    mixing, packed = lax.optimization_barrier((mixing, packed))
    parts = lax.all_to_all(packed, "yl", 0, 0)
    mixing = call(order_body, jax.ShapeDtypeStruct((64, 20, 256), BF), [SM, VM], "order")(
        place, mixing
    ).reshape(Q_DIM, 256)
    attended = call(divide_body, jax.ShapeDtypeStruct((ROWS, Q_DIM), BF), [VM], "divide")(parts)
    attended = lax.all_gather(attended, ("yl", "c"), axis=0, tiled=True)
    hidden_out = call(
        mix_body, jax.ShapeDtypeStruct((PAGES_DEV, 8, 8, 256), BF), [VM] * 3, "mix"
    )(attended, mixing, hidden_in.reshape(PAGES_DEV, 8, 8, 256))
    return (hidden_out.reshape(TOK_DEV, 256), cache)


def solution(mesh):
    fine = Mesh(mesh.devices.reshape(2, 8, 4, 4, 2), ("yh", "z", "x", "yl", "c"))
    rows, columns = ("yh", "z", "x"), ("yl", "c")
    return jax.shard_map(
        on_device,
        mesh=fine,
        in_specs=(
            P(rows, columns),
            P(columns),
            P(columns, rows),
            P(),
            P(),
            P(rows, columns),
            P(),
            P(rows),
        ),
        out_specs=(P(rows, columns), P(rows, columns, None)),
        check_vma=False,
    )
```

```python
import functools
import math

import jax
import jax.numpy as jnp
from jax import lax
from jax.experimental import pallas as pl
from jax.experimental.pallas import tpu as pltpu
from jax.sharding import Mesh, PartitionSpec as P

D = 2048
HEADS = 20
KV_HEADS = 5
HEAD = 64
GROUP = 4
Q_DIM = 1280
KV_DIM = 640
QKV_DIM = 1920
TOK_DEV = 256
PAGE = 64
PAGES_DEV = 4
ROWS = 32
PIECE = 30
ROPE_BASE = 10000.0
SUMS = Q_DIM + 128
BF = jnp.bfloat16
F32 = jnp.float32
HIDDEN_BIAS = -1e30
EXP2_SCALE = HEAD ** (-0.5) * math.log2(math.e)

VM = pl.BlockSpec(memory_space=pltpu.VMEM)
SM = pl.BlockSpec(memory_space=pltpu.SMEM)


def call(body, out_shape, in_specs, name, scratch=()):
    many = isinstance(out_shape, tuple)
    return pl.pallas_call(
        body,
        out_shape=out_shape,
        in_specs=in_specs,
        out_specs=(VM,) * len(out_shape) if many else VM,
        scratch_shapes=list(scratch),
        compiler_params=pltpu.CompilerParams(vmem_limit_bytes=48 << 20),
        name=name,
    )


def project_body(flip, place, gain, weight, here, one, two, three, out):
    core = place[3] if not flip else 1 - place[3]
    x = place[5]
    columns = weight[:, :32, :].reshape(512, 256)
    lane = lax.broadcasted_iota(jnp.int32, (128, 128), 1)
    for step, hidden in enumerate((here, one, two, three)):
        rows = [hidden[p, yl, core].astype(F32) for yl in range(4) for p in range(PAGES_DEV)]
        values = jnp.concatenate(rows, axis=0)
        scaled = (values * gain[...].astype(F32)).astype(BF)
        product = lax.dot_general(
            scaled, columns, (((1,), (1,)), ((), ())), preferred_element_type=F32
        )
        squares = jnp.sum(values * values, axis=1, keepdims=True)
        owner = lax.rem(x + 4 - step, 4)
        out[pl.ds(owner, 1), :, :128] = jnp.where(lane == 30, squares, product[:, :128])[None]
        out[pl.ds(owner, 1), :, 128:] = product[None, :, 128:]


def round_body(here, there, out):
    lane = lax.broadcasted_iota(jnp.int32, (128, 128), 1)
    for k in range(4):
        for tile in range(4):
            at = pl.ds(tile * 128, 128)
            total = here[k, :, at] + there[k, :, at]
            low = total.astype(BF)
            if tile == 0:
                rest = pltpu.roll(total - low.astype(F32), 1, 1)
                low = jnp.where(lane == 31, rest, low.astype(F32)).astype(BF)
            if tile >= 2:
                rest = (total - low.astype(F32)).astype(BF)
                out[k, :, pl.ds((7 - tile) * 128, 128)] = rest
            out[k, :, at] = low


def pieces_in_order(parts, first_tile, count):
    lane = lax.broadcasted_iota(jnp.int32, (ROWS, 128), 1)

    def summed(x, tile):
        def part(k):
            value = parts[4 * x + k, :, pl.ds(tile * 128, 128)].astype(F32)
            if tile < 2:
                return value
            return value + parts[4 * x + k, :, pl.ds((7 - tile) * 128, 128)].astype(F32)

        return (part(0) + part(1)) + (part(2) + part(3))

    squares = summed(0, 0)
    inverse = lax.rsqrt((squares[:, 30:31] + squares[:, 31:32]) / D + 1e-06)
    tiles = [None] * count
    for tile in range(4):
        for x in range(4):
            source = None
            for piece in range(4):
                yh, z = divmod(tile * 4 + piece, 8)
                start = PIECE * (yh * 32 + z * 4 + x) - 128 * first_tile
                touched = range(start // 128, (start + PIECE - 1) // 128 + 1)
                touched = [t for t in touched if 0 <= t < count]
                if not touched:
                    continue
                source = summed(x, tile) if source is None else source
                moved = pltpu.roll(source, (start - piece * 32) % 128, 1)
                for t in touched:
                    inside = (lane >= start - t * 128) & (lane < start + PIECE - t * 128)
                    tiles[t] = jnp.where(inside, moved, 0.0 if tiles[t] is None else tiles[t])
    return [u * inverse for u in tiles]


def turn(u, cosine, sine, gain):
    lane = lax.broadcasted_iota(jnp.int32, (ROWS, 128), 1)
    upper_head = lane >= HEAD
    lower_part = (lane % HEAD) < HEAD // 2
    square = u * u
    both = jnp.sum(jnp.where(upper_head, 0.0, square), axis=1, keepdims=True)
    other = jnp.sum(jnp.where(upper_head, square, 0.0), axis=1, keepdims=True)
    mean = jnp.where(upper_head, other, both) * (1.0 / HEAD)
    w = u * lax.rsqrt(mean + 1e-06) * gain[...]
    partner = jnp.where(lower_part, pltpu.roll(w, 96, 1), pltpu.roll(w, 32, 1))
    return w * cosine[...] + partner * jnp.where(lower_part, -sine[...], sine[...])


def rotate_queries_body(parts, cosine, sine, gain, queries):
    for tile, u in enumerate(pieces_in_order(parts, 0, 10)):
        queries[:, tile * 128 : tile * 128 + 128] = turn(u, cosine, sine, gain).astype(BF)


def rotate_keys_body(table, parts, cosine, sine, gain, kv, cache):
    upper_head = lax.broadcasted_iota(jnp.int32, (ROWS, 128), 1) >= HEAD
    for tile, u in enumerate(pieces_in_order(parts, 10, 5)):
        if tile == 2:
            u = jnp.where(upper_head, u, turn(u, cosine, sine, gain))
        elif tile < 2:
            u = turn(u, cosine, sine, gain)
        kv[:, tile * 128 : tile * 128 + 128] = u.astype(BF)
    for p in range(PAGES_DEV):
        cache[pl.ds(table[p], 1)] = kv[p * 8 : p * 8 + 8, :].reshape(1, 8, KV_DIM)


def attend_body(flip, place, lengths, q, blocks, far, out, bias, bias_far):
    yh, index, wide, narrow, yl = place[0], place[1], place[2], place[4], place[6]
    core = place[3] if not flip else 1 - place[3]
    row = lax.broadcasted_iota(jnp.int32, (128, 1), 0)
    owner = ((yl + 4 - row // ROWS) & 3) * 2 + core
    token = wide * TOK_DEV + (row % ROWS) // 8 * PAGE + owner * 8 + row % 8
    begin = jnp.zeros_like(token)
    end = jnp.int32(0)
    for s in range(3):
        end = end + lengths[s]
        begin = jnp.where(token >= end, end, begin)

    def hide(first_block, lanes, fixed):
        lane = lax.broadcasted_iota(jnp.int32, (1, lanes), 1)
        block = first_block + lane // ROWS
        if fixed:
            source = (1 - yh) * 32 + block
        else:
            source = jnp.where(block <= index, yh, 1 - yh) * 32 + block
        key = source * TOK_DEV + (lane % ROWS) // 8 * PAGE + narrow * 8 + lane % 8
        return jnp.where((key <= token) & (key >= begin), 0.0, HIDDEN_BIAS)

    for chunk in range(4):
        bias[chunk] = hide(chunk * 8, 256, False)
    bias_far[...] = hide(index, ROWS, True)
    half = q[...].reshape(128, Q_DIM)
    owners = [(yl + 4 - k) & 3 for k in range(4)]
    out[:, :, Q_DIM:] = jnp.zeros((4, ROWS, 128), F32)
    for g in range(KV_HEADS):
        heads = [
            half[:, (g * GROUP + h) * HEAD : (g * GROUP + h + 1) * HEAD] for h in range(GROUP)
        ]
        stacked = jnp.concatenate(heads, axis=0)
        denominator = None
        numerator = None
        tail = None
        for chunk in range(5):
            if chunk < 4:
                keys = blocks[chunk * 8 : chunk * 8 + 8, :, g * HEAD : (g + 1) * HEAD]
                keys = keys.reshape(256, HEAD)
                values = blocks[chunk * 8 : chunk * 8 + 8, :, 320 + g * HEAD : 320 + (g + 1) * HEAD]
                values = values.reshape(256, HEAD)
                shade = bias[chunk]
            else:
                keys = far[:, g * HEAD : (g + 1) * HEAD]
                values = far[:, 320 + g * HEAD : 320 + (g + 1) * HEAD]
                shade = bias_far[...]
            scores = lax.dot_general(
                stacked, keys, (((1,), (1,)), ((), ())), preferred_element_type=F32
            )
            wide_scores = scores.reshape(GROUP, 128, keys.shape[0]) * EXP2_SCALE + shade[None]
            weight = jnp.exp2(wide_scores).reshape(GROUP * 128, keys.shape[0])
            product = jnp.dot(weight.astype(BF), values, preferred_element_type=F32)
            numerator = product if numerator is None else numerator + product
            if chunk < 4:
                folded = weight[:, :128] + weight[:, 128:]
                denominator = folded if denominator is None else denominator + folded
            else:
                tail = jnp.sum(weight, axis=1, keepdims=True)
        denominator = jnp.sum(denominator, axis=1, keepdims=True) + tail
        for h in range(GROUP):
            head = g * GROUP + h
            for k in range(4):
                at = slice(h * 128 + k * ROWS, h * 128 + (k + 1) * ROWS)
                to = pl.ds(owners[k], 1)
                out[to, :, head * HEAD : (head + 1) * HEAD] = numerator[at][None]
                for lane in (Q_DIM + head, Q_DIM + HEAD + head):
                    out[to, :, lane : lane + 1] = denominator[at][None]


def pack_body(here, there, out):
    lane = lax.broadcasted_iota(jnp.int32, (ROWS, 128), 1)
    for k in range(4):
        for tile in range(11):
            at = pl.ds(tile * 128, 128)
            total = here[k, :, at] + there[k, :, at]
            low = total.astype(BF)
            if tile == 10:
                rest = total - low.astype(F32)
                low = jnp.where(lane < HEAD, low.astype(F32), rest).astype(BF)
            out[k, :, at] = low


def divide_body(parts, out):
    upper_head = lax.broadcasted_iota(jnp.int32, (ROWS, 128), 1) >= HEAD

    def total(tile):
        at = pl.ds(tile * 128, 128)
        four = [parts[k, :, at].astype(F32) for k in range(4)]
        return (four[0] + four[1]) + (four[2] + four[3])

    under = total(10)
    under = under + pltpu.roll(under, HEAD, 1)
    for tile in range(10):
        low, high = under[:, 2 * tile : 2 * tile + 1], under[:, 2 * tile + 1 : 2 * tile + 2]
        out[:, tile * 128 : tile * 128 + 128] = (
            total(tile) / jnp.where(upper_head, high, low)
        ).astype(BF)


def mix_body(attended, weight, hidden, out):
    mixed = jnp.dot(attended[...], weight[...], preferred_element_type=F32)
    for n in range(8):
        for p in range(PAGES_DEV):
            at = (n * PAGES_DEV + p) * 8
            out[p, n] = (hidden[p, n].astype(F32) + mixed[at : at + 8]).astype(BF)


def order_body(place, blocks, out):
    for i in range(4):
        x = (place[5] + 4 - i) & 3
        for k in range(16):
            out[pl.ds(k * 4 + x, 1)] = blocks[i, k, :20][None]


def spread(x, axes, count):
    return lax.all_to_all(jnp.broadcast_to(x[None], (count,) + x.shape), axes, 0, 0)


def on_device(hidden_in, attn_gain, qkv_weight, q_gain, k_gain, out_weight, lengths, page_table):
    yh, z, x = lax.axis_index("yh"), lax.axis_index("z"), lax.axis_index("x")
    yl, core = lax.axis_index("yl"), lax.axis_index("c")
    index = z * 4 + x
    wide = yh * 32 + index
    narrow = yl * 2 + core
    place = jnp.stack([yh, index, wide, core, narrow, x, yl]).astype(jnp.int32)
    swap = [(0, 1), (1, 0)]

    def shift(value, axis, count, step):
        return lax.ppermute(value, axis, [(i, (i + step) % count) for i in range(count)])

    def gather(value, axis, size, count):
        step = 1
        while step < count:
            value = jnp.concatenate([value, shift(value, axis, size, step)], axis=0)
            step *= 2
        return value

    own = [jnp.pad(qkv_weight.T, ((0, 2), (0, 0))), jnp.pad(out_weight, ((0, 4), (0, 0)))]
    weight = spread(jnp.concatenate(own, axis=0), ("yh", "z"), 16)
    hidden = [hidden_in] + [shift(hidden_in, "x", 4, step) for step in range(1, 4)]
    hidden = [h.reshape(PAGES_DEV, 4, 2, 8, 256) for h in hidden]
    gain = attn_gain.reshape(1, 256)
    half_shape = jax.ShapeDtypeStruct((4, 128, 512), F32)

    def project(flip):
        return call(
            functools.partial(project_body, flip), half_shape, [SM] + [VM] * 6, f"project{flip}"
        )(place, gain, weight, *hidden)

    sent = project(1)
    arrived = lax.ppermute(sent, "c", swap)
    partial = call(round_body, jax.ShapeDtypeStruct((4, 128, 768), BF), [VM, VM], "round")(
        project(0), arrived
    ).reshape(16, ROWS, 768)
    mixing, partial = lax.optimization_barrier((weight[None, :, 32:], partial))
    parts = lax.all_to_all(partial, ("x", "yl"), 0, 0)
    mixing = gather(mixing, "x", 4, 2)
    mixing, parts = lax.optimization_barrier((mixing, parts))

    row = jnp.arange(ROWS, dtype=jnp.int32)
    own = wide * TOK_DEV + row // 8 * PAGE + narrow * 8 + row % 8
    ends = jnp.cumsum(lengths)
    begin = jnp.max(jnp.where(own[:, None] >= ends[None, :], ends[None, :], 0), axis=1)
    position = own - begin
    half = HEAD // 2
    frequency = jnp.exp(jnp.arange(half, dtype=F32) * (-2.0 * math.log(ROPE_BASE) / HEAD))
    angles = position.astype(F32)[:, None] * jnp.tile(frequency, 4)[None, :]
    tables = (jnp.cos(angles), jnp.sin(angles))
    gains = [jnp.tile(g.astype(F32), 2)[None, :] for g in (q_gain, k_gain)]
    kv, cache = call(
        rotate_keys_body,
        (
            jax.ShapeDtypeStruct((ROWS, KV_DIM), BF),
            jax.ShapeDtypeStruct((PAGES_DEV, 8, KV_DIM), BF),
        ),
        [SM] + [VM] * 4,
        "rotate_keys",
    )(page_table, parts, *tables, gains[1])
    far = lax.ppermute(kv, "yh", swap)
    queries = call(
        rotate_queries_body, jax.ShapeDtypeStruct((ROWS, Q_DIM), BF), [VM] * 4, "rotate_queries"
    )(parts, *tables, gains[0])
    far, queries = lax.optimization_barrier((far, queries))
    kept = gather(queries[None], "yl", 4, 4)
    mixing = jnp.concatenate([mixing, shift(mixing, "x", 4, 2)], axis=0)
    given = lax.ppermute(kept, "c", swap)
    target = jnp.arange(32, dtype=jnp.int32)[:, None, None]
    blocks = lax.all_to_all(jnp.where(target >= index, kv[None], far[None]), ("z", "x"), 0, 0)

    blocks, mixing, kept, given = lax.optimization_barrier((blocks, mixing, kept, given))

    def attend(flip):
        return call(
            functools.partial(attend_body, flip),
            jax.ShapeDtypeStruct((4, ROWS, SUMS), F32),
            [SM, SM] + [VM] * 3,
            f"attend{flip}",
            [pltpu.VMEM((4, 128, 256), F32), pltpu.VMEM((128, ROWS), F32)],
        )(place, lengths, given if flip else kept, blocks, far)

    sent = attend(1)
    arrived = lax.ppermute(sent, "c", swap)
    packed = call(pack_body, jax.ShapeDtypeStruct((4, ROWS, SUMS), BF), [VM, VM], "pack")(
        attend(0), arrived
    )
    mixing, packed = lax.optimization_barrier((mixing, packed))
    parts = lax.all_to_all(packed, "yl", 0, 0)
    mixing = call(order_body, jax.ShapeDtypeStruct((64, 20, 256), BF), [SM, VM], "order")(
        place, mixing
    ).reshape(Q_DIM, 256)
    attended = call(divide_body, jax.ShapeDtypeStruct((ROWS, Q_DIM), BF), [VM], "divide")(parts)
    attended = lax.all_gather(attended, ("yl", "c"), axis=0, tiled=True)
    hidden_out = call(
        mix_body, jax.ShapeDtypeStruct((PAGES_DEV, 8, 8, 256), BF), [VM] * 3, "mix"
    )(attended, mixing, hidden_in.reshape(PAGES_DEV, 8, 8, 256))
    return (hidden_out.reshape(TOK_DEV, 256), cache)


def solution(mesh):
    fine = Mesh(mesh.devices.reshape(2, 8, 4, 4, 2), ("yh", "z", "x", "yl", "c"))
    rows, columns = ("yh", "z", "x"), ("yl", "c")
    return jax.shard_map(
        on_device,
        mesh=fine,
        in_specs=(
            P(rows, columns),
            P(columns),
            P(columns, rows),
            P(),
            P(),
            P(rows, columns),
            P(),
            P(rows),
        ),
        out_specs=(P(rows, columns), P(rows, columns, None)),
        check_vma=False,
    )
```

```python
import functools
import math

import jax
import jax.numpy as jnp
from jax import lax
from jax.experimental import pallas as pl
from jax.experimental.pallas import tpu as pltpu
from jax.sharding import Mesh, PartitionSpec as P

D = 2048
HEADS = 20
KV_HEADS = 5
HEAD = 64
GROUP = 4
Q_DIM = 1280
KV_DIM = 640
QKV_DIM = 1920
TOK_DEV = 256
PAGE = 64
PAGES_DEV = 4
ROWS = 32
PIECE = 30
ROPE_BASE = 10000.0
SUMS = Q_DIM + 128
BF = jnp.bfloat16
F32 = jnp.float32
HIDDEN_BIAS = -1e30
EXP2_SCALE = HEAD ** (-0.5) * math.log2(math.e)

VM = pl.BlockSpec(memory_space=pltpu.VMEM)
SM = pl.BlockSpec(memory_space=pltpu.SMEM)


def call(body, out_shape, in_specs, name, scratch=()):
    many = isinstance(out_shape, tuple)
    return pl.pallas_call(
        body,
        out_shape=out_shape,
        in_specs=in_specs,
        out_specs=(VM,) * len(out_shape) if many else VM,
        scratch_shapes=list(scratch),
        compiler_params=pltpu.CompilerParams(vmem_limit_bytes=48 << 20),
        name=name,
    )


def project_body(flip, place, gain, weight, here, one, two, three, out):
    core = place[3] if not flip else 1 - place[3]
    x = place[5]
    columns = weight[:, :32, :].reshape(512, 256)
    lane = lax.broadcasted_iota(jnp.int32, (128, 128), 1)
    for step, hidden in enumerate((here, one, two, three)):
        rows = [hidden[p, yl, core].astype(F32) for yl in range(4) for p in range(PAGES_DEV)]
        values = jnp.concatenate(rows, axis=0)
        scaled = (values * gain[...].astype(F32)).astype(BF)
        product = lax.dot_general(
            scaled, columns, (((1,), (1,)), ((), ())), preferred_element_type=F32
        )
        squares = jnp.sum(values * values, axis=1, keepdims=True)
        owner = lax.rem(x + 4 - step, 4)
        out[pl.ds(owner, 1), :, :128] = jnp.where(lane == 30, squares, product[:, :128])[None]
        out[pl.ds(owner, 1), :, 128:] = product[None, :, 128:]


def round_body(here, there, out):
    lane = lax.broadcasted_iota(jnp.int32, (128, 128), 1)
    for k in range(4):
        for tile in range(4):
            at = pl.ds(tile * 128, 128)
            total = here[k, :, at] + there[k, :, at]
            low = total.astype(BF)
            if tile == 0:
                rest = pltpu.roll(total - low.astype(F32), 1, 1)
                low = jnp.where(lane == 31, rest, low.astype(F32)).astype(BF)
            if tile >= 2:
                rest = (total - low.astype(F32)).astype(BF)
                out[k, :, pl.ds((7 - tile) * 128, 128)] = rest
            out[k, :, at] = low


def pieces_in_order(parts, first_tile, count):
    lane = lax.broadcasted_iota(jnp.int32, (ROWS, 128), 1)

    def summed(x, tile):
        def part(k):
            value = parts[4 * x + k, :, pl.ds(tile * 128, 128)].astype(F32)
            if tile < 2:
                return value
            return value + parts[4 * x + k, :, pl.ds((7 - tile) * 128, 128)].astype(F32)

        return (part(0) + part(1)) + (part(2) + part(3))

    squares = summed(0, 0)
    inverse = lax.rsqrt((squares[:, 30:31] + squares[:, 31:32]) / D + 1e-06)
    tiles = [None] * count
    for tile in range(4):
        for x in range(4):
            source = None
            for piece in range(4):
                yh, z = divmod(tile * 4 + piece, 8)
                start = PIECE * (yh * 32 + z * 4 + x) - 128 * first_tile
                touched = range(start // 128, (start + PIECE - 1) // 128 + 1)
                touched = [t for t in touched if 0 <= t < count]
                if not touched:
                    continue
                source = summed(x, tile) if source is None else source
                moved = pltpu.roll(source, (start - piece * 32) % 128, 1)
                for t in touched:
                    inside = (lane >= start - t * 128) & (lane < start + PIECE - t * 128)
                    tiles[t] = jnp.where(inside, moved, 0.0 if tiles[t] is None else tiles[t])
    return [u * inverse for u in tiles]


def turn(u, cosine, sine, gain):
    lane = lax.broadcasted_iota(jnp.int32, (ROWS, 128), 1)
    upper_head = lane >= HEAD
    lower_part = (lane % HEAD) < HEAD // 2
    square = u * u
    both = jnp.sum(jnp.where(upper_head, 0.0, square), axis=1, keepdims=True)
    other = jnp.sum(jnp.where(upper_head, square, 0.0), axis=1, keepdims=True)
    mean = jnp.where(upper_head, other, both) * (1.0 / HEAD)
    w = u * lax.rsqrt(mean + 1e-06) * gain[...]
    partner = jnp.where(lower_part, pltpu.roll(w, 96, 1), pltpu.roll(w, 32, 1))
    return w * cosine[...] + partner * jnp.where(lower_part, -sine[...], sine[...])


def rotate_queries_body(parts, cosine, sine, gain, queries):
    for tile, u in enumerate(pieces_in_order(parts, 0, 10)):
        queries[:, tile * 128 : tile * 128 + 128] = turn(u, cosine, sine, gain).astype(BF)


def rotate_keys_body(table, parts, cosine, sine, gain, kv, cache):
    upper_head = lax.broadcasted_iota(jnp.int32, (ROWS, 128), 1) >= HEAD
    for tile, u in enumerate(pieces_in_order(parts, 10, 5)):
        if tile == 2:
            u = jnp.where(upper_head, u, turn(u, cosine, sine, gain))
        elif tile < 2:
            u = turn(u, cosine, sine, gain)
        kv[:, tile * 128 : tile * 128 + 128] = u.astype(BF)
    for p in range(PAGES_DEV):
        cache[pl.ds(table[p], 1)] = kv[p * 8 : p * 8 + 8, :].reshape(1, 8, KV_DIM)


def attend_body(flip, place, lengths, q, blocks, far, out, bias, bias_far):
    yh, index, wide, narrow, yl = place[0], place[1], place[2], place[4], place[6]
    core = place[3] if not flip else 1 - place[3]
    row = lax.broadcasted_iota(jnp.int32, (128, 1), 0)
    owner = ((yl + 4 - row // ROWS) & 3) * 2 + core
    token = wide * TOK_DEV + (row % ROWS) // 8 * PAGE + owner * 8 + row % 8
    begin = jnp.zeros_like(token)
    end = jnp.int32(0)
    for s in range(3):
        end = end + lengths[s]
        begin = jnp.where(token >= end, end, begin)

    def hide(first_block, lanes, fixed):
        lane = lax.broadcasted_iota(jnp.int32, (1, lanes), 1)
        block = first_block + lane // ROWS
        if fixed:
            source = (1 - yh) * 32 + block
        else:
            source = jnp.where(block <= index, yh, 1 - yh) * 32 + block
        key = source * TOK_DEV + (lane % ROWS) // 8 * PAGE + narrow * 8 + lane % 8
        return jnp.where((key <= token) & (key >= begin), 0.0, HIDDEN_BIAS)

    for chunk in range(4):
        bias[chunk] = hide(chunk * 8, 256, False)
    bias_far[...] = hide(index, ROWS, True)
    half = q[...].reshape(128, Q_DIM)
    owners = [(yl + 4 - k) & 3 for k in range(4)]
    out[:, :, Q_DIM:] = jnp.zeros((4, ROWS, 128), F32)
    for g in range(KV_HEADS):
        heads = [
            half[:, (g * GROUP + h) * HEAD : (g * GROUP + h + 1) * HEAD] for h in range(GROUP)
        ]
        stacked = jnp.concatenate(heads, axis=0)
        denominator = None
        numerator = None
        tail = None
        for chunk in range(5):
            if chunk < 4:
                keys = blocks[chunk * 8 : chunk * 8 + 8, :, g * HEAD : (g + 1) * HEAD]
                keys = keys.reshape(256, HEAD)
                values = blocks[chunk * 8 : chunk * 8 + 8, :, 320 + g * HEAD : 320 + (g + 1) * HEAD]
                values = values.reshape(256, HEAD)
                shade = bias[chunk]
            else:
                keys = far[:, g * HEAD : (g + 1) * HEAD]
                values = far[:, 320 + g * HEAD : 320 + (g + 1) * HEAD]
                shade = bias_far[...]
            scores = lax.dot_general(
                stacked, keys, (((1,), (1,)), ((), ())), preferred_element_type=F32
            )
            wide_scores = scores.reshape(GROUP, 128, keys.shape[0]) * EXP2_SCALE + shade[None]
            weight = jnp.exp2(wide_scores).reshape(GROUP * 128, keys.shape[0])
            product = jnp.dot(weight.astype(BF), values, preferred_element_type=F32)
            numerator = product if numerator is None else numerator + product
            if chunk < 4:
                folded = weight[:, :128] + weight[:, 128:]
                denominator = folded if denominator is None else denominator + folded
            else:
                tail = jnp.sum(weight, axis=1, keepdims=True)
        denominator = jnp.sum(denominator, axis=1, keepdims=True) + tail
        for h in range(GROUP):
            head = g * GROUP + h
            for k in range(4):
                at = slice(h * 128 + k * ROWS, h * 128 + (k + 1) * ROWS)
                to = pl.ds(owners[k], 1)
                out[to, :, head * HEAD : (head + 1) * HEAD] = numerator[at][None]
                for lane in (Q_DIM + head, Q_DIM + HEAD + head):
                    out[to, :, lane : lane + 1] = denominator[at][None]


def pack_body(here, there, out):
    lane = lax.broadcasted_iota(jnp.int32, (ROWS, 128), 1)
    for k in range(4):
        for tile in range(11):
            at = pl.ds(tile * 128, 128)
            total = here[k, :, at] + there[k, :, at]
            low = total.astype(BF)
            if tile == 10:
                rest = total - low.astype(F32)
                low = jnp.where(lane < HEAD, low.astype(F32), rest).astype(BF)
            out[k, :, at] = low


def divide_body(parts, out):
    upper_head = lax.broadcasted_iota(jnp.int32, (ROWS, 128), 1) >= HEAD

    def total(tile):
        at = pl.ds(tile * 128, 128)
        four = [parts[k, :, at].astype(F32) for k in range(4)]
        return (four[0] + four[1]) + (four[2] + four[3])

    under = total(10)
    under = under + pltpu.roll(under, HEAD, 1)
    for tile in range(10):
        low, high = under[:, 2 * tile : 2 * tile + 1], under[:, 2 * tile + 1 : 2 * tile + 2]
        out[:, tile * 128 : tile * 128 + 128] = (
            total(tile) / jnp.where(upper_head, high, low)
        ).astype(BF)


def mix_body(attended, weight, hidden, out):
    mixed = jnp.dot(attended[...], weight[...], preferred_element_type=F32)
    for n in range(8):
        for p in range(PAGES_DEV):
            at = (n * PAGES_DEV + p) * 8
            out[p, n] = (hidden[p, n].astype(F32) + mixed[at : at + 8]).astype(BF)


def order_body(place, own, one, two, three, out):
    for i, blocks in enumerate((own, one, two, three)):
        x = (place[5] + 4 - i) & 3
        for k in range(16):
            out[pl.ds(k * 4 + x, 1)] = blocks[k, :20][None]


def spread(x, axes, count):
    return lax.all_to_all(jnp.broadcast_to(x[None], (count,) + x.shape), axes, 0, 0)


def on_device(hidden_in, attn_gain, qkv_weight, q_gain, k_gain, out_weight, lengths, page_table):
    yh, z, x = lax.axis_index("yh"), lax.axis_index("z"), lax.axis_index("x")
    yl, core = lax.axis_index("yl"), lax.axis_index("c")
    index = z * 4 + x
    wide = yh * 32 + index
    narrow = yl * 2 + core
    place = jnp.stack([yh, index, wide, core, narrow, x, yl]).astype(jnp.int32)
    swap = [(0, 1), (1, 0)]

    def shift(value, axis, count, step):
        return lax.ppermute(value, axis, [(i, (i + step) % count) for i in range(count)])

    def gather(value, axis, size, count):
        step = 1
        while step < count:
            value = jnp.concatenate([value, shift(value, axis, size, step)], axis=0)
            step *= 2
        return value

    own = [jnp.pad(qkv_weight.T, ((0, 2), (0, 0))), jnp.pad(out_weight, ((0, 4), (0, 0)))]
    weight = spread(jnp.concatenate(own, axis=0), ("yh", "z"), 16)
    hidden = [hidden_in] + [shift(hidden_in, "x", 4, step) for step in range(1, 4)]
    hidden = [h.reshape(PAGES_DEV, 4, 2, 8, 256) for h in hidden]
    gain = attn_gain.reshape(1, 256)
    half_shape = jax.ShapeDtypeStruct((4, 128, 512), F32)

    def project(flip):
        return call(
            functools.partial(project_body, flip), half_shape, [SM] + [VM] * 6, f"project{flip}"
        )(place, gain, weight, *hidden)

    sent = project(1)
    arrived = lax.ppermute(sent, "c", swap)
    partial = call(round_body, jax.ShapeDtypeStruct((4, 128, 768), BF), [VM, VM], "round")(
        project(0), arrived
    ).reshape(16, ROWS, 768)
    mixing, partial = lax.optimization_barrier((weight[:, 32:], partial))
    parts = lax.all_to_all(partial, ("x", "yl"), 0, 0)
    after = shift(mixing, "x", 4, 1)
    mixing, after, parts = lax.optimization_barrier((mixing, after, parts))

    row = jnp.arange(ROWS, dtype=jnp.int32)
    own = wide * TOK_DEV + row // 8 * PAGE + narrow * 8 + row % 8
    ends = jnp.cumsum(lengths)
    begin = jnp.max(jnp.where(own[:, None] >= ends[None, :], ends[None, :], 0), axis=1)
    position = own - begin
    half = HEAD // 2
    frequency = jnp.exp(jnp.arange(half, dtype=F32) * (-2.0 * math.log(ROPE_BASE) / HEAD))
    angles = position.astype(F32)[:, None] * jnp.tile(frequency, 4)[None, :]
    tables = (jnp.cos(angles), jnp.sin(angles))
    gains = [jnp.tile(g.astype(F32), 2)[None, :] for g in (q_gain, k_gain)]
    kv, cache = call(
        rotate_keys_body,
        (
            jax.ShapeDtypeStruct((ROWS, KV_DIM), BF),
            jax.ShapeDtypeStruct((PAGES_DEV, 8, KV_DIM), BF),
        ),
        [SM] + [VM] * 4,
        "rotate_keys",
    )(page_table, parts, *tables, gains[1])
    far = lax.ppermute(kv, "yh", swap)
    queries = call(
        rotate_queries_body, jax.ShapeDtypeStruct((ROWS, Q_DIM), BF), [VM] * 4, "rotate_queries"
    )(parts, *tables, gains[0])
    far, queries = lax.optimization_barrier((far, queries))
    kept = gather(queries[None], "yl", 4, 4)
    before = shift(mixing, "x", 4, 3)
    given = lax.ppermute(kept, "c", swap)
    target = jnp.arange(32, dtype=jnp.int32)[:, None, None]
    blocks = lax.all_to_all(jnp.where(target >= index, kv[None], far[None]), ("z", "x"), 0, 0)

    blocks, before, kept, given = lax.optimization_barrier((blocks, before, kept, given))

    def attend(flip):
        return call(
            functools.partial(attend_body, flip),
            jax.ShapeDtypeStruct((4, ROWS, SUMS), F32),
            [SM, SM] + [VM] * 3,
            f"attend{flip}",
            [pltpu.VMEM((4, 128, 256), F32), pltpu.VMEM((128, ROWS), F32)],
        )(place, lengths, given if flip else kept, blocks, far)

    sent = attend(1)
    arrived = lax.ppermute(sent, "c", swap)
    packed = call(pack_body, jax.ShapeDtypeStruct((4, ROWS, SUMS), BF), [VM, VM], "pack")(
        attend(0), arrived
    )
    mixing, packed = lax.optimization_barrier((mixing, packed))
    parts = lax.all_to_all(packed, "yl", 0, 0)
    mixing = call(order_body, jax.ShapeDtypeStruct((64, 20, 256), BF), [SM] + [VM] * 4, "order")(
        place, mixing, after, shift(mixing, "x", 4, 2), before
    ).reshape(Q_DIM, 256)
    attended = call(divide_body, jax.ShapeDtypeStruct((ROWS, Q_DIM), BF), [VM], "divide")(parts)
    attended = lax.all_gather(attended, ("yl", "c"), axis=0, tiled=True)
    hidden_out = call(
        mix_body, jax.ShapeDtypeStruct((PAGES_DEV, 8, 8, 256), BF), [VM] * 3, "mix"
    )(attended, mixing, hidden_in.reshape(PAGES_DEV, 8, 8, 256))
    return (hidden_out.reshape(TOK_DEV, 256), cache)


def solution(mesh):
    fine = Mesh(mesh.devices.reshape(2, 8, 4, 4, 2), ("yh", "z", "x", "yl", "c"))
    rows, columns = ("yh", "z", "x"), ("yl", "c")
    return jax.shard_map(
        on_device,
        mesh=fine,
        in_specs=(
            P(rows, columns),
            P(columns),
            P(columns, rows),
            P(),
            P(),
            P(rows, columns),
            P(),
            P(rows),
        ),
        out_specs=(P(rows, columns), P(rows, columns, None)),
        check_vma=False,
    )
```

```python
import functools
import math

import jax
import jax.numpy as jnp
from jax import lax
from jax.experimental import pallas as pl
from jax.experimental.pallas import tpu as pltpu
from jax.sharding import Mesh, PartitionSpec as P

D = 2048
HEADS = 20
KV_HEADS = 5
HEAD = 64
GROUP = 4
Q_DIM = 1280
KV_DIM = 640
QKV_DIM = 1920
TOK_DEV = 256
PAGE = 64
PAGES_DEV = 4
ROWS = 32
PIECE = 30
ROPE_BASE = 10000.0
SUMS = Q_DIM + 128
BF = jnp.bfloat16
F32 = jnp.float32
HIDDEN_BIAS = -1e30
EXP2_SCALE = HEAD ** (-0.5) * math.log2(math.e)

VM = pl.BlockSpec(memory_space=pltpu.VMEM)
SM = pl.BlockSpec(memory_space=pltpu.SMEM)


def call(body, out_shape, in_specs, name, scratch=()):
    many = isinstance(out_shape, tuple)
    return pl.pallas_call(
        body,
        out_shape=out_shape,
        in_specs=in_specs,
        out_specs=(VM,) * len(out_shape) if many else VM,
        scratch_shapes=list(scratch),
        compiler_params=pltpu.CompilerParams(vmem_limit_bytes=48 << 20),
        name=name,
    )


def project_body(flip, place, gain, weight, here, one, two, three, out):
    core = place[3] if not flip else 1 - place[3]
    x = place[5]
    columns = weight[:, :32, :].reshape(512, 256)
    lane = lax.broadcasted_iota(jnp.int32, (128, 128), 1)
    for step, hidden in enumerate((here, one, two, three)):
        rows = [hidden[p, yl, core].astype(F32) for yl in range(4) for p in range(PAGES_DEV)]
        values = jnp.concatenate(rows, axis=0)
        scaled = (values * gain[...].astype(F32)).astype(BF)
        product = lax.dot_general(
            scaled, columns, (((1,), (1,)), ((), ())), preferred_element_type=F32
        )
        squares = jnp.sum(values * values, axis=1, keepdims=True)
        owner = lax.rem(x + 4 - step, 4)
        out[pl.ds(owner, 1), :, :128] = jnp.where(lane == 30, squares, product[:, :128])[None]
        out[pl.ds(owner, 1), :, 128:] = product[None, :, 128:]


def round_body(here, there, out):
    lane = lax.broadcasted_iota(jnp.int32, (128, 128), 1)
    for k in range(4):
        for tile in range(4):
            at = pl.ds(tile * 128, 128)
            total = here[k, :, at] + there[k, :, at]
            low = total.astype(BF)
            if tile == 0:
                rest = pltpu.roll(total - low.astype(F32), 1, 1)
                low = jnp.where(lane == 31, rest, low.astype(F32)).astype(BF)
            if tile >= 2:
                rest = (total - low.astype(F32)).astype(BF)
                out[k, :, pl.ds((7 - tile) * 128, 128)] = rest
            out[k, :, at] = low


def pieces_in_order(parts, first_tile, count):
    lane = lax.broadcasted_iota(jnp.int32, (ROWS, 128), 1)

    def summed(x, tile):
        def part(k):
            value = parts[4 * x + k, :, pl.ds(tile * 128, 128)].astype(F32)
            if tile < 2:
                return value
            return value + parts[4 * x + k, :, pl.ds((7 - tile) * 128, 128)].astype(F32)

        return (part(0) + part(1)) + (part(2) + part(3))

    squares = summed(0, 0)
    inverse = lax.rsqrt((squares[:, 30:31] + squares[:, 31:32]) / D + 1e-06)
    tiles = [None] * count
    for tile in range(4):
        for x in range(4):
            source = None
            for piece in range(4):
                yh, z = divmod(tile * 4 + piece, 8)
                start = PIECE * (yh * 32 + z * 4 + x) - 128 * first_tile
                touched = range(start // 128, (start + PIECE - 1) // 128 + 1)
                touched = [t for t in touched if 0 <= t < count]
                if not touched:
                    continue
                source = summed(x, tile) if source is None else source
                moved = pltpu.roll(source, (start - piece * 32) % 128, 1)
                for t in touched:
                    inside = (lane >= start - t * 128) & (lane < start + PIECE - t * 128)
                    tiles[t] = jnp.where(inside, moved, 0.0 if tiles[t] is None else tiles[t])
    return [u * inverse for u in tiles]


def turn(u, cosine, sine, gain):
    lane = lax.broadcasted_iota(jnp.int32, (ROWS, 128), 1)
    upper_head = lane >= HEAD
    lower_part = (lane % HEAD) < HEAD // 2
    square = u * u
    both = jnp.sum(jnp.where(upper_head, 0.0, square), axis=1, keepdims=True)
    other = jnp.sum(jnp.where(upper_head, square, 0.0), axis=1, keepdims=True)
    mean = jnp.where(upper_head, other, both) * (1.0 / HEAD)
    w = u * lax.rsqrt(mean + 1e-06) * gain[...]
    partner = jnp.where(lower_part, pltpu.roll(w, 96, 1), pltpu.roll(w, 32, 1))
    return w * cosine[...] + partner * jnp.where(lower_part, -sine[...], sine[...])


def rotate_queries_body(parts, cosine, sine, gain, queries):
    for tile, u in enumerate(pieces_in_order(parts, 0, 10)):
        queries[:, tile * 128 : tile * 128 + 128] = turn(u, cosine, sine, gain).astype(BF)


def rotate_keys_body(table, parts, cosine, sine, gain, kv, cache):
    upper_head = lax.broadcasted_iota(jnp.int32, (ROWS, 128), 1) >= HEAD
    for tile, u in enumerate(pieces_in_order(parts, 10, 5)):
        if tile == 2:
            u = jnp.where(upper_head, u, turn(u, cosine, sine, gain))
        elif tile < 2:
            u = turn(u, cosine, sine, gain)
        kv[:, tile * 128 : tile * 128 + 128] = u.astype(BF)
    for p in range(PAGES_DEV):
        cache[pl.ds(table[p], 1)] = kv[p * 8 : p * 8 + 8, :].reshape(1, 8, KV_DIM)


def attend_body(flip, place, lengths, q, blocks, far, out, bias, bias_far):
    yh, index, wide, narrow, yl = place[0], place[1], place[2], place[4], place[6]
    core = place[3] if not flip else 1 - place[3]
    row = lax.broadcasted_iota(jnp.int32, (128, 1), 0)
    owner = ((yl + 4 - row // ROWS) & 3) * 2 + core
    token = wide * TOK_DEV + (row % ROWS) // 8 * PAGE + owner * 8 + row % 8
    begin = jnp.zeros_like(token)
    end = jnp.int32(0)
    for s in range(3):
        end = end + lengths[s]
        begin = jnp.where(token >= end, end, begin)

    def hide(first_block, lanes, fixed):
        lane = lax.broadcasted_iota(jnp.int32, (1, lanes), 1)
        block = first_block + lane // ROWS
        if fixed:
            source = (1 - yh) * 32 + block
        else:
            source = jnp.where(block <= index, yh, 1 - yh) * 32 + block
        key = source * TOK_DEV + (lane % ROWS) // 8 * PAGE + narrow * 8 + lane % 8
        return jnp.where((key <= token) & (key >= begin), 0.0, HIDDEN_BIAS)

    for chunk in range(4):
        bias[chunk] = hide(chunk * 8, 256, False)
    bias_far[...] = hide(index, ROWS, True)
    half = q[...].reshape(128, Q_DIM)
    owners = [(yl + 4 - k) & 3 for k in range(4)]
    out[:, :, Q_DIM:] = jnp.zeros((4, ROWS, 128), F32)
    for g in range(KV_HEADS):
        heads = [
            half[:, (g * GROUP + h) * HEAD : (g * GROUP + h + 1) * HEAD] for h in range(GROUP)
        ]
        stacked = jnp.concatenate(heads, axis=0)
        denominator = None
        numerator = None
        tail = None
        for chunk in range(5):
            if chunk < 4:
                keys = blocks[chunk * 8 : chunk * 8 + 8, :, g * HEAD : (g + 1) * HEAD]
                keys = keys.reshape(256, HEAD)
                values = blocks[chunk * 8 : chunk * 8 + 8, :, 320 + g * HEAD : 320 + (g + 1) * HEAD]
                values = values.reshape(256, HEAD)
                shade = bias[chunk]
            else:
                keys = far[:, g * HEAD : (g + 1) * HEAD]
                values = far[:, 320 + g * HEAD : 320 + (g + 1) * HEAD]
                shade = bias_far[...]
            scores = lax.dot_general(
                stacked, keys, (((1,), (1,)), ((), ())), preferred_element_type=F32
            )
            wide_scores = scores.reshape(GROUP, 128, keys.shape[0]) * EXP2_SCALE + shade[None]
            weight = jnp.exp2(wide_scores).reshape(GROUP * 128, keys.shape[0])
            product = jnp.dot(weight.astype(BF), values, preferred_element_type=F32)
            numerator = product if numerator is None else numerator + product
            if chunk < 4:
                folded = weight[:, :128] + weight[:, 128:]
                denominator = folded if denominator is None else denominator + folded
            else:
                tail = jnp.sum(weight, axis=1, keepdims=True)
        denominator = jnp.sum(denominator, axis=1, keepdims=True) + tail
        for h in range(GROUP):
            head = g * GROUP + h
            for k in range(4):
                at = slice(h * 128 + k * ROWS, h * 128 + (k + 1) * ROWS)
                to = pl.ds(owners[k], 1)
                out[to, :, head * HEAD : (head + 1) * HEAD] = numerator[at][None]
                for lane in (Q_DIM + head, Q_DIM + HEAD + head):
                    out[to, :, lane : lane + 1] = denominator[at][None]


def pack_body(here, there, out):
    lane = lax.broadcasted_iota(jnp.int32, (ROWS, 128), 1)
    for k in range(4):
        for tile in range(11):
            at = pl.ds(tile * 128, 128)
            total = here[k, :, at] + there[k, :, at]
            low = total.astype(BF)
            if tile == 10:
                rest = total - low.astype(F32)
                low = jnp.where(lane < HEAD, low.astype(F32), rest).astype(BF)
            out[k, :, at] = low


def divide_body(parts, out):
    upper_head = lax.broadcasted_iota(jnp.int32, (ROWS, 128), 1) >= HEAD

    def total(tile):
        at = pl.ds(tile * 128, 128)
        four = [parts[k, :, at].astype(F32) for k in range(4)]
        return (four[0] + four[1]) + (four[2] + four[3])

    under = total(10)
    under = under + pltpu.roll(under, HEAD, 1)
    for tile in range(10):
        low, high = under[:, 2 * tile : 2 * tile + 1], under[:, 2 * tile + 1 : 2 * tile + 2]
        out[:, tile * 128 : tile * 128 + 128] = (
            total(tile) / jnp.where(upper_head, high, low)
        ).astype(BF)


def mix_body(attended, weight, hidden, out):
    mixed = jnp.dot(attended[...], weight[...], preferred_element_type=F32)
    for n in range(8):
        for p in range(PAGES_DEV):
            at = (n * PAGES_DEV + p) * 8
            out[p, n] = (hidden[p, n].astype(F32) + mixed[at : at + 8]).astype(BF)


def order_body(place, own, one, two, three, out):
    for i, blocks in enumerate((own, one, two, three)):
        x = (place[5] + 4 - i) & 3
        for k in range(16):
            out[pl.ds(k * 4 + x, 1)] = blocks[k, :20][None]


def spread(x, axes, count):
    return lax.all_to_all(jnp.broadcast_to(x[None], (count,) + x.shape), axes, 0, 0)


def on_device(hidden_in, attn_gain, qkv_weight, q_gain, k_gain, out_weight, lengths, page_table):
    yh, z, x = lax.axis_index("yh"), lax.axis_index("z"), lax.axis_index("x")
    yl, core = lax.axis_index("yl"), lax.axis_index("c")
    index = z * 4 + x
    wide = yh * 32 + index
    narrow = yl * 2 + core
    place = jnp.stack([yh, index, wide, core, narrow, x, yl]).astype(jnp.int32)
    swap = [(0, 1), (1, 0)]

    def shift(value, axis, count, step):
        return lax.ppermute(value, axis, [(i, (i + step) % count) for i in range(count)])

    def gather(value, axis, size, count):
        step = 1
        while step < count:
            value = jnp.concatenate([value, shift(value, axis, size, step)], axis=0)
            step *= 2
        return value

    own = [jnp.pad(qkv_weight.T, ((0, 2), (0, 0))), jnp.pad(out_weight, ((0, 4), (0, 0)))]
    weight = spread(jnp.concatenate(own, axis=0), ("yh", "z"), 16)
    hidden = [hidden_in] + [shift(hidden_in, "x", 4, step) for step in range(1, 4)]
    hidden = [h.reshape(PAGES_DEV, 4, 2, 8, 256) for h in hidden]
    gain = attn_gain.reshape(1, 256)
    half_shape = jax.ShapeDtypeStruct((4, 128, 512), F32)

    def project(flip):
        return call(
            functools.partial(project_body, flip), half_shape, [SM] + [VM] * 6, f"project{flip}"
        )(place, gain, weight, *hidden)

    sent = project(1)
    arrived = lax.ppermute(sent, "c", swap)
    partial = call(round_body, jax.ShapeDtypeStruct((4, 128, 768), BF), [VM, VM], "round")(
        project(0), arrived
    ).reshape(16, ROWS, 768)
    mixing, partial = lax.optimization_barrier((weight[:, 32:], partial))
    parts = lax.all_to_all(partial, ("x", "yl"), 0, 0)
    after, across = shift(mixing, "x", 4, 1), shift(mixing, "x", 4, 2)
    mixing, after, across, parts = lax.optimization_barrier((mixing, after, across, parts))

    row = jnp.arange(ROWS, dtype=jnp.int32)
    own = wide * TOK_DEV + row // 8 * PAGE + narrow * 8 + row % 8
    ends = jnp.cumsum(lengths)
    begin = jnp.max(jnp.where(own[:, None] >= ends[None, :], ends[None, :], 0), axis=1)
    position = own - begin
    half = HEAD // 2
    frequency = jnp.exp(jnp.arange(half, dtype=F32) * (-2.0 * math.log(ROPE_BASE) / HEAD))
    angles = position.astype(F32)[:, None] * jnp.tile(frequency, 4)[None, :]
    tables = (jnp.cos(angles), jnp.sin(angles))
    gains = [jnp.tile(g.astype(F32), 2)[None, :] for g in (q_gain, k_gain)]
    kv, cache = call(
        rotate_keys_body,
        (
            jax.ShapeDtypeStruct((ROWS, KV_DIM), BF),
            jax.ShapeDtypeStruct((PAGES_DEV, 8, KV_DIM), BF),
        ),
        [SM] + [VM] * 4,
        "rotate_keys",
    )(page_table, parts, *tables, gains[1])
    far = lax.ppermute(kv, "yh", swap)
    queries = call(
        rotate_queries_body, jax.ShapeDtypeStruct((ROWS, Q_DIM), BF), [VM] * 4, "rotate_queries"
    )(parts, *tables, gains[0])
    far, queries = lax.optimization_barrier((far, queries))
    kept = gather(queries[None], "yl", 4, 4)
    before = shift(mixing, "x", 4, 3)
    given = lax.ppermute(kept, "c", swap)
    target = jnp.arange(32, dtype=jnp.int32)[:, None, None]
    blocks = lax.all_to_all(jnp.where(target >= index, kv[None], far[None]), ("z", "x"), 0, 0)

    blocks, before, kept, given = lax.optimization_barrier((blocks, before, kept, given))

    def attend(flip):
        return call(
            functools.partial(attend_body, flip),
            jax.ShapeDtypeStruct((4, ROWS, SUMS), F32),
            [SM, SM] + [VM] * 3,
            f"attend{flip}",
            [pltpu.VMEM((4, 128, 256), F32), pltpu.VMEM((128, ROWS), F32)],
        )(place, lengths, given if flip else kept, blocks, far)

    sent = attend(1)
    arrived = lax.ppermute(sent, "c", swap)
    packed = call(pack_body, jax.ShapeDtypeStruct((4, ROWS, SUMS), BF), [VM, VM], "pack")(
        attend(0), arrived
    )
    mixing, packed = lax.optimization_barrier((mixing, packed))
    parts = lax.all_to_all(packed, "yl", 0, 0)
    mixing = call(order_body, jax.ShapeDtypeStruct((64, 20, 256), BF), [SM] + [VM] * 4, "order")(
        place, mixing, after, across, before
    ).reshape(Q_DIM, 256)
    attended = call(divide_body, jax.ShapeDtypeStruct((ROWS, Q_DIM), BF), [VM], "divide")(parts)
    attended = lax.all_gather(attended, ("yl", "c"), axis=0, tiled=True)
    hidden_out = call(
        mix_body, jax.ShapeDtypeStruct((PAGES_DEV, 8, 8, 256), BF), [VM] * 3, "mix"
    )(attended, mixing, hidden_in.reshape(PAGES_DEV, 8, 8, 256))
    return (hidden_out.reshape(TOK_DEV, 256), cache)


def solution(mesh):
    fine = Mesh(mesh.devices.reshape(2, 8, 4, 4, 2), ("yh", "z", "x", "yl", "c"))
    rows, columns = ("yh", "z", "x"), ("yl", "c")
    return jax.shard_map(
        on_device,
        mesh=fine,
        in_specs=(
            P(rows, columns),
            P(columns),
            P(columns, rows),
            P(),
            P(),
            P(rows, columns),
            P(),
            P(rows),
        ),
        out_specs=(P(rows, columns), P(rows, columns, None)),
        check_vma=False,
    )
```

```python
import functools
import math

import jax
import jax.numpy as jnp
from jax import lax
from jax.experimental import pallas as pl
from jax.experimental.pallas import tpu as pltpu
from jax.sharding import Mesh, PartitionSpec as P

D = 2048
HEADS = 20
KV_HEADS = 5
HEAD = 64
GROUP = 4
Q_DIM = 1280
KV_DIM = 640
QKV_DIM = 1920
TOK_DEV = 256
PAGE = 64
PAGES_DEV = 4
ROWS = 32
PIECE = 30
ROPE_BASE = 10000.0
SUMS = Q_DIM + 128
BF = jnp.bfloat16
F32 = jnp.float32
HIDDEN_BIAS = -1e30
EXP2_SCALE = HEAD ** (-0.5) * math.log2(math.e)

VM = pl.BlockSpec(memory_space=pltpu.VMEM)
SM = pl.BlockSpec(memory_space=pltpu.SMEM)


def call(body, out_shape, in_specs, name, scratch=()):
    many = isinstance(out_shape, tuple)
    return pl.pallas_call(
        body,
        out_shape=out_shape,
        in_specs=in_specs,
        out_specs=(VM,) * len(out_shape) if many else VM,
        scratch_shapes=list(scratch),
        compiler_params=pltpu.CompilerParams(vmem_limit_bytes=48 << 20),
        name=name,
    )


def project_body(flip, place, gain, weight, here, one, two, three, out):
    core = place[3] if not flip else 1 - place[3]
    x = place[5]
    columns = weight[:, :32, :].reshape(512, 256)
    lane = lax.broadcasted_iota(jnp.int32, (128, 128), 1)
    for step, hidden in enumerate((here, one, two, three)):
        rows = [hidden[p, yl, core].astype(F32) for yl in range(4) for p in range(PAGES_DEV)]
        values = jnp.concatenate(rows, axis=0)
        scaled = (values * gain[...].astype(F32)).astype(BF)
        product = lax.dot_general(
            scaled, columns, (((1,), (1,)), ((), ())), preferred_element_type=F32
        )
        squares = jnp.sum(values * values, axis=1, keepdims=True)
        owner = lax.rem(x + 4 - step, 4)
        out[pl.ds(owner, 1), :, :128] = jnp.where(lane == 30, squares, product[:, :128])[None]
        out[pl.ds(owner, 1), :, 128:] = product[None, :, 128:]


def round_body(here, there, out):
    lane = lax.broadcasted_iota(jnp.int32, (128, 128), 1)
    for k in range(4):
        for tile in range(4):
            at = pl.ds(tile * 128, 128)
            total = here[k, :, at] + there[k, :, at]
            low = total.astype(BF)
            if tile == 0:
                rest = pltpu.roll(total - low.astype(F32), 1, 1)
                low = jnp.where(lane == 31, rest, low.astype(F32)).astype(BF)
            if tile >= 2:
                rest = (total - low.astype(F32)).astype(BF)
                out[k, :, pl.ds((7 - tile) * 128, 128)] = rest
            out[k, :, at] = low


def pieces_in_order(parts, first_tile, count):
    lane = lax.broadcasted_iota(jnp.int32, (ROWS, 128), 1)

    def summed(x, tile):
        def part(k):
            value = parts[4 * x + k, :, pl.ds(tile * 128, 128)].astype(F32)
            if tile < 2:
                return value
            return value + parts[4 * x + k, :, pl.ds((7 - tile) * 128, 128)].astype(F32)

        return (part(0) + part(1)) + (part(2) + part(3))

    squares = summed(0, 0)
    inverse = lax.rsqrt((squares[:, 30:31] + squares[:, 31:32]) / D + 1e-06)
    tiles = [None] * count
    for tile in range(4):
        for x in range(4):
            source = None
            for piece in range(4):
                yh, z = divmod(tile * 4 + piece, 8)
                start = PIECE * (yh * 32 + z * 4 + x) - 128 * first_tile
                touched = range(start // 128, (start + PIECE - 1) // 128 + 1)
                touched = [t for t in touched if 0 <= t < count]
                if not touched:
                    continue
                source = summed(x, tile) if source is None else source
                moved = pltpu.roll(source, (start - piece * 32) % 128, 1)
                for t in touched:
                    inside = (lane >= start - t * 128) & (lane < start + PIECE - t * 128)
                    tiles[t] = jnp.where(inside, moved, 0.0 if tiles[t] is None else tiles[t])
    return [u * inverse for u in tiles]


def turn(u, cosine, sine, gain):
    lane = lax.broadcasted_iota(jnp.int32, (ROWS, 128), 1)
    upper_head = lane >= HEAD
    lower_part = (lane % HEAD) < HEAD // 2
    square = u * u
    both = jnp.sum(jnp.where(upper_head, 0.0, square), axis=1, keepdims=True)
    other = jnp.sum(jnp.where(upper_head, square, 0.0), axis=1, keepdims=True)
    mean = jnp.where(upper_head, other, both) * (1.0 / HEAD)
    w = u * lax.rsqrt(mean + 1e-06) * gain[...]
    partner = jnp.where(lower_part, pltpu.roll(w, 96, 1), pltpu.roll(w, 32, 1))
    return w * cosine[...] + partner * jnp.where(lower_part, -sine[...], sine[...])


def rotate_queries_body(parts, cosine, sine, gain, queries):
    for tile, u in enumerate(pieces_in_order(parts, 0, 10)):
        queries[:, tile * 128 : tile * 128 + 128] = turn(u, cosine, sine, gain).astype(BF)


def rotate_keys_body(table, parts, cosine, sine, gain, kv, cache):
    upper_head = lax.broadcasted_iota(jnp.int32, (ROWS, 128), 1) >= HEAD
    for tile, u in enumerate(pieces_in_order(parts, 10, 5)):
        if tile == 2:
            u = jnp.where(upper_head, u, turn(u, cosine, sine, gain))
        elif tile < 2:
            u = turn(u, cosine, sine, gain)
        kv[:, tile * 128 : tile * 128 + 128] = u.astype(BF)
    for p in range(PAGES_DEV):
        cache[pl.ds(table[p], 1)] = kv[p * 8 : p * 8 + 8, :].reshape(1, 8, KV_DIM)


def attend_body(flip, place, lengths, q, blocks, far, out, bias, bias_far, tops, unders):
    yh, index, wide, narrow, yl = place[0], place[1], place[2], place[4], place[6]
    core = place[3] if not flip else 1 - place[3]
    row = lax.broadcasted_iota(jnp.int32, (128, 1), 0)
    owner = ((yl + 4 - row // ROWS) & 3) * 2 + core
    token = wide * TOK_DEV + (row % ROWS) // 8 * PAGE + owner * 8 + row % 8
    begin = jnp.zeros_like(token)
    end = jnp.int32(0)
    for s in range(3):
        end = end + lengths[s]
        begin = jnp.where(token >= end, end, begin)

    def hide(first_block, lanes, fixed):
        lane = lax.broadcasted_iota(jnp.int32, (1, lanes), 1)
        block = first_block + lane // ROWS
        if fixed:
            source = (1 - yh) * 32 + block
        else:
            source = jnp.where(block <= index, yh, 1 - yh) * 32 + block
        key = source * TOK_DEV + (lane % ROWS) // 8 * PAGE + narrow * 8 + lane % 8
        return jnp.where((key <= token) & (key >= begin), 0.0, HIDDEN_BIAS)

    half = q[...].reshape(128, Q_DIM)
    owners = [(yl + 4 - k) & 3 for k in range(4)]

    def stacked_heads(g):
        heads = [
            half[:, (g * GROUP + h) * HEAD : (g * GROUP + h + 1) * HEAD] for h in range(GROUP)
        ]
        return jnp.concatenate(heads, axis=0)

    def keys_values(g, chunk):
        key_at = slice(g * HEAD, (g + 1) * HEAD)
        value_at = slice(320 + g * HEAD, 320 + (g + 1) * HEAD)
        if chunk == 4:
            return far[:, key_at], far[:, value_at]
        keys = blocks[chunk * 8 : chunk * 8 + 8, :, key_at].reshape(256, HEAD)
        return keys, blocks[chunk * 8 : chunk * 8 + 8, :, value_at].reshape(256, HEAD)

    def weigh(stacked, keys, values, shade):
        scores = lax.dot_general(
            stacked, keys, (((1,), (1,)), ((), ())), preferred_element_type=F32
        )
        wide_scores = scores.reshape(GROUP, 128, keys.shape[0]) * EXP2_SCALE + shade[None]
        weight = jnp.exp2(wide_scores).reshape(GROUP * 128, keys.shape[0])
        return weight, jnp.dot(weight.astype(BF), values, preferred_element_type=F32)

    def put(g, numerator, denominator):
        for h in range(GROUP):
            head = g * GROUP + h
            for k in range(4):
                at = slice(h * 128 + k * ROWS, h * 128 + (k + 1) * ROWS)
                to = pl.ds(owners[k], 1)
                out[to, :, head * HEAD : (head + 1) * HEAD] = numerator[at][None]
                for lane in (Q_DIM + head, Q_DIM + HEAD + head):
                    out[to, :, lane : lane + 1] = denominator[at][None]

    first = jnp.int32(0)
    end = jnp.int32(0)
    for s in range(3):
        end = end + lengths[s]
        first = jnp.where(wide * TOK_DEV >= end, end, first)
    first = first >> 8
    needed = []
    for chunk in range(4):
        low, high = chunk * 8, chunk * 8 + 7
        near = (low <= index) & (yh * 32 + jnp.minimum(high, index) >= first)
        needed.append(near | ((yh == 1) & (high > index) & (high >= first)))
    far_needed = (yh == 1) & (index >= first)
    every = needed[0] & needed[1] & needed[2] & needed[3]
    out[:, :, Q_DIM:] = jnp.zeros((4, ROWS, 128), F32)

    @pl.when(every)
    def _():
        for chunk in range(4):
            bias[chunk] = hide(chunk * 8, 256, False)
        bias_far[...] = hide(index, ROWS, True)
        for g in range(KV_HEADS):
            stacked = stacked_heads(g)
            numerator, denominator = None, None
            for chunk in range(4):
                weight, product = weigh(stacked, *keys_values(g, chunk), bias[chunk])
                numerator = product if numerator is None else numerator + product
                folded = weight[:, :128] + weight[:, 128:]
                denominator = folded if denominator is None else denominator + folded
            weight, product = weigh(stacked, *keys_values(g, 4), bias_far[...])
            denominator = jnp.sum(denominator, axis=1, keepdims=True)
            denominator = denominator + jnp.sum(weight, axis=1, keepdims=True)
            put(g, numerator + product, denominator)

    @pl.when(jnp.logical_not(every))
    def _():
        tops[...] = jnp.zeros_like(tops)
        unders[...] = jnp.zeros_like(unders)
        for chunk in range(4):

            @pl.when(needed[chunk])
            def _(chunk=chunk):
                bias[chunk] = hide(chunk * 8, 256, False)
                for g in range(KV_HEADS):
                    weight, product = weigh(
                        stacked_heads(g), *keys_values(g, chunk), bias[chunk]
                    )
                    tops[g] += product
                    unders[g] += weight[:, :128] + weight[:, 128:]

        @pl.when(far_needed)
        def _():
            bias_far[...] = hide(index, ROWS, True)
            for g in range(KV_HEADS):
                weight, product = weigh(stacked_heads(g), *keys_values(g, 4), bias_far[...])
                tops[g] += product
                unders[g, :, :ROWS] += weight

        for g in range(KV_HEADS):
            put(g, tops[g], jnp.sum(unders[g], axis=1, keepdims=True))


def pack_body(here, there, out):
    lane = lax.broadcasted_iota(jnp.int32, (ROWS, 128), 1)
    for k in range(4):
        for tile in range(11):
            at = pl.ds(tile * 128, 128)
            total = here[k, :, at] + there[k, :, at]
            low = total.astype(BF)
            if tile == 10:
                rest = total - low.astype(F32)
                low = jnp.where(lane < HEAD, low.astype(F32), rest).astype(BF)
            out[k, :, at] = low


def divide_body(parts, out):
    upper_head = lax.broadcasted_iota(jnp.int32, (ROWS, 128), 1) >= HEAD

    def total(tile):
        at = pl.ds(tile * 128, 128)
        four = [parts[k, :, at].astype(F32) for k in range(4)]
        return (four[0] + four[1]) + (four[2] + four[3])

    under = total(10)
    under = under + pltpu.roll(under, HEAD, 1)
    for tile in range(10):
        low, high = under[:, 2 * tile : 2 * tile + 1], under[:, 2 * tile + 1 : 2 * tile + 2]
        out[:, tile * 128 : tile * 128 + 128] = (
            total(tile) / jnp.where(upper_head, high, low)
        ).astype(BF)


def mix_body(attended, weight, hidden, out):
    mixed = jnp.dot(attended[...], weight[...], preferred_element_type=F32)
    for n in range(8):
        for p in range(PAGES_DEV):
            at = (n * PAGES_DEV + p) * 8
            out[p, n] = (hidden[p, n].astype(F32) + mixed[at : at + 8]).astype(BF)


def order_body(place, own, one, two, three, out):
    for i, blocks in enumerate((own, one, two, three)):
        x = (place[5] + 4 - i) & 3
        for k in range(16):
            out[pl.ds(k * 4 + x, 1)] = blocks[k, :20][None]


def spread(x, axes, count):
    return lax.all_to_all(jnp.broadcast_to(x[None], (count,) + x.shape), axes, 0, 0)


def on_device(hidden_in, attn_gain, qkv_weight, q_gain, k_gain, out_weight, lengths, page_table):
    yh, z, x = lax.axis_index("yh"), lax.axis_index("z"), lax.axis_index("x")
    yl, core = lax.axis_index("yl"), lax.axis_index("c")
    index = z * 4 + x
    wide = yh * 32 + index
    narrow = yl * 2 + core
    place = jnp.stack([yh, index, wide, core, narrow, x, yl]).astype(jnp.int32)
    swap = [(0, 1), (1, 0)]

    def shift(value, axis, count, step):
        return lax.ppermute(value, axis, [(i, (i + step) % count) for i in range(count)])

    def gather(value, axis, size, count):
        step = 1
        while step < count:
            value = jnp.concatenate([value, shift(value, axis, size, step)], axis=0)
            step *= 2
        return value

    own = [jnp.pad(qkv_weight.T, ((0, 2), (0, 0))), jnp.pad(out_weight, ((0, 4), (0, 0)))]
    weight = spread(jnp.concatenate(own, axis=0), ("yh", "z"), 16)
    hidden = [hidden_in] + [shift(hidden_in, "x", 4, step) for step in range(1, 4)]
    hidden = [h.reshape(PAGES_DEV, 4, 2, 8, 256) for h in hidden]
    gain = attn_gain.reshape(1, 256)
    half_shape = jax.ShapeDtypeStruct((4, 128, 512), F32)

    def project(flip):
        return call(
            functools.partial(project_body, flip), half_shape, [SM] + [VM] * 6, f"project{flip}"
        )(place, gain, weight, *hidden)

    sent = project(1)
    arrived = lax.ppermute(sent, "c", swap)
    partial = call(round_body, jax.ShapeDtypeStruct((4, 128, 768), BF), [VM, VM], "round")(
        project(0), arrived
    ).reshape(16, ROWS, 768)
    mixing, partial = lax.optimization_barrier((weight[:, 32:], partial))
    parts = lax.all_to_all(partial, ("x", "yl"), 0, 0)
    after, across = shift(mixing, "x", 4, 1), shift(mixing, "x", 4, 2)
    mixing, after, across, parts = lax.optimization_barrier((mixing, after, across, parts))

    row = jnp.arange(ROWS, dtype=jnp.int32)
    own = wide * TOK_DEV + row // 8 * PAGE + narrow * 8 + row % 8
    ends = jnp.cumsum(lengths)
    begin = jnp.max(jnp.where(own[:, None] >= ends[None, :], ends[None, :], 0), axis=1)
    position = own - begin
    half = HEAD // 2
    frequency = jnp.exp(jnp.arange(half, dtype=F32) * (-2.0 * math.log(ROPE_BASE) / HEAD))
    angles = position.astype(F32)[:, None] * jnp.tile(frequency, 4)[None, :]
    tables = (jnp.cos(angles), jnp.sin(angles))
    gains = [jnp.tile(g.astype(F32), 2)[None, :] for g in (q_gain, k_gain)]
    kv, cache = call(
        rotate_keys_body,
        (
            jax.ShapeDtypeStruct((ROWS, KV_DIM), BF),
            jax.ShapeDtypeStruct((PAGES_DEV, 8, KV_DIM), BF),
        ),
        [SM] + [VM] * 4,
        "rotate_keys",
    )(page_table, parts, *tables, gains[1])
    far = lax.ppermute(kv, "yh", swap)
    queries = call(
        rotate_queries_body, jax.ShapeDtypeStruct((ROWS, Q_DIM), BF), [VM] * 4, "rotate_queries"
    )(parts, *tables, gains[0])
    far, queries = lax.optimization_barrier((far, queries))
    kept = gather(queries[None], "yl", 4, 4)
    before = shift(mixing, "x", 4, 3)
    given = lax.ppermute(kept, "c", swap)
    target = jnp.arange(32, dtype=jnp.int32)[:, None, None]
    blocks = lax.all_to_all(jnp.where(target >= index, kv[None], far[None]), ("z", "x"), 0, 0)

    blocks, before, kept, given = lax.optimization_barrier((blocks, before, kept, given))

    def attend(flip):
        return call(
            functools.partial(attend_body, flip),
            jax.ShapeDtypeStruct((4, ROWS, SUMS), F32),
            [SM, SM] + [VM] * 3,
            f"attend{flip}",
            [
                pltpu.VMEM((4, 128, 256), F32),
                pltpu.VMEM((128, ROWS), F32),
                pltpu.VMEM((KV_HEADS, GROUP * 128, HEAD), F32),
                pltpu.VMEM((KV_HEADS, GROUP * 128, 128), F32),
            ],
        )(place, lengths, given if flip else kept, blocks, far)

    sent = attend(1)
    arrived = lax.ppermute(sent, "c", swap)
    packed = call(pack_body, jax.ShapeDtypeStruct((4, ROWS, SUMS), BF), [VM, VM], "pack")(
        attend(0), arrived
    )
    mixing, packed = lax.optimization_barrier((mixing, packed))
    parts = lax.all_to_all(packed, "yl", 0, 0)
    mixing = call(order_body, jax.ShapeDtypeStruct((64, 20, 256), BF), [SM] + [VM] * 4, "order")(
        place, mixing, after, across, before
    ).reshape(Q_DIM, 256)
    attended = call(divide_body, jax.ShapeDtypeStruct((ROWS, Q_DIM), BF), [VM], "divide")(parts)
    attended = lax.all_gather(attended, ("yl", "c"), axis=0, tiled=True)
    hidden_out = call(
        mix_body, jax.ShapeDtypeStruct((PAGES_DEV, 8, 8, 256), BF), [VM] * 3, "mix"
    )(attended, mixing, hidden_in.reshape(PAGES_DEV, 8, 8, 256))
    return (hidden_out.reshape(TOK_DEV, 256), cache)


def solution(mesh):
    fine = Mesh(mesh.devices.reshape(2, 8, 4, 4, 2), ("yh", "z", "x", "yl", "c"))
    rows, columns = ("yh", "z", "x"), ("yl", "c")
    return jax.shard_map(
        on_device,
        mesh=fine,
        in_specs=(
            P(rows, columns),
            P(columns),
            P(columns, rows),
            P(),
            P(),
            P(rows, columns),
            P(),
            P(rows),
        ),
        out_specs=(P(rows, columns), P(rows, columns, None)),
        check_vma=False,
    )
```

```python
import functools
import math

import jax
import jax.numpy as jnp
from jax import lax
from jax.experimental import pallas as pl
from jax.experimental.pallas import tpu as pltpu
from jax.sharding import Mesh, PartitionSpec as P

D = 2048
HEADS = 20
KV_HEADS = 5
HEAD = 64
GROUP = 4
Q_DIM = 1280
KV_DIM = 640
QKV_DIM = 1920
TOK_DEV = 256
PAGE = 64
PAGES_DEV = 4
ROWS = 32
PIECE = 30
ROPE_BASE = 10000.0
SUMS = Q_DIM + 128
BF = jnp.bfloat16
F32 = jnp.float32
HIDDEN_BIAS = -1e30
EXP2_SCALE = HEAD ** (-0.5) * math.log2(math.e)

VM = pl.BlockSpec(memory_space=pltpu.VMEM)
SM = pl.BlockSpec(memory_space=pltpu.SMEM)


def call(body, out_shape, in_specs, name, scratch=()):
    many = isinstance(out_shape, tuple)
    return pl.pallas_call(
        body,
        out_shape=out_shape,
        in_specs=in_specs,
        out_specs=(VM,) * len(out_shape) if many else VM,
        scratch_shapes=list(scratch),
        compiler_params=pltpu.CompilerParams(vmem_limit_bytes=48 << 20),
        name=name,
    )


def project_body(flip, place, gain, weight, here, one, two, three, out):
    core = place[3] if not flip else 1 - place[3]
    x = place[5]
    columns = weight[:, :32, :].reshape(512, 256)
    lane = lax.broadcasted_iota(jnp.int32, (128, 128), 1)
    for step, hidden in enumerate((here, one, two, three)):
        rows = [hidden[p, yl, core].astype(F32) for yl in range(4) for p in range(PAGES_DEV)]
        values = jnp.concatenate(rows, axis=0)
        scaled = (values * gain[...].astype(F32)).astype(BF)
        product = lax.dot_general(
            scaled, columns, (((1,), (1,)), ((), ())), preferred_element_type=F32
        )
        squares = jnp.sum(values * values, axis=1, keepdims=True)
        owner = lax.rem(x + 4 - step, 4)
        out[pl.ds(owner, 1), :, :128] = jnp.where(lane == 30, squares, product[:, :128])[None]
        out[pl.ds(owner, 1), :, 128:] = product[None, :, 128:]


def round_body(here, there, out):
    lane = lax.broadcasted_iota(jnp.int32, (128, 128), 1)
    for k in range(4):
        for tile in range(4):
            at = pl.ds(tile * 128, 128)
            total = here[k, :, at] + there[k, :, at]
            low = total.astype(BF)
            if tile == 0:
                rest = pltpu.roll(total - low.astype(F32), 1, 1)
                low = jnp.where(lane == 31, rest, low.astype(F32)).astype(BF)
            if tile >= 2:
                rest = (total - low.astype(F32)).astype(BF)
                out[k, :, pl.ds((7 - tile) * 128, 128)] = rest
            out[k, :, at] = low


def pieces_in_order(parts, first_tile, count):
    lane = lax.broadcasted_iota(jnp.int32, (ROWS, 128), 1)

    def summed(x, tile):
        def part(k):
            value = parts[4 * x + k, :, pl.ds(tile * 128, 128)].astype(F32)
            if tile < 2:
                return value
            return value + parts[4 * x + k, :, pl.ds((7 - tile) * 128, 128)].astype(F32)

        return (part(0) + part(1)) + (part(2) + part(3))

    squares = summed(0, 0)
    inverse = lax.rsqrt((squares[:, 30:31] + squares[:, 31:32]) / D + 1e-06)
    tiles = [None] * count
    for tile in range(4):
        for x in range(4):
            source = None
            for piece in range(4):
                yh, z = divmod(tile * 4 + piece, 8)
                start = PIECE * (yh * 32 + z * 4 + x) - 128 * first_tile
                touched = range(start // 128, (start + PIECE - 1) // 128 + 1)
                touched = [t for t in touched if 0 <= t < count]
                if not touched:
                    continue
                source = summed(x, tile) if source is None else source
                moved = pltpu.roll(source, (start - piece * 32) % 128, 1)
                for t in touched:
                    inside = (lane >= start - t * 128) & (lane < start + PIECE - t * 128)
                    tiles[t] = jnp.where(inside, moved, 0.0 if tiles[t] is None else tiles[t])
    return [u * inverse for u in tiles]


def turn(u, cosine, sine, gain):
    lane = lax.broadcasted_iota(jnp.int32, (ROWS, 128), 1)
    upper_head = lane >= HEAD
    lower_part = (lane % HEAD) < HEAD // 2
    square = u * u
    both = jnp.sum(jnp.where(upper_head, 0.0, square), axis=1, keepdims=True)
    other = jnp.sum(jnp.where(upper_head, square, 0.0), axis=1, keepdims=True)
    mean = jnp.where(upper_head, other, both) * (1.0 / HEAD)
    w = u * lax.rsqrt(mean + 1e-06) * gain[...]
    partner = jnp.where(lower_part, pltpu.roll(w, 96, 1), pltpu.roll(w, 32, 1))
    return w * cosine[...] + partner * jnp.where(lower_part, -sine[...], sine[...])


def rotate_queries_body(parts, cosine, sine, gain, queries):
    for tile, u in enumerate(pieces_in_order(parts, 0, 10)):
        queries[:, tile * 128 : tile * 128 + 128] = turn(u, cosine, sine, gain).astype(BF)


def rotate_keys_body(table, parts, cosine, sine, gain, kv, cache):
    upper_head = lax.broadcasted_iota(jnp.int32, (ROWS, 128), 1) >= HEAD
    for tile, u in enumerate(pieces_in_order(parts, 10, 5)):
        if tile == 2:
            u = jnp.where(upper_head, u, turn(u, cosine, sine, gain))
        elif tile < 2:
            u = turn(u, cosine, sine, gain)
        kv[:, tile * 128 : tile * 128 + 128] = u.astype(BF)
    for p in range(PAGES_DEV):
        cache[pl.ds(table[p], 1)] = kv[p * 8 : p * 8 + 8, :].reshape(1, 8, KV_DIM)


def attend_body(flip, place, lengths, q, blocks, far, out, bias, bias_far, tops, unders):
    yh, index, wide, narrow, yl = place[0], place[1], place[2], place[4], place[6]
    core = place[3] if not flip else 1 - place[3]
    row = lax.broadcasted_iota(jnp.int32, (128, 1), 0)
    owner = ((yl + 4 - row // ROWS) & 3) * 2 + core
    token = wide * TOK_DEV + (row % ROWS) // 8 * PAGE + owner * 8 + row % 8
    begin = jnp.zeros_like(token)
    end = jnp.int32(0)
    for s in range(3):
        end = end + lengths[s]
        begin = jnp.where(token >= end, end, begin)

    def hide(first_block, lanes, fixed):
        lane = lax.broadcasted_iota(jnp.int32, (1, lanes), 1)
        block = first_block + lane // ROWS
        if fixed:
            source = (1 - yh) * 32 + block
        else:
            source = jnp.where(block <= index, yh, 1 - yh) * 32 + block
        key = source * TOK_DEV + (lane % ROWS) // 8 * PAGE + narrow * 8 + lane % 8
        return jnp.where((key <= token) & (key >= begin), 0.0, HIDDEN_BIAS)

    half = q[...].reshape(128, Q_DIM)
    owners = [(yl + 4 - k) & 3 for k in range(4)]

    def stacked_heads(g):
        heads = [
            half[:, (g * GROUP + h) * HEAD : (g * GROUP + h + 1) * HEAD] for h in range(GROUP)
        ]
        return jnp.concatenate(heads, axis=0)

    def keys_values(g, chunk):
        key_at = slice(g * HEAD, (g + 1) * HEAD)
        value_at = slice(320 + g * HEAD, 320 + (g + 1) * HEAD)
        if chunk == 4:
            return far[:, key_at], far[:, value_at]
        keys = blocks[chunk * 8 : chunk * 8 + 8, :, key_at].reshape(256, HEAD)
        return keys, blocks[chunk * 8 : chunk * 8 + 8, :, value_at].reshape(256, HEAD)

    def weigh(stacked, keys, values, shade):
        scores = lax.dot_general(
            stacked, keys, (((1,), (1,)), ((), ())), preferred_element_type=F32
        )
        wide_scores = scores.reshape(GROUP, 128, keys.shape[0]) * EXP2_SCALE + shade[None]
        weight = jnp.exp2(wide_scores).reshape(GROUP * 128, keys.shape[0])
        return weight, jnp.dot(weight.astype(BF), values, preferred_element_type=F32)

    def put(g, numerator, denominator):
        for h in range(GROUP):
            head = g * GROUP + h
            for k in range(4):
                at = slice(h * 128 + k * ROWS, h * 128 + (k + 1) * ROWS)
                to = pl.ds(owners[k], 1)
                out[to, :, head * HEAD : (head + 1) * HEAD] = numerator[at][None]
                for lane in (Q_DIM + head, Q_DIM + HEAD + head):
                    out[to, :, lane : lane + 1] = denominator[at][None]

    first = jnp.int32(0)
    end = jnp.int32(0)
    for s in range(3):
        end = end + lengths[s]
        first = jnp.where(wide * TOK_DEV >= end, end, first)
    first = first >> 8
    needed = []
    for chunk in range(4):
        low, high = chunk * 8, chunk * 8 + 7
        near = (low <= index) & (yh * 32 + jnp.minimum(high, index) >= first)
        needed.append(near | ((yh == 1) & (high > index) & (high >= first)))
    far_needed = (yh == 1) & (index >= first)
    every = needed[0] & needed[1] & needed[2] & needed[3]
    out[:, :, Q_DIM:] = jnp.zeros((4, ROWS, 128), F32)

    @pl.when(every)
    def _():
        for chunk in range(4):
            bias[chunk] = hide(chunk * 8, 256, False)
        bias_far[...] = hide(index, ROWS, True)
        for g in range(KV_HEADS):
            stacked = stacked_heads(g)
            numerator, denominator = None, None
            for chunk in range(4):
                weight, product = weigh(stacked, *keys_values(g, chunk), bias[chunk])
                numerator = product if numerator is None else numerator + product
                folded = weight[:, :128] + weight[:, 128:]
                denominator = folded if denominator is None else denominator + folded
            weight, product = weigh(stacked, *keys_values(g, 4), bias_far[...])
            denominator = jnp.sum(denominator, axis=1, keepdims=True)
            denominator = denominator + jnp.sum(weight, axis=1, keepdims=True)
            put(g, numerator + product, denominator)

    @pl.when(jnp.logical_not(every))
    def _():
        tops[...] = jnp.zeros_like(tops)
        unders[...] = jnp.zeros_like(unders)
        for chunk in range(4):

            @pl.when(needed[chunk])
            def _(chunk=chunk):
                bias[chunk] = hide(chunk * 8, 256, False)
                for g in range(KV_HEADS):
                    weight, product = weigh(
                        stacked_heads(g), *keys_values(g, chunk), bias[chunk]
                    )
                    tops[g] += product
                    unders[g] += weight[:, :128] + weight[:, 128:]

        @pl.when(far_needed)
        def _():
            bias_far[...] = hide(index, ROWS, True)
            for g in range(KV_HEADS):
                weight, product = weigh(stacked_heads(g), *keys_values(g, 4), bias_far[...])
                tops[g] += product
                unders[g, :, :ROWS] += weight

        for g in range(KV_HEADS):
            put(g, tops[g], jnp.sum(unders[g], axis=1, keepdims=True))


def pack_body(here, there, out):
    lane = lax.broadcasted_iota(jnp.int32, (ROWS, 128), 1)
    for k in range(4):
        for tile in range(11):
            at = pl.ds(tile * 128, 128)
            total = here[k, :, at] + there[k, :, at]
            low = total.astype(BF)
            if tile == 10:
                rest = total - low.astype(F32)
                low = jnp.where(lane < HEAD, low.astype(F32), rest).astype(BF)
            out[k, :, at] = low


def divide_body(parts, out):
    upper_head = lax.broadcasted_iota(jnp.int32, (ROWS, 128), 1) >= HEAD

    def total(tile):
        at = pl.ds(tile * 128, 128)
        four = [parts[k, :, at].astype(F32) for k in range(4)]
        return (four[0] + four[1]) + (four[2] + four[3])

    under = total(10)
    under = under + pltpu.roll(under, HEAD, 1)
    for tile in range(10):
        low, high = under[:, 2 * tile : 2 * tile + 1], under[:, 2 * tile + 1 : 2 * tile + 2]
        out[:, tile * 128 : tile * 128 + 128] = (
            total(tile) / jnp.where(upper_head, high, low)
        ).astype(BF)


def mix_body(attended, weight, hidden, out):
    mixed = jnp.dot(attended[...], weight[...], preferred_element_type=F32)
    for n in range(8):
        for p in range(PAGES_DEV):
            at = (n * PAGES_DEV + p) * 8
            out[p, n] = (hidden[p, n].astype(F32) + mixed[at : at + 8]).astype(BF)


def order_body(place, own, one, two, three, out):
    for i, blocks in enumerate((own, one, two, three)):
        x = (place[5] + 4 - i) & 3
        for k in range(16):
            out[pl.ds(k * 4 + x, 1)] = blocks[k, :20][None]


def spread(x, axes, count):
    return lax.all_to_all(jnp.broadcast_to(x[None], (count,) + x.shape), axes, 0, 0)


def on_device(hidden_in, attn_gain, qkv_weight, q_gain, k_gain, out_weight, lengths, page_table):
    yh, z, x = lax.axis_index("yh"), lax.axis_index("z"), lax.axis_index("x")
    yl, core = lax.axis_index("yl"), lax.axis_index("c")
    index = z * 4 + x
    wide = yh * 32 + index
    narrow = yl * 2 + core
    place = jnp.stack([yh, index, wide, core, narrow, x, yl]).astype(jnp.int32)
    swap = [(0, 1), (1, 0)]

    def shift(value, axis, count, step):
        return lax.ppermute(value, axis, [(i, (i + step) % count) for i in range(count)])

    def gather(value, axis, size, count):
        step = 1
        while step < count:
            value = jnp.concatenate([value, shift(value, axis, size, step)], axis=0)
            step *= 2
        return value

    own = [jnp.pad(qkv_weight.T, ((0, 2), (0, 0))), jnp.pad(out_weight, ((0, 4), (0, 0)))]
    weight = spread(jnp.concatenate(own, axis=0), ("yh", "z"), 16)
    hidden = [hidden_in] + [shift(hidden_in, "x", 4, step) for step in range(1, 4)]
    hidden = [h.reshape(PAGES_DEV, 4, 2, 8, 256) for h in hidden]
    gain = attn_gain.reshape(1, 256)
    half_shape = jax.ShapeDtypeStruct((4, 128, 512), F32)

    def project(flip):
        return call(
            functools.partial(project_body, flip), half_shape, [SM] + [VM] * 6, f"project{flip}"
        )(place, gain, weight, *hidden)

    sent = project(1)
    arrived = lax.ppermute(sent, "c", swap)
    partial = call(round_body, jax.ShapeDtypeStruct((4, 128, 768), BF), [VM, VM], "round")(
        project(0), arrived
    ).reshape(16, ROWS, 768)
    mixing, partial = lax.optimization_barrier((weight[:, 32:], partial))
    parts = lax.all_to_all(partial, ("x", "yl"), 0, 0)
    after, before = shift(mixing, "x", 4, 1), shift(mixing, "x", 4, 3)
    mixing, after, before, parts = lax.optimization_barrier((mixing, after, before, parts))

    row = jnp.arange(ROWS, dtype=jnp.int32)
    own = wide * TOK_DEV + row // 8 * PAGE + narrow * 8 + row % 8
    ends = jnp.cumsum(lengths)
    begin = jnp.max(jnp.where(own[:, None] >= ends[None, :], ends[None, :], 0), axis=1)
    position = own - begin
    half = HEAD // 2
    frequency = jnp.exp(jnp.arange(half, dtype=F32) * (-2.0 * math.log(ROPE_BASE) / HEAD))
    angles = position.astype(F32)[:, None] * jnp.tile(frequency, 4)[None, :]
    tables = (jnp.cos(angles), jnp.sin(angles))
    gains = [jnp.tile(g.astype(F32), 2)[None, :] for g in (q_gain, k_gain)]
    kv, cache = call(
        rotate_keys_body,
        (
            jax.ShapeDtypeStruct((ROWS, KV_DIM), BF),
            jax.ShapeDtypeStruct((PAGES_DEV, 8, KV_DIM), BF),
        ),
        [SM] + [VM] * 4,
        "rotate_keys",
    )(page_table, parts, *tables, gains[1])
    far = lax.ppermute(kv, "yh", swap)
    queries = call(
        rotate_queries_body, jax.ShapeDtypeStruct((ROWS, Q_DIM), BF), [VM] * 4, "rotate_queries"
    )(parts, *tables, gains[0])
    far, queries = lax.optimization_barrier((far, queries))
    kept = gather(queries[None], "yl", 4, 4)
    across = shift(mixing, "x", 4, 2)
    given = lax.ppermute(kept, "c", swap)
    target = jnp.arange(32, dtype=jnp.int32)[:, None, None]
    blocks = lax.all_to_all(jnp.where(target >= index, kv[None], far[None]), ("z", "x"), 0, 0)

    blocks, across, kept, given = lax.optimization_barrier((blocks, across, kept, given))

    def attend(flip):
        return call(
            functools.partial(attend_body, flip),
            jax.ShapeDtypeStruct((4, ROWS, SUMS), F32),
            [SM, SM] + [VM] * 3,
            f"attend{flip}",
            [
                pltpu.VMEM((4, 128, 256), F32),
                pltpu.VMEM((128, ROWS), F32),
                pltpu.VMEM((KV_HEADS, GROUP * 128, HEAD), F32),
                pltpu.VMEM((KV_HEADS, GROUP * 128, 128), F32),
            ],
        )(place, lengths, given if flip else kept, blocks, far)

    sent = attend(1)
    arrived = lax.ppermute(sent, "c", swap)
    packed = call(pack_body, jax.ShapeDtypeStruct((4, ROWS, SUMS), BF), [VM, VM], "pack")(
        attend(0), arrived
    )
    mixing, packed = lax.optimization_barrier((mixing, packed))
    parts = lax.all_to_all(packed, "yl", 0, 0)
    mixing = call(order_body, jax.ShapeDtypeStruct((64, 20, 256), BF), [SM] + [VM] * 4, "order")(
        place, mixing, after, across, before
    ).reshape(Q_DIM, 256)
    attended = call(divide_body, jax.ShapeDtypeStruct((ROWS, Q_DIM), BF), [VM], "divide")(parts)
    attended = lax.all_gather(attended, ("yl", "c"), axis=0, tiled=True)
    hidden_out = call(
        mix_body, jax.ShapeDtypeStruct((PAGES_DEV, 8, 8, 256), BF), [VM] * 3, "mix"
    )(attended, mixing, hidden_in.reshape(PAGES_DEV, 8, 8, 256))
    return (hidden_out.reshape(TOK_DEV, 256), cache)


def solution(mesh):
    fine = Mesh(mesh.devices.reshape(2, 8, 4, 4, 2), ("yh", "z", "x", "yl", "c"))
    rows, columns = ("yh", "z", "x"), ("yl", "c")
    return jax.shard_map(
        on_device,
        mesh=fine,
        in_specs=(
            P(rows, columns),
            P(columns),
            P(columns, rows),
            P(),
            P(),
            P(rows, columns),
            P(),
            P(rows),
        ),
        out_specs=(P(rows, columns), P(rows, columns, None)),
        check_vma=False,
    )
```
